32 devices in a mesh: dp: 8 (over z, x), tensor: 4 (over y, core).
Axes of the slice: x: 2, y: 2, z: 4, core: 2. Of those that a mesh axis runs over, the one named last changes fastest.
Arguments:
- hidden_in: bfloat16 [4096, 1024], P(('dp', 'tensor')), may hold values from -8 to 8
- cotangent: bfloat16 [4096, 1024], P(('dp', 'tensor')), may hold values from -6 to 6
- lengths: int32 [8], P('dp'), may hold values from 128 to 512, as said below
- query_weight: bfloat16 [1024, 1024], P('dp', 'tensor'), as said below
- key_weight: bfloat16 [1024, 1024], P('dp', 'tensor'), as said below
- value_weight: bfloat16 [1024, 1024], P('dp', 'tensor'), may hold values from -0.1875 to 0.1875
- output_weight: bfloat16 [1024, 1024], P('tensor', 'dp'), may hold values from -1 to 1
- up_weight: bfloat16 [1024, 4096], P('dp', 'tensor'), may hold values from -0.1875 to 0.1875
- down_weight: bfloat16 [4096, 1024], P('tensor', 'dp'), may hold values from -0.09375 to 0.09375
- query_bias: float32 [1024], P('tensor'), may hold values from -3 to 3
- value_bias: float32 [1024], P('tensor'), may hold values from -3 to 3
- output_bias: float32 [1024], replicated, may hold values from -3 to 3
- up_bias: float32 [4096], P('tensor'), may hold values from -3 to 3
- down_bias: float32 [1024], replicated, may hold values from -3 to 3
- first_gain: float32 [1024], replicated, may hold values from 0.5 to 1.5
- first_shift: float32 [1024], replicated, may hold values from -3 to 3
- second_gain: float32 [1024], replicated, may hold values from 0.5 to 1.5
- second_shift: float32 [1024], replicated, may hold values from -3 to 3
Outputs:
- hidden_out: bfloat16 [4096, 1024], P(('dp', 'tensor'))
- grad_in: bfloat16 [4096, 1024], P(('dp', 'tensor'))
- grad_query_weight: float32 [1024, 1024], P('dp', 'tensor')
- grad_key_weight: float32 [1024, 1024], P('dp', 'tensor')
- grad_value_weight: float32 [1024, 1024], P('dp', 'tensor')
- grad_output_weight: float32 [1024, 1024], P('tensor', 'dp')
- grad_up_weight: float32 [1024, 4096], P('dp', 'tensor')
- grad_down_weight: float32 [4096, 1024], P('tensor', 'dp')
- grad_query_bias: float32 [1024], P('tensor')
- grad_value_bias: float32 [1024], P('tensor')
- grad_output_bias: float32 [1024], replicated
- grad_up_bias: float32 [4096], P('tensor')
- grad_down_bias: float32 [1024], replicated
- grad_first_gain: float32 [1024], replicated
- grad_first_shift: float32 [1024], replicated
- grad_second_gain: float32 [1024], replicated
- grad_second_shift: float32 [1024], replicated
The draws below stay inside these ranges and needn't reach their ends.
Inputs may be any that keep to these rules, and one draw needn't show every extreme that they name: `lengths`: positions of a sequence at or past its entry are padding keys. Some sequence is full. `query_weight`: A projection scaled by its fan-in. `key_weight`: A projection scaled by its fan-in.
All inputs are finite; a program needn't handle non-finite values.
Results may differ from the reference program's by a relative error of at most 0.02.
Values may be sent and summed in bfloat16 or wider, within the bound.
No kernel may reach another device: no remote copies, remote signals or barrier semaphores. Data moves between devices by JAX's collectives and lax.ppermute only.
A program may use at most 128 MiB of HBM per device.

```python
import jax
import jax.numpy as jnp
from jax import lax

D = 1024
HEADS = 16
HD = 64
FF = 4096
SEQ = 512
SEQS = 8
TOKENS = 4096


def draw_lengths(key, part):
    drawn = jax.random.randint(key, (SEQS,), SEQ // 4, SEQ + 1, dtype=jnp.int32)
    chosen = jax.random.randint(jax.random.fold_in(key, 7), (), 0, SEQS, dtype=jnp.int32)
    second_slot = (chosen + 1) % SEQS
    positions = jnp.arange(SEQS, dtype=jnp.int32)
    drawn = jnp.where(positions == chosen, SEQ, drawn)
    drawn = jnp.where((positions == second_slot) & (second_slot != chosen), SEQ // 4, drawn)
    return drawn


def weight_pair(key):
    base_query = jax.random.normal(jax.random.fold_in(key, 11), (D, D), jnp.float32) * D ** (-0.5)
    noise_part = jax.random.normal(jax.random.fold_in(key, 12), (D, D), jnp.float32) * D ** (-0.5)
    return (base_query, noise_part)


def draw_query_weight(key, part):
    base_query, noise_part = weight_pair(key)
    return base_query.astype(jnp.bfloat16)


def draw_key_weight(key, part):
    base_query, noise_part = weight_pair(key)
    result = noise_part
    return result.astype(jnp.bfloat16)


def draw_hidden_in(key, part):
    drawn_part = jnp.clip(jax.random.normal(jax.random.fold_in(key, 1), (SEQS, SEQ, D), jnp.float32), -8.0, 8.0)
    return drawn_part.reshape(TOKENS, D).astype(jnp.bfloat16)


def spiked(array, key, source, target, parts, factor):
    def block_of(axis_at):
        return (jnp.arange(array.shape[axis_at]) // (array.shape[axis_at] // parts)).reshape((-1,) + (1,) * (array.ndim - 1 - axis_at))

    one_side = jax.random.permutation(key, parts)[block_of(target)]
    second = (block_of(target) + parts // 2) % parts
    return jnp.where((block_of(source) == one_side) | (block_of(source) == second), factor * array, array)


def levels(own_key, extent, shards, smallest, top_value):
    gain, own = 1.0, jax.random.fold_in(own_key, 6)
    for dim, shards_of in shards:
        draws = jnp.exp(jax.random.uniform(jax.random.fold_in(own, dim), (shards_of,), jnp.float32, smallest / len(shards), top_value / len(shards)))
        gain = gain * jnp.repeat(draws, extent[dim] // shards_of).reshape([-1 if axis == dim else 1 for axis in range(len(extent))])
    return gain


def centred(stream_key, extent, deviation, most, shards=(), kind=jnp.bfloat16):
    values = jax.random.normal(stream_key, extent, jnp.float32) * deviation
    if len(shards) > 0:
        values = levels(stream_key, extent, shards, -0.22, 0.18) * values
    return jnp.clip(values, min=-most, max=most).astype(kind)


def heavy_noise(own_key, extent, scale, bound, pieces, heavy, held_as=jnp.bfloat16):
    values = scale * jax.random.normal(own_key, extent, jnp.float32)
    if pieces:
        values = values * levels(own_key, extent, pieces, -0.22, 0.18)
    return jnp.clip(spiked(values, jax.random.fold_in(own_key, 3), *heavy), -bound, bound).astype(held_as)


def setup_inputs(seed: int = 0) -> dict:
    streams_of = jax.random.split(jax.random.key(seed), 19)
    hidden_in = draw_hidden_in(jax.random.fold_in(streams_of[18], 71), 0)
    cotangent = heavy_noise(streams_of[1], (TOKENS, D), 1.0, 6.0, ((0, 32),), (0, 1, 32, 2.75))
    lengths = draw_lengths(jax.random.fold_in(streams_of[18], 71), 0)
    query_weight = draw_query_weight(jax.random.fold_in(streams_of[18], 71), 0)
    key_weight = draw_key_weight(jax.random.fold_in(streams_of[18], 71), 0)
    value_weight = centred(streams_of[5], (D, D), D ** -0.5, 0.1875, ((0, 8), (1, 4)))
    output_weight = centred(streams_of[6], (D, D), (D * 16 // SEQ) ** -0.5, 1.0, ((0, 4), (1, 8)))
    up_weight = centred(streams_of[7], (D, FF), D ** -0.5, 0.1875, ((0, 8), (1, 4)))
    down_weight = centred(streams_of[8], (FF, D), FF ** -0.5, 0.09375, ((0, 4), (1, 8)))
    query_bias = centred(streams_of[9], (D,), 0.5, 3.0, ((0, 4),), jnp.float32)
    value_bias = centred(streams_of[10], (D,), 0.5, 3.0, ((0, 4),), jnp.float32)
    output_bias = centred(streams_of[11], (D,), 0.5, 3.0, (), jnp.float32)
    up_bias = centred(streams_of[12], (FF,), 0.5, 3.0, ((0, 4),), jnp.float32)
    down_bias = centred(streams_of[13], (D,), 0.5, 3.0, (), jnp.float32)
    first_gain = jnp.clip(1.0 + 0.1 * jax.random.normal(streams_of[14], (D,), jnp.float32), 0.5, 1.5)
    first_shift = centred(streams_of[15], (D,), 0.5, 3.0, (), jnp.float32)
    second_gain = jnp.clip(1.0 + 0.1 * jax.random.normal(streams_of[16], (D,), jnp.float32), 0.5, 1.5)
    second_shift = centred(streams_of[17], (D,), 0.5, 3.0, (), jnp.float32)
    return dict(hidden_in=hidden_in, cotangent=cotangent, lengths=lengths, query_weight=query_weight, key_weight=key_weight, value_weight=value_weight, output_weight=output_weight, up_weight=up_weight, down_weight=down_weight, query_bias=query_bias, value_bias=value_bias, output_bias=output_bias, up_bias=up_bias, down_bias=down_bias, first_gain=first_gain, first_shift=first_shift, second_gain=second_gain, second_shift=second_shift)


EPSILON = 1e-12
ROOT_HALF = 0.7071067811865476
INV_ROOT_TWO_PI = 0.3989422804014327
MASKED = -1e+30

def matmul(left_side, right_side):
    return jnp.dot(left_side, right_side, preferred_element_type=jnp.float32)

def gelu_value(pre_act):
    return pre_act * 0.5 * (1.0 + lax.erf(pre_act * ROOT_HALF))

def gelu_slope(pre_act):
    cumulative = 0.5 * (1.0 + lax.erf(pre_act * ROOT_HALF))
    density = jnp.exp(-0.5 * pre_act * pre_act) * INV_ROOT_TWO_PI
    return cumulative + pre_act * density

def norm_forward(summed, gain_vector, shift_vector):
    centre = summed - lax.optimization_barrier(jnp.mean(summed, axis=-1, keepdims=True))
    spread = lax.optimization_barrier(jnp.mean(centre * centre, axis=-1, keepdims=True))
    inverse = lax.rsqrt(spread + EPSILON)
    normed = centre * inverse
    return (normed * gain_vector + shift_vector, normed, inverse)

def norm_backward(upstream, gain_vector, normed, inverse):
    scaled = upstream * gain_vector
    return inverse * (scaled - lax.optimization_barrier(jnp.mean(scaled, axis=-1, keepdims=True)) - normed * lax.optimization_barrier(jnp.mean(scaled * normed, axis=-1, keepdims=True)))

def reference(hidden_in, cotangent, lengths, query_weight, key_weight, value_weight, output_weight, up_weight, down_weight, query_bias, value_bias, output_bias, up_bias, down_bias, first_gain, first_shift, second_gain, second_shift):
    score_scale = HD ** (-0.5)
    position = jnp.arange(SEQ, dtype=jnp.int32)

    def one_sequence(totals, inputs):
        hidden, upstream_low, length = inputs
        queries = (matmul(hidden, query_weight) + query_bias).astype(jnp.bfloat16)
        key_rows = matmul(hidden, key_weight).astype(jnp.bfloat16)
        value_rows = (matmul(hidden, value_weight) + value_bias).astype(jnp.bfloat16)
        query_heads = queries.astype(jnp.float32).reshape(SEQ, HEADS, HD)
        key_heads = key_rows.astype(jnp.float32).reshape(SEQ, HEADS, HD)
        value_heads = value_rows.astype(jnp.float32).reshape(SEQ, HEADS, HD)
        key_valid = position < length
        scores = jnp.einsum('qhd,khd->hqk', query_heads, key_heads) * score_scale
        scores = jnp.where(key_valid[None, None, :], scores, MASKED)
        row_peak = lax.optimization_barrier(jnp.max(scores, axis=-1, keepdims=True))
        log_total = row_peak + jnp.log(lax.optimization_barrier(jnp.sum(jnp.exp(scores - row_peak), axis=-1, keepdims=True)))
        attn_probs = jnp.exp(scores - log_total)
        probs_low = attn_probs.astype(jnp.bfloat16)
        context = jnp.einsum('hqk,khd->qhd', probs_low.astype(jnp.float32), value_heads)
        context = context.reshape(SEQ, D).astype(jnp.bfloat16)
        first_sum = hidden.astype(jnp.float32) + matmul(context, output_weight) + output_bias
        first_out, first_normed, first_inverse = norm_forward(first_sum, first_gain, first_shift)
        first_low = first_out.astype(jnp.bfloat16)
        pre_act = matmul(first_low, up_weight) + up_bias
        activated = gelu_value(pre_act).astype(jnp.bfloat16)
        second_sum = first_out + matmul(activated, down_weight) + down_bias
        second_out, second_normed, second_inverse = norm_forward(second_sum, second_gain, second_shift)
        hidden_out = second_out.astype(jnp.bfloat16)
        upstream = upstream_low.astype(jnp.float32)
        second_grad = norm_backward(upstream, second_gain, second_normed, second_inverse)
        second_low = second_grad.astype(jnp.bfloat16)
        pre_grad = matmul(second_low, down_weight.T) * gelu_slope(pre_act)
        pre_low = pre_grad.astype(jnp.bfloat16)
        first_grad_in = second_grad + matmul(pre_low, up_weight.T)
        first_grad = norm_backward(first_grad_in, first_gain, first_normed, first_inverse)
        first_grad_low = first_grad.astype(jnp.bfloat16)
        context_grad = matmul(first_grad_low, output_weight.T).astype(jnp.bfloat16)
        grad_heads = context_grad.astype(jnp.float32).reshape(SEQ, HEADS, HD)
        prob_grad = jnp.einsum('qhd,khd->hqk', grad_heads, value_heads)
        row_inner = lax.optimization_barrier(jnp.sum(attn_probs * prob_grad, axis=-1, keepdims=True))
        score_grad = (attn_probs * (prob_grad - row_inner) * score_scale).astype(jnp.bfloat16)
        score_wide = score_grad.astype(jnp.float32)
        query_grad = jnp.einsum('hqk,khd->qhd', score_wide, key_heads).reshape(SEQ, D)
        key_grad = jnp.einsum('hqk,qhd->khd', score_wide, query_heads).reshape(SEQ, D)
        value_grad = jnp.einsum('hqk,qhd->khd', probs_low.astype(jnp.float32), grad_heads).reshape(SEQ, D)
        query_low = query_grad.astype(jnp.bfloat16)
        key_low = key_grad.astype(jnp.bfloat16)
        value_low = value_grad.astype(jnp.bfloat16)
        grad_in = (first_grad + matmul(query_low, query_weight.T) + matmul(key_low, key_weight.T) + matmul(value_low, value_weight.T)).astype(jnp.bfloat16)
        terms = (matmul(hidden.T, query_low), matmul(hidden.T, key_low), matmul(hidden.T, value_low), matmul(context.T, first_grad_low), matmul(first_low.T, pre_low), matmul(activated.T, second_low), lax.optimization_barrier(jnp.sum(query_grad, axis=0)), lax.optimization_barrier(jnp.sum(value_grad, axis=0)), lax.optimization_barrier(jnp.sum(first_grad, axis=0)), lax.optimization_barrier(jnp.sum(pre_grad, axis=0)), lax.optimization_barrier(jnp.sum(second_grad, axis=0)), lax.optimization_barrier(jnp.sum(first_grad_in * first_normed, axis=0)), lax.optimization_barrier(jnp.sum(first_grad_in, axis=0)), lax.optimization_barrier(jnp.sum(upstream * second_normed, axis=0)), lax.optimization_barrier(jnp.sum(upstream, axis=0)))
        totals = jax.tree.map(lambda running, addend: running + addend, totals, terms)
        return (totals, (hidden_out, grad_in))
    zero_square = jnp.zeros((D, D), jnp.float32)
    zero_vector = jnp.zeros((D,), jnp.float32)
    initial = (zero_square, zero_square, zero_square, zero_square, jnp.zeros((D, FF), jnp.float32), jnp.zeros((FF, D), jnp.float32), zero_vector, zero_vector, zero_vector, jnp.zeros((FF,), jnp.float32), zero_vector, zero_vector, zero_vector, zero_vector, zero_vector)
    totals, (outputs_all, grads_all) = lax.scan(one_sequence, initial, (hidden_in.reshape(SEQS, SEQ, D), cotangent.reshape(SEQS, SEQ, D), lengths))
    return (outputs_all.reshape(TOKENS, D), grads_all.reshape(TOKENS, D), totals[0], totals[1], totals[2], totals[3], totals[4], totals[5], totals[6], totals[7], totals[8], totals[9], totals[10], totals[11], totals[12], totals[13], totals[14])
```

```python
import jax
import jax.numpy as jnp
from jax import lax
from jax.sharding import PartitionSpec as P

HD = 64


EPSILON = 1e-12
ROOT_HALF = 0.7071067811865476
INV_ROOT_TWO_PI = 0.3989422804014327
MASKED = -1e30
BF16 = jnp.bfloat16
F32 = jnp.float32


def matmul(left_side, right_side):
    return jnp.dot(left_side, right_side, preferred_element_type=F32)


def matmul_nt(left_side, right_side):
    return lax.dot_general(left_side, right_side, (((1,), (1,)), ((), ())), preferred_element_type=F32)


def matmul_tn(left_side, right_side):
    return lax.dot_general(left_side, right_side, (((0,), (0,)), ((), ())), preferred_element_type=F32)


def gelu_value(pre_act):
    return pre_act * 0.5 * (1.0 + lax.erf(pre_act * ROOT_HALF))


def gelu_slope(pre_act):
    cumulative = 0.5 * (1.0 + lax.erf(pre_act * ROOT_HALF))
    density = jnp.exp(-0.5 * pre_act * pre_act) * INV_ROOT_TWO_PI
    return cumulative + pre_act * density


def norm_forward(summed, gain_vector, shift_vector):
    centre = summed - jnp.mean(summed, axis=-1, keepdims=True)
    spread = jnp.mean(centre * centre, axis=-1, keepdims=True)
    inverse = lax.rsqrt(spread + EPSILON)
    normed = centre * inverse
    return (normed * gain_vector + shift_vector, normed, inverse)


def norm_backward(upstream, gain_vector, normed, inverse):
    scaled = upstream * gain_vector
    return inverse * (
        scaled
        - jnp.mean(scaled, axis=-1, keepdims=True)
        - normed * jnp.mean(scaled * normed, axis=-1, keepdims=True)
    )


def swap(array, axis, bit):
    size = lax.axis_size(axis)
    return lax.ppermute(array, axis, [(i, i ^ bit) for i in range(size)])


def sum_over(array, axis):
    size = lax.axis_size(axis)
    if size & (size - 1) or size > 16:
        return lax.psum(array, axis)
    bit = 1
    while bit < size:
        array = array + swap(array, axis, bit)
        bit *= 2
    return array


def gather_rows(block):
    other_core = swap(block, "tensor", 1)
    far = swap(block, "tensor", 2)
    far_core = swap(far, "tensor", 1)
    return jnp.concatenate([block, other_core, far, far_core], axis=0)


def scatter_rows(partial):
    rows = partial.shape[0] // 4
    own, other_core, far, far_core = (partial[i * rows : (i + 1) * rows] for i in range(4))
    far_sum = (far.astype(F32) + swap(far_core, "tensor", 1).astype(F32)).astype(BF16)
    from_far = swap(far_sum, "tensor", 2)
    from_core = swap(other_core, "tensor", 1)
    return own.astype(F32) + from_core.astype(F32) + from_far.astype(F32)


class Ring:
    def __init__(self):
        self.size = lax.axis_size("dp")
        half = self.size // 2
        order = [2 * i for i in range(half)] + [2 * (self.size - 1 - i) + 1 for i in range(half, self.size)]
        self.up = [(order[i], order[(i + 1) % self.size]) for i in range(self.size)]
        self.down = [(b, a) for a, b in self.up]
        index = lax.axis_index("dp")
        row, column = index // 2, index % 2
        self.place = jnp.where(column == 0, row, self.size - 1 - row)
        self.small = self.size <= 16 and self.size % 2 == 0

    def owner(self, distance):
        place = (self.place + distance + 2 * self.size) % self.size
        return jnp.where(place < self.size // 2, 2 * place, 2 * (self.size - 1 - place) + 1)

    def gather(self, block, dim):
        if not self.small:
            return lax.all_gather(block, "dp", axis=dim, tiled=True)
        length = block.shape[dim]
        shape = list(block.shape)
        shape[dim] = length * self.size

        def put(whole, part, distance, offset=0):
            return lax.dynamic_update_slice_in_dim(whole, part, self.owner(distance) * length + offset, dim)

        whole = put(jnp.zeros(shape, block.dtype), block, 0)
        going_up = going_down = block
        for step in range(1, self.size // 2):
            going_up = lax.ppermute(going_up, "dp", self.up)
            going_down = lax.ppermute(going_down, "dp", self.down)
            whole = put(put(whole, going_up, -step), going_down, step)
        cut = block.shape[0] // 2
        first = lax.ppermute(going_up[:cut], "dp", self.up)
        second = lax.ppermute(going_down[cut:], "dp", self.down)
        last = jnp.concatenate([first, second], axis=0)
        return put(whole, last, self.size // 2)

    def scatter(self, whole, dim):
        if not self.small:
            return lax.psum_scatter(whole.astype(BF16), "dp", scatter_dimension=dim, tiled=True).astype(F32)
        length = whole.shape[dim] // self.size

        def term(distance):
            return lax.dynamic_slice_in_dim(whole, self.owner(distance) * length, length, dim).astype(F32)

        middle = self.size // 2
        far = term(middle).astype(BF16)
        cut = far.shape[0] // 2
        from_below = lax.ppermute(far[:cut], "dp", self.up).astype(F32)
        from_above = lax.ppermute(far[cut:], "dp", self.down).astype(F32)
        for step in range(middle - 1, 0, -1):
            above, below = term(step), term(-step)
            if step == middle - 1:
                above = jnp.concatenate([above[:cut] + from_below, above[cut:]], axis=0)
                below = jnp.concatenate([below[:cut], below[cut:] + from_above], axis=0)
            else:
                above, below = above + from_below, below + from_above
            from_below = lax.ppermute(above.astype(BF16), "dp", self.up).astype(F32)
            from_above = lax.ppermute(below.astype(BF16), "dp", self.down).astype(F32)
        return term(0) + from_below + from_above


def masked_scores(query_block, key_heads, key_valid, score_scale):
    scores = jnp.einsum("qhd,khd->hqk", query_block, key_heads, preferred_element_type=F32) * score_scale
    return jnp.where(key_valid[None, None, :], scores, MASKED)


def shards(
    hidden_in,
    cotangent,
    lengths,
    query_weight,
    key_weight,
    value_weight,
    output_weight,
    up_weight,
    down_weight,
    query_bias,
    value_bias,
    output_bias,
    up_bias,
    down_bias,
    first_gain,
    first_shift,
    second_gain,
    second_shift,
):
    n_tensor = lax.axis_size("tensor")
    tensor_index = lax.axis_index("tensor")
    local_rows = hidden_in.shape[0]
    seq_len = local_rows * n_tensor
    local_width = query_weight.shape[1]
    local_heads = local_width // HD
    score_scale = HD ** (-0.5)
    length = lengths[0]
    ring = Ring()
    blocks = jnp.arange(n_tensor, dtype=jnp.int32) ^ tensor_index
    positions = (blocks[:, None] * local_rows + jnp.arange(local_rows, dtype=jnp.int32)[None, :]).reshape(-1)
    key_valid = positions < length

    qkv_full = ring.gather(jnp.concatenate([query_weight, key_weight, value_weight], axis=1), 0)
    hidden_full = gather_rows(hidden_in)
    output_full = ring.gather(output_weight, 1)
    up_full = ring.gather(up_weight, 0)
    down_full = ring.gather(down_weight, 1)

    qkv = matmul(hidden_full, qkv_full)
    queries = (qkv[:, :local_width] + query_bias).astype(BF16)
    key_rows = qkv[:, local_width : 2 * local_width].astype(BF16)
    value_rows = (qkv[:, 2 * local_width :] + value_bias).astype(BF16)
    query_heads = queries.reshape(seq_len, local_heads, HD)
    key_heads = key_rows.reshape(seq_len, local_heads, HD)
    value_heads = value_rows.reshape(seq_len, local_heads, HD)
    scores = masked_scores(query_heads, key_heads, key_valid, score_scale)
    row_peak = jnp.max(scores, axis=-1, keepdims=True)
    log_total = row_peak + jnp.log(jnp.sum(jnp.exp(scores - row_peak), axis=-1, keepdims=True))
    probs_low = jnp.exp(scores - log_total).astype(BF16)
    context_block = jnp.einsum("hqk,khd->qhd", probs_low, value_heads, preferred_element_type=F32)
    context = context_block.astype(BF16).reshape(seq_len, local_width)
    attn_rows = scatter_rows(matmul(context, output_full).astype(BF16))
    first_sum = hidden_in.astype(F32) + attn_rows + output_bias
    first_out, first_normed, first_inverse = norm_forward(first_sum, first_gain, first_shift)
    normed_full = gather_rows(first_out.astype(BF16))
    pre_act = matmul(normed_full, up_full) + up_bias
    activated = gelu_value(pre_act).astype(BF16)
    mlp_rows = scatter_rows(matmul(activated, down_full).astype(BF16))
    second_sum = first_out + mlp_rows + down_bias
    second_out, second_normed, second_inverse = norm_forward(second_sum, second_gain, second_shift)
    hidden_out = second_out.astype(BF16)

    upstream = cotangent.astype(F32)
    grad_second_gain = jnp.sum(upstream * second_normed, axis=0)
    grad_second_shift = jnp.sum(upstream, axis=0)
    second_grad = norm_backward(upstream, second_gain, second_normed, second_inverse)
    grad_down_bias = jnp.sum(second_grad, axis=0)
    second_full = gather_rows(second_grad.astype(BF16))
    grad_down = matmul_tn(activated, second_full).astype(BF16)
    down_owned = ring.scatter(grad_down, 1)
    pre_grad = matmul_nt(second_full, down_full) * gelu_slope(pre_act)
    grad_up_bias = jnp.sum(pre_grad, axis=0)
    pre_low = pre_grad.astype(BF16)
    first_grad_in = second_grad + scatter_rows(matmul_nt(pre_low, up_full).astype(BF16))
    grad_up = matmul_tn(normed_full, pre_low).astype(BF16)
    up_owned = ring.scatter(grad_up, 0)
    grad_first_gain = jnp.sum(first_grad_in * first_normed, axis=0)
    grad_first_shift = jnp.sum(first_grad_in, axis=0)
    first_grad = norm_backward(first_grad_in, first_gain, first_normed, first_inverse)
    grad_output_bias = jnp.sum(first_grad, axis=0)
    attn_grad_full = gather_rows(first_grad.astype(BF16))
    context_grad = matmul_nt(attn_grad_full, output_full).astype(BF16)
    grad_output = matmul_tn(context, attn_grad_full).astype(BF16)
    output_owned = ring.scatter(grad_output, 1)

    everywhere = jnp.stack(
        [grad_second_gain, grad_second_shift, grad_down_bias, grad_first_gain, grad_first_shift, grad_output_bias]
    )
    everywhere = sum_over(sum_over(everywhere, "tensor"), "dp")
    up_bias_grad = sum_over(grad_up_bias, "dp")

    grad_heads = context_grad.reshape(seq_len, local_heads, HD)
    scores = masked_scores(query_heads, key_heads, key_valid, score_scale)
    attn_probs = jnp.exp(scores - log_total)
    probs_low = attn_probs.astype(BF16)
    prob_grad = jnp.einsum("qhd,khd->hqk", grad_heads, value_heads, preferred_element_type=F32)
    row_inner = jnp.sum(attn_probs * prob_grad, axis=-1, keepdims=True)
    score_grad = (attn_probs * (prob_grad - row_inner) * score_scale).astype(BF16)
    query_parts = jnp.einsum("hqk,khd->qhd", score_grad, key_heads, preferred_element_type=F32)
    key_total = jnp.einsum("hqk,qhd->khd", score_grad, query_heads, preferred_element_type=F32)
    value_total = jnp.einsum("hqk,qhd->khd", probs_low, grad_heads, preferred_element_type=F32)
    query_grad = query_parts.reshape(seq_len, local_width)
    key_grad = key_total.reshape(seq_len, local_width)
    value_grad = value_total.reshape(seq_len, local_width)
    late = sum_over(jnp.stack([jnp.sum(query_grad, axis=0), jnp.sum(value_grad, axis=0)]), "dp")
    qkv_low = jnp.concatenate([query_grad.astype(BF16), key_grad.astype(BF16), value_grad.astype(BF16)], axis=1)
    grad_qkv = matmul_tn(hidden_full, qkv_low).astype(BF16)
    qkv_owned = ring.scatter(grad_qkv, 0)
    back = scatter_rows(matmul_nt(qkv_low, qkv_full).astype(BF16))
    grad_in = (first_grad + back).astype(BF16)
    return (
        hidden_out,
        grad_in,
        qkv_owned[:, :local_width],
        qkv_owned[:, local_width : 2 * local_width],
        qkv_owned[:, 2 * local_width :],
        output_owned,
        up_owned,
        down_owned,
        late[0],
        late[1],
        everywhere[5],
        up_bias_grad,
        everywhere[2],
        everywhere[3],
        everywhere[4],
        everywhere[0],
        everywhere[1],
    )


def solution(mesh):
    in_specs = (
        P(("dp", "tensor"), None),
        P(("dp", "tensor"), None),
        P("dp"),
        P("dp", "tensor"),
        P("dp", "tensor"),
        P("dp", "tensor"),
        P("tensor", "dp"),
        P("dp", "tensor"),
        P("tensor", "dp"),
        P("tensor"),
        P("tensor"),
        P(),
        P("tensor"),
        P(),
        P(),
        P(),
        P(),
        P(),
    )
    out_specs = (
        P(("dp", "tensor"), None),
        P(("dp", "tensor"), None),
        P("dp", "tensor"),
        P("dp", "tensor"),
        P("dp", "tensor"),
        P("tensor", "dp"),
        P("dp", "tensor"),
        P("tensor", "dp"),
        P("tensor"),
        P("tensor"),
        P(),
        P("tensor"),
        P(),
        P(),
        P(),
        P(),
        P(),
    )
    return jax.shard_map(shards, mesh=mesh, in_specs=in_specs, out_specs=out_specs, check_vma=False)
```

```python
import functools

import jax
import jax.numpy as jnp
from jax import lax
from jax.experimental import pallas as pl
from jax.experimental.pallas import tpu as pltpu
from jax.sharding import PartitionSpec as P

HD = 64


EPSILON = 1e-12
ROOT_HALF = 0.7071067811865476
INV_ROOT_TWO_PI = 0.3989422804014327
MASKED = -1e30
BF16 = jnp.bfloat16
F32 = jnp.float32


def matmul(left_side, right_side):
    return jnp.dot(left_side, right_side, preferred_element_type=F32)


def matmul_nt(left_side, right_side):
    return lax.dot_general(left_side, right_side, (((1,), (1,)), ((), ())), preferred_element_type=F32)


def matmul_tn(left_side, right_side):
    return lax.dot_general(left_side, right_side, (((0,), (0,)), ((), ())), preferred_element_type=F32)


def gelu_value(pre_act):
    return pre_act * 0.5 * (1.0 + lax.erf(pre_act * ROOT_HALF))


def gelu_slope(pre_act):
    cumulative = 0.5 * (1.0 + lax.erf(pre_act * ROOT_HALF))
    density = jnp.exp(-0.5 * pre_act * pre_act) * INV_ROOT_TWO_PI
    return cumulative + pre_act * density


def norm_forward(summed, gain_vector, shift_vector):
    centre = summed - jnp.mean(summed, axis=-1, keepdims=True)
    spread = jnp.mean(centre * centre, axis=-1, keepdims=True)
    inverse = lax.rsqrt(spread + EPSILON)
    normed = centre * inverse
    return (normed * gain_vector + shift_vector, normed, inverse)


def norm_backward(upstream, gain_vector, normed, inverse):
    scaled = upstream * gain_vector
    return inverse * (
        scaled
        - jnp.mean(scaled, axis=-1, keepdims=True)
        - normed * jnp.mean(scaled * normed, axis=-1, keepdims=True)
    )


def swap(array, axis, bit):
    size = lax.axis_size(axis)
    return lax.ppermute(array, axis, [(i, i ^ bit) for i in range(size)])


def sum_over(array, axis):
    size = lax.axis_size(axis)
    if size & (size - 1) or size > 16:
        return lax.psum(array, axis)
    bit = 1
    while bit < size:
        array = array + swap(array, axis, bit)
        bit *= 2
    return array


def gather_rows(block):
    other_core = swap(block, "tensor", 1)
    far = swap(block, "tensor", 2)
    far_core = swap(far, "tensor", 1)
    return jnp.concatenate([block, other_core, far, far_core], axis=0)


def scatter_rows(partial):
    rows = partial.shape[0] // 4
    own, other_core, far, far_core = (partial[i * rows : (i + 1) * rows] for i in range(4))
    far_sum = (far.astype(F32) + swap(far_core, "tensor", 1).astype(F32)).astype(BF16)
    from_far = swap(far_sum, "tensor", 2)
    from_core = swap(other_core, "tensor", 1)
    return own.astype(F32) + from_core.astype(F32) + from_far.astype(F32)


class Ring:
    def __init__(self):
        self.size = lax.axis_size("dp")
        half = self.size // 2
        order = [2 * i for i in range(half)] + [2 * (self.size - 1 - i) + 1 for i in range(half, self.size)]
        self.up = [(order[i], order[(i + 1) % self.size]) for i in range(self.size)]
        self.down = [(b, a) for a, b in self.up]
        index = lax.axis_index("dp")
        row, column = index // 2, index % 2
        self.place = jnp.where(column == 0, row, self.size - 1 - row)
        self.small = self.size <= 16 and self.size % 2 == 0

    def owner(self, distance):
        place = (self.place + distance + 2 * self.size) % self.size
        return jnp.where(place < self.size // 2, 2 * place, 2 * (self.size - 1 - place) + 1)

    def gather(self, block, dim):
        if not self.small:
            return lax.all_gather(block, "dp", axis=dim, tiled=True)
        length = block.shape[dim]
        shape = list(block.shape)
        shape[dim] = length * self.size

        def put(whole, part, distance, offset=0):
            return lax.dynamic_update_slice_in_dim(whole, part, self.owner(distance) * length + offset, dim)

        whole = put(jnp.zeros(shape, block.dtype), block, 0)
        going_up = going_down = block
        for step in range(1, self.size // 2):
            going_up = lax.ppermute(going_up, "dp", self.up)
            going_down = lax.ppermute(going_down, "dp", self.down)
            whole = put(put(whole, going_up, -step), going_down, step)
        cut = block.shape[0] // 2
        first = lax.ppermute(going_up[:cut], "dp", self.up)
        second = lax.ppermute(going_down[cut:], "dp", self.down)
        last = jnp.concatenate([first, second], axis=0)
        return put(whole, last, self.size // 2)

    def scatter(self, whole, dim):
        if not self.small:
            return lax.psum_scatter(whole.astype(BF16), "dp", scatter_dimension=dim, tiled=True).astype(F32)
        length = whole.shape[dim] // self.size

        def term(distance):
            return lax.dynamic_slice_in_dim(whole, self.owner(distance) * length, length, dim).astype(F32)

        middle = self.size // 2
        far = term(middle).astype(BF16)
        cut = far.shape[0] // 2
        from_below = lax.ppermute(far[:cut], "dp", self.up).astype(F32)
        from_above = lax.ppermute(far[cut:], "dp", self.down).astype(F32)
        for step in range(middle - 1, 0, -1):
            above, below = term(step), term(-step)
            if step == middle - 1:
                above = jnp.concatenate([above[:cut] + from_below, above[cut:]], axis=0)
                below = jnp.concatenate([below[:cut], below[cut:] + from_above], axis=0)
            else:
                above, below = above + from_below, below + from_above
            from_below = lax.ppermute(above.astype(BF16), "dp", self.up).astype(F32)
            from_above = lax.ppermute(below.astype(BF16), "dp", self.down).astype(F32)
        return term(0) + from_below + from_above


LANES = 128
QUERY_TILE = 256


def head_lanes(shape, head):
    lane = lax.broadcasted_iota(jnp.int32, shape, 1)
    return (lane >= head * HD) & (lane < (head + 1) * HD)


def keep_head(block, head):
    return jnp.where(head_lanes(block.shape, head), block, jnp.zeros_like(block))


def scores_of(key_block, query_block, counts_ref, score_scale):
    scores = matmul_nt(key_block, query_block) * score_scale
    rows = scores.shape[0] // counts_ref.shape[0]
    valid = [
        lax.broadcasted_iota(jnp.int32, (rows, scores.shape[1]), 0) < counts_ref[r]
        for r in range(counts_ref.shape[0])
    ]
    return jnp.where(jnp.concatenate(valid, axis=0), scores, MASKED)


def attention_kernel(score_scale, counts_ref, query_ref, key_ref, value_ref, context_ref, log_total_ref):
    keys, values = key_ref[...], value_ref[...]
    pieces = []
    for head in range(LANES // HD):
        scores = scores_of(keys, keep_head(query_ref[...], head), counts_ref, score_scale)
        row_peak = jnp.max(scores, axis=0, keepdims=True)
        raised = jnp.exp(scores - row_peak)
        total = jnp.sum(raised, axis=0, keepdims=True)
        log_total_ref[0, head : head + 1, :] = row_peak + jnp.log(total)
        probs_low = (raised * (1.0 / total)).astype(BF16)
        both = matmul_tn(values, probs_low)
        pieces.append(both[head * HD : (head + 1) * HD])
    context_ref[...] = jnp.concatenate(pieces, axis=0).T.astype(BF16)


def attention(qkv_low, counts, local_width, score_scale):
    seq_len = qkv_low.shape[0]
    pairs = local_width // LANES
    tiles = seq_len // QUERY_TILE
    return pl.pallas_call(
        functools.partial(attention_kernel, score_scale),
        grid=(pairs, tiles),
        in_specs=[
            pl.BlockSpec(memory_space=pltpu.SMEM),
            pl.BlockSpec((QUERY_TILE, LANES), lambda j, i: (i, j)),
            pl.BlockSpec((seq_len, LANES), lambda j, i: (0, pairs + j)),
            pl.BlockSpec((seq_len, LANES), lambda j, i: (0, 2 * pairs + j)),
        ],
        out_specs=[
            pl.BlockSpec((QUERY_TILE, LANES), lambda j, i: (i, j)),
            pl.BlockSpec((1, LANES // HD, QUERY_TILE), lambda j, i: (j, 0, i)),
        ],
        out_shape=[
            jax.ShapeDtypeStruct((seq_len, local_width), BF16),
            jax.ShapeDtypeStruct((pairs, LANES // HD, seq_len), F32),
        ],
        cost_estimate=pl.CostEstimate(
            flops=4 * seq_len * seq_len * local_width,
            bytes_accessed=8 * seq_len * local_width,
            transcendentals=seq_len * seq_len * local_width // HD,
        ),
        name="attention",
    )(counts, qkv_low, qkv_low, qkv_low)


def attention_grad_kernel(
    score_scale,
    counts_ref,
    query_ref,
    key_ref,
    value_ref,
    upstream_ref,
    log_total_ref,
    query_grad_ref,
    key_grad_ref,
    value_grad_ref,
    query_sum_ref,
    value_sum_ref,
    key_total,
    value_total,
):
    step = pl.program_id(1)

    @pl.when(step == 0)
    def _():
        key_total[...] = jnp.zeros_like(key_total)
        value_total[...] = jnp.zeros_like(value_total)
        query_sum_ref[...] = jnp.zeros_like(query_sum_ref)

    keys, values = key_ref[...], value_ref[...]
    pieces = []
    for head in range(LANES // HD):
        queries = keep_head(query_ref[...], head)
        upstream = keep_head(upstream_ref[...], head)
        scores = scores_of(keys, queries, counts_ref, score_scale)
        probs = jnp.exp(scores - log_total_ref[0, head : head + 1, :])
        prob_grad = matmul_nt(values, upstream)
        row_inner = jnp.sum(probs * prob_grad, axis=0, keepdims=True)
        score_grad = (probs * (prob_grad - row_inner) * score_scale).astype(BF16)
        value_total[...] += matmul(probs.astype(BF16), upstream)
        key_total[...] += matmul(score_grad, queries)
        both = matmul_tn(keys, score_grad)
        pieces.append(both[head * HD : (head + 1) * HD])
    query_grad = jnp.concatenate(pieces, axis=0).T
    query_grad_ref[...] = query_grad.astype(BF16)
    query_sum_ref[...] += jnp.sum(query_grad, axis=0, keepdims=True)

    @pl.when(step == pl.num_programs(1) - 1)
    def _():
        key_grad_ref[...] = key_total[...].astype(BF16)
        value_grad_ref[...] = value_total[...].astype(BF16)
        value_sum_ref[...] = jnp.sum(value_total[...], axis=0, keepdims=True)


def attention_grad(qkv_low, upstream, log_total, counts, local_width, score_scale):
    seq_len = qkv_low.shape[0]
    pairs = local_width // LANES
    tiles = seq_len // QUERY_TILE
    tile_spec = pl.BlockSpec((QUERY_TILE, LANES), lambda j, i: (i, j))
    whole_spec = pl.BlockSpec((seq_len, LANES), lambda j, i: (0, j))
    sum_spec = pl.BlockSpec((1, LANES), lambda j, i: (0, j))
    low = jax.ShapeDtypeStruct((seq_len, local_width), BF16)
    sums = jax.ShapeDtypeStruct((1, local_width), F32)
    return pl.pallas_call(
        functools.partial(attention_grad_kernel, score_scale),
        grid=(pairs, tiles),
        in_specs=[
            pl.BlockSpec(memory_space=pltpu.SMEM),
            tile_spec,
            pl.BlockSpec((seq_len, LANES), lambda j, i: (0, pairs + j)),
            pl.BlockSpec((seq_len, LANES), lambda j, i: (0, 2 * pairs + j)),
            tile_spec,
            pl.BlockSpec((1, LANES // HD, QUERY_TILE), lambda j, i: (j, 0, i)),
        ],
        out_specs=[tile_spec, whole_spec, whole_spec, sum_spec, sum_spec],
        out_shape=[low, low, low, sums, sums],
        scratch_shapes=[pltpu.VMEM((seq_len, LANES), F32), pltpu.VMEM((seq_len, LANES), F32)],
        cost_estimate=pl.CostEstimate(
            flops=10 * seq_len * seq_len * local_width,
            bytes_accessed=16 * seq_len * local_width,
            transcendentals=seq_len * seq_len * local_width // HD,
        ),
        name="attention_grad",
    )(counts, qkv_low, qkv_low, qkv_low, upstream, log_total)


def shards(
    hidden_in,
    cotangent,
    lengths,
    query_weight,
    key_weight,
    value_weight,
    output_weight,
    up_weight,
    down_weight,
    query_bias,
    value_bias,
    output_bias,
    up_bias,
    down_bias,
    first_gain,
    first_shift,
    second_gain,
    second_shift,
):
    n_tensor = lax.axis_size("tensor")
    tensor_index = lax.axis_index("tensor")
    local_rows = hidden_in.shape[0]
    local_width = query_weight.shape[1]
    score_scale = HD ** (-0.5)
    ring = Ring()
    blocks = jnp.arange(n_tensor, dtype=jnp.int32) ^ tensor_index
    counts = lengths[0] - blocks * local_rows

    packed = jnp.concatenate([query_weight, key_weight, value_weight, output_weight.T], axis=1)
    packed_full = ring.gather(packed, 0)
    up_full = lax.all_gather(up_weight, "dp", axis=0, tiled=True)
    down_full = lax.all_gather(down_weight, "dp", axis=1, tiled=True)
    hidden_full = gather_rows(hidden_in)
    qkv_full = packed_full[:, : 3 * local_width]
    output_turned = packed_full[:, 3 * local_width :]

    qkv_bias = jnp.concatenate([query_bias, jnp.zeros_like(query_bias), value_bias])
    qkv_low = (matmul(hidden_full, qkv_full) + qkv_bias).astype(BF16)
    context, log_total = attention(qkv_low, counts, local_width, score_scale)
    attn_rows = scatter_rows(matmul_nt(context, output_turned).astype(BF16))
    first_sum = hidden_in.astype(F32) + attn_rows + output_bias
    first_out, first_normed, first_inverse = norm_forward(first_sum, first_gain, first_shift)
    normed_full = gather_rows(first_out.astype(BF16))
    pre_act = matmul(normed_full, up_full) + up_bias
    activated, slope = lax.optimization_barrier((gelu_value(pre_act).astype(BF16), gelu_slope(pre_act)))
    mlp_rows = scatter_rows(matmul(activated, down_full).astype(BF16))
    second_sum = first_out + mlp_rows + down_bias
    second_out, second_normed, second_inverse = norm_forward(second_sum, second_gain, second_shift)
    hidden_out = second_out.astype(BF16)

    upstream = cotangent.astype(F32)
    grad_second_gain = jnp.sum(upstream * second_normed, axis=0)
    grad_second_shift = jnp.sum(upstream, axis=0)
    second_grad = norm_backward(upstream, second_gain, second_normed, second_inverse)
    grad_down_bias = jnp.sum(second_grad, axis=0)
    second_full = gather_rows(second_grad.astype(BF16))
    grad_down = matmul_tn(activated, second_full).astype(BF16)
    down_owned = lax.psum_scatter(grad_down, "dp", scatter_dimension=1, tiled=True).astype(F32)
    pre_grad = matmul_nt(second_full, down_full) * slope
    grad_up_bias = jnp.sum(pre_grad, axis=0)
    pre_low = pre_grad.astype(BF16)
    first_grad_in = second_grad + scatter_rows(matmul_nt(pre_low, up_full).astype(BF16))
    grad_up = matmul_tn(normed_full, pre_low).astype(BF16)
    up_owned = lax.psum_scatter(grad_up, "dp", scatter_dimension=0, tiled=True).astype(F32)
    grad_first_gain = jnp.sum(first_grad_in * first_normed, axis=0)
    grad_first_shift = jnp.sum(first_grad_in, axis=0)
    first_grad = norm_backward(first_grad_in, first_gain, first_normed, first_inverse)
    grad_output_bias = jnp.sum(first_grad, axis=0)
    attn_grad_full = gather_rows(first_grad.astype(BF16))
    context_grad = matmul(attn_grad_full, output_turned).astype(BF16)

    everywhere = jnp.stack(
        [grad_second_gain, grad_second_shift, grad_down_bias, grad_first_gain, grad_first_shift, grad_output_bias]
    )
    everywhere = sum_over(everywhere, "tensor")

    query_low, key_low, value_low, query_sum, value_sum = attention_grad(
        qkv_low, context_grad, log_total, counts, local_width, score_scale
    )
    narrow = jnp.concatenate([query_sum.reshape(-1), value_sum.reshape(-1), grad_up_bias])
    vectors = sum_over(jnp.concatenate([everywhere.reshape(-1), narrow]), "dp")
    everywhere = vectors[: everywhere.size].reshape(everywhere.shape)
    narrow = vectors[everywhere.size :]
    low = jnp.concatenate([query_low, key_low, value_low], axis=1)
    packed_grad = jnp.concatenate([matmul_tn(hidden_full, low), matmul_tn(attn_grad_full, context)], axis=1)
    packed_owned = ring.scatter(packed_grad.astype(BF16), 0)
    back = scatter_rows(matmul_nt(low, qkv_full).astype(BF16))
    grad_in = (first_grad + back).astype(BF16)
    return (
        hidden_out,
        grad_in,
        packed_owned[:, :local_width],
        packed_owned[:, local_width : 2 * local_width],
        packed_owned[:, 2 * local_width : 3 * local_width],
        packed_owned[:, 3 * local_width :].T,
        up_owned,
        down_owned,
        narrow[:local_width],
        narrow[local_width : 2 * local_width],
        everywhere[5],
        narrow[2 * local_width :],
        everywhere[2],
        everywhere[3],
        everywhere[4],
        everywhere[0],
        everywhere[1],
    )


def solution(mesh):
    in_specs = (
        P(("dp", "tensor"), None),
        P(("dp", "tensor"), None),
        P("dp"),
        P("dp", "tensor"),
        P("dp", "tensor"),
        P("dp", "tensor"),
        P("tensor", "dp"),
        P("dp", "tensor"),
        P("tensor", "dp"),
        P("tensor"),
        P("tensor"),
        P(),
        P("tensor"),
        P(),
        P(),
        P(),
        P(),
        P(),
    )
    out_specs = (
        P(("dp", "tensor"), None),
        P(("dp", "tensor"), None),
        P("dp", "tensor"),
        P("dp", "tensor"),
        P("dp", "tensor"),
        P("tensor", "dp"),
        P("dp", "tensor"),
        P("tensor", "dp"),
        P("tensor"),
        P("tensor"),
        P(),
        P("tensor"),
        P(),
        P(),
        P(),
        P(),
        P(),
    )
    return jax.shard_map(shards, mesh=mesh, in_specs=in_specs, out_specs=out_specs, check_vma=False)
```

```python
import functools

import jax
import jax.numpy as jnp
from jax import lax
from jax.experimental import pallas as pl
from jax.experimental.layout import Layout, with_layout_constraint
from jax.experimental.pallas import tpu as pltpu
from jax.sharding import PartitionSpec as P

HD = 64


EPSILON = 1e-12
ROOT_HALF = 0.7071067811865476
INV_ROOT_TWO_PI = 0.3989422804014327
MASKED = -1e30
BF16 = jnp.bfloat16
F32 = jnp.float32


def matmul(left_side, right_side):
    return jnp.dot(left_side, right_side, preferred_element_type=F32)


def matmul_nt(left_side, right_side):
    return lax.dot_general(left_side, right_side, (((1,), (1,)), ((), ())), preferred_element_type=F32)


def matmul_tn(left_side, right_side):
    return lax.dot_general(left_side, right_side, (((0,), (0,)), ((), ())), preferred_element_type=F32)


def gelu_value(pre_act):
    return pre_act * 0.5 * (1.0 + lax.erf(pre_act * ROOT_HALF))


def gelu_slope(pre_act):
    cumulative = 0.5 * (1.0 + lax.erf(pre_act * ROOT_HALF))
    density = jnp.exp(-0.5 * pre_act * pre_act) * INV_ROOT_TWO_PI
    return cumulative + pre_act * density


def norm_forward(summed, gain_vector, shift_vector):
    centre = summed - jnp.mean(summed, axis=-1, keepdims=True)
    spread = jnp.mean(centre * centre, axis=-1, keepdims=True)
    inverse = lax.rsqrt(spread + EPSILON)
    normed = centre * inverse
    return (normed * gain_vector + shift_vector, normed, inverse)


def norm_backward(upstream, gain_vector, normed, inverse):
    scaled = upstream * gain_vector
    return inverse * (
        scaled
        - jnp.mean(scaled, axis=-1, keepdims=True)
        - normed * jnp.mean(scaled * normed, axis=-1, keepdims=True)
    )


def swap(array, axis, bit):
    size = lax.axis_size(axis)
    return lax.ppermute(array, axis, [(i, i ^ bit) for i in range(size)])


def sum_over(array, axis):
    size = lax.axis_size(axis)
    if size & (size - 1) or size > 16:
        return lax.psum(array, axis)
    bit = 1
    while bit < size:
        array = array + swap(array, axis, bit)
        bit *= 2
    return array


def gather_rows(block):
    other_core = swap(block, "tensor", 1)
    far = swap(block, "tensor", 2)
    far_core = swap(far, "tensor", 1)
    return jnp.concatenate([block, other_core, far, far_core], axis=0)


def scatter_rows(partial):
    rows = partial.shape[0] // 4
    own, other_core, far, far_core = (partial[i * rows : (i + 1) * rows] for i in range(4))
    far_sum = (far.astype(F32) + swap(far_core, "tensor", 1).astype(F32)).astype(BF16)
    from_far = swap(far_sum, "tensor", 2)
    from_core = swap(other_core, "tensor", 1)
    return own.astype(F32) + from_core.astype(F32) + from_far.astype(F32)


class Ring:
    def __init__(self):
        self.size = lax.axis_size("dp")
        half = self.size // 2
        order = [2 * i for i in range(half)] + [2 * (self.size - 1 - i) + 1 for i in range(half, self.size)]
        self.up = [(order[i], order[(i + 1) % self.size]) for i in range(self.size)]
        self.down = [(b, a) for a, b in self.up]
        index = lax.axis_index("dp")
        row, column = index // 2, index % 2
        self.place = jnp.where(column == 0, row, self.size - 1 - row)
        self.small = self.size <= 16 and self.size % 2 == 0

    def owner(self, distance):
        place = (self.place + distance + 2 * self.size) % self.size
        return jnp.where(place < self.size // 2, 2 * place, 2 * (self.size - 1 - place) + 1)

    def step(self, going_up, going_down):
        return lax.ppermute(going_up, "dp", self.up), lax.ppermute(going_down, "dp", self.down)

    def gather(self, block, splits):
        if not self.small:
            whole = lax.all_gather(block.reshape(1, *block.shape), "dp", axis=0, tiled=True)
            parts, start = [], 0
            for rows in splits:
                part = whole[:, start : start + rows]
                parts.append(part.reshape(self.size * rows, block.shape[1]))
                start += rows
            yield
            while True:
                yield parts
        total = block.shape[0]
        wholes = [jnp.zeros((self.size * rows, block.shape[1]), block.dtype) for rows in splits]

        def put(part, first, distance):
            start = 0
            for i, rows in enumerate(splits):
                low, high = max(start, first), min(start + rows, first + part.shape[0])
                if low < high:
                    wholes[i] = lax.dynamic_update_slice_in_dim(
                        wholes[i],
                        part[low - first : high - first],
                        self.owner(distance) * rows + (low - start),
                        0,
                    )
                start += rows

        put(block, 0, 0)
        going_up = going_down = block
        middle = self.size // 2
        for step in range(1, middle):
            going_up, going_down = self.step(going_up, going_down)
            put(going_up, 0, -step)
            put(going_down, 0, step)
            gate = yield
            if gate is not None:
                going_up, going_down, _ = lax.optimization_barrier((going_up, going_down, gate))
        cut = total // 2
        first, second = self.step(going_up[:cut], going_down[cut:])
        put(first, 0, middle)
        put(second, cut, middle)
        while True:
            yield wholes

    def scatter(self, wholes):
        lengths = [whole.shape[0] // self.size for whole in wholes]
        if not self.small:
            owned = [
                lax.psum_scatter(whole.astype(BF16), "dp", scatter_dimension=0, tiled=True).astype(F32)
                for whole in wholes
            ]
            while True:
                yield owned

        def term(distance):
            pieces = [
                lax.dynamic_slice_in_dim(whole, self.owner(distance) * length, length, 0)
                for whole, length in zip(wholes, lengths)
            ]
            return jnp.concatenate(pieces, axis=0) if len(pieces) > 1 else pieces[0]

        middle = self.size // 2
        far = term(middle)
        cut = far.shape[0] // 2
        from_below, from_above = self.step(far[:cut], far[cut:])
        gate = yield
        for step in range(middle - 1, 0, -1):
            above, below = term(step), term(-step)
            if gate is not None:
                above, below, _ = lax.optimization_barrier((above, below, gate))
            if step == middle - 1:
                lower, upper = above[:cut].astype(F32) + from_below, below[cut:].astype(F32) + from_above
                above = jnp.concatenate([lower.astype(BF16), above[cut:]], axis=0)
                below = jnp.concatenate([below[:cut], upper.astype(BF16)], axis=0)
            else:
                above = (above.astype(F32) + from_below).astype(BF16)
                below = (below.astype(F32) + from_above).astype(BF16)
            from_below, from_above = self.step(above, below)
            gate = yield
        own = term(0)
        if gate is not None:
            own, _ = lax.optimization_barrier((own, gate))
        total = own.astype(F32) + from_below.astype(F32) + from_above.astype(F32)
        owned, start = [], 0
        for length in lengths:
            owned.append(total[start : start + length])
            start += length
        while True:
            yield owned


def row_major(array):
    return with_layout_constraint(array, Layout(major_to_minor=(0, 1)))


LANES = 128
QUERY_TILE = 256


def head_lanes(shape, head):
    lane = lax.broadcasted_iota(jnp.int32, shape, 1)
    return (lane >= head * HD) & (lane < (head + 1) * HD)


def keep_head(block, head):
    return jnp.where(head_lanes(block.shape, head), block, jnp.zeros_like(block))


def scores_of(key_block, query_block, counts_ref, score_scale):
    scores = matmul_nt(key_block, query_block) * score_scale
    rows = scores.shape[0] // counts_ref.shape[0]
    valid = [
        lax.broadcasted_iota(jnp.int32, (rows, scores.shape[1]), 0) < counts_ref[r]
        for r in range(counts_ref.shape[0])
    ]
    return jnp.where(jnp.concatenate(valid, axis=0), scores, MASKED)


def attention_kernel(score_scale, counts_ref, query_ref, key_ref, value_ref, context_ref, log_total_ref):
    keys, values = key_ref[...], value_ref[...]
    pieces = []
    for head in range(LANES // HD):
        scores = scores_of(keys, keep_head(query_ref[...], head), counts_ref, score_scale)
        row_peak = jnp.max(scores, axis=0, keepdims=True)
        raised = jnp.exp(scores - row_peak)
        total = jnp.sum(raised, axis=0, keepdims=True)
        log_total_ref[0, head : head + 1, :] = row_peak + jnp.log(total)
        probs_low = (raised * (1.0 / total)).astype(BF16)
        both = matmul_tn(values, probs_low)
        pieces.append(both[head * HD : (head + 1) * HD])
    context_ref[...] = jnp.concatenate(pieces, axis=0).T.astype(BF16)


def attention(qkv_low, counts, local_width, score_scale):
    seq_len = qkv_low.shape[0]
    pairs = local_width // LANES
    tiles = seq_len // QUERY_TILE
    return pl.pallas_call(
        functools.partial(attention_kernel, score_scale),
        grid=(pairs, tiles),
        in_specs=[
            pl.BlockSpec(memory_space=pltpu.SMEM),
            pl.BlockSpec((QUERY_TILE, LANES), lambda j, i: (i, j)),
            pl.BlockSpec((seq_len, LANES), lambda j, i: (0, pairs + j)),
            pl.BlockSpec((seq_len, LANES), lambda j, i: (0, 2 * pairs + j)),
        ],
        out_specs=[
            pl.BlockSpec((QUERY_TILE, LANES), lambda j, i: (i, j)),
            pl.BlockSpec((1, LANES // HD, QUERY_TILE), lambda j, i: (j, 0, i)),
        ],
        out_shape=[
            jax.ShapeDtypeStruct((seq_len, local_width), BF16),
            jax.ShapeDtypeStruct((pairs, LANES // HD, seq_len), F32),
        ],
        cost_estimate=pl.CostEstimate(
            flops=4 * seq_len * seq_len * local_width,
            bytes_accessed=8 * seq_len * local_width,
            transcendentals=seq_len * seq_len * local_width // HD,
        ),
        name="attention",
    )(counts, qkv_low, qkv_low, qkv_low)


def attention_grad_kernel(
    score_scale,
    counts_ref,
    query_ref,
    key_ref,
    value_ref,
    upstream_ref,
    log_total_ref,
    query_grad_ref,
    key_grad_ref,
    value_grad_ref,
    query_sum_ref,
    value_sum_ref,
    key_total,
    value_total,
):
    step = pl.program_id(1)

    @pl.when(step == 0)
    def _():
        key_total[...] = jnp.zeros_like(key_total)
        value_total[...] = jnp.zeros_like(value_total)
        query_sum_ref[...] = jnp.zeros_like(query_sum_ref)

    keys, values = key_ref[...], value_ref[...]
    pieces = []
    for head in range(LANES // HD):
        queries = keep_head(query_ref[...], head)
        upstream = keep_head(upstream_ref[...], head)
        scores = scores_of(keys, queries, counts_ref, score_scale)
        probs = jnp.exp(scores - log_total_ref[0, head : head + 1, :])
        prob_grad = matmul_nt(values, upstream)
        row_inner = jnp.sum(probs * prob_grad, axis=0, keepdims=True)
        score_grad = (probs * (prob_grad - row_inner) * score_scale).astype(BF16)
        value_total[...] += matmul(probs.astype(BF16), upstream)
        key_total[...] += matmul(score_grad, queries)
        both = matmul_tn(keys, score_grad)
        pieces.append(both[head * HD : (head + 1) * HD])
    query_grad = jnp.concatenate(pieces, axis=0).T
    query_grad_ref[...] = query_grad.astype(BF16)
    query_sum_ref[...] += jnp.sum(query_grad, axis=0, keepdims=True)

    @pl.when(step == pl.num_programs(1) - 1)
    def _():
        key_grad_ref[...] = key_total[...].astype(BF16)
        value_grad_ref[...] = value_total[...].astype(BF16)
        value_sum_ref[...] = jnp.sum(value_total[...], axis=0, keepdims=True)


def attention_grad(qkv_low, upstream, log_total, counts, local_width, score_scale):
    seq_len = qkv_low.shape[0]
    pairs = local_width // LANES
    tiles = seq_len // QUERY_TILE
    tile_spec = pl.BlockSpec((QUERY_TILE, LANES), lambda j, i: (i, j))
    whole_spec = pl.BlockSpec((seq_len, LANES), lambda j, i: (0, j))
    sum_spec = pl.BlockSpec((1, LANES), lambda j, i: (0, j))
    low = jax.ShapeDtypeStruct((seq_len, local_width), BF16)
    sums = jax.ShapeDtypeStruct((1, local_width), F32)
    return pl.pallas_call(
        functools.partial(attention_grad_kernel, score_scale),
        grid=(pairs, tiles),
        in_specs=[
            pl.BlockSpec(memory_space=pltpu.SMEM),
            tile_spec,
            pl.BlockSpec((seq_len, LANES), lambda j, i: (0, pairs + j)),
            pl.BlockSpec((seq_len, LANES), lambda j, i: (0, 2 * pairs + j)),
            tile_spec,
            pl.BlockSpec((1, LANES // HD, QUERY_TILE), lambda j, i: (j, 0, i)),
        ],
        out_specs=[tile_spec, whole_spec, whole_spec, sum_spec, sum_spec],
        out_shape=[low, low, low, sums, sums],
        scratch_shapes=[pltpu.VMEM((seq_len, LANES), F32), pltpu.VMEM((seq_len, LANES), F32)],
        cost_estimate=pl.CostEstimate(
            flops=10 * seq_len * seq_len * local_width,
            bytes_accessed=16 * seq_len * local_width,
            transcendentals=seq_len * seq_len * local_width // HD,
        ),
        name="attention_grad",
    )(counts, qkv_low, qkv_low, qkv_low, upstream, log_total)


def shards(
    hidden_in,
    cotangent,
    lengths,
    query_weight,
    key_weight,
    value_weight,
    output_weight,
    up_weight,
    down_weight,
    query_bias,
    value_bias,
    output_bias,
    up_bias,
    down_bias,
    first_gain,
    first_shift,
    second_gain,
    second_shift,
):
    n_tensor = lax.axis_size("tensor")
    tensor_index = lax.axis_index("tensor")
    local_rows = hidden_in.shape[0]
    local_width = query_weight.shape[1]
    score_scale = HD ** (-0.5)
    ring = Ring()
    blocks = jnp.arange(n_tensor, dtype=jnp.int32) ^ tensor_index
    counts = lengths[0] - blocks * local_rows

    packed = row_major(jnp.concatenate([query_weight, key_weight, value_weight, output_weight.T], axis=1))
    first_ring = ring.gather(packed, (packed.shape[0],))
    next(first_ring)
    hidden_full = gather_rows(hidden_in)
    stacked = row_major(jnp.concatenate([up_weight, down_weight.T], axis=0))
    first_ring.send(None)
    first_ring.send(None)
    (packed_full,) = first_ring.send(None)
    second_ring = ring.gather(stacked, (up_weight.shape[0], down_weight.shape[1]))
    next(second_ring)
    qkv_full = packed_full[:, : 3 * local_width]
    output_turned = packed_full[:, 3 * local_width :]

    qkv_bias = jnp.concatenate([query_bias, jnp.zeros_like(query_bias), value_bias])
    qkv_low = (matmul(hidden_full, qkv_full) + qkv_bias).astype(BF16)
    context, log_total = attention(qkv_low, counts, local_width, score_scale)
    second_ring.send(context[:8, :128])
    attn_rows = scatter_rows(matmul_nt(context, output_turned).astype(BF16))
    first_sum = hidden_in.astype(F32) + attn_rows + output_bias
    first_out, first_normed, first_inverse = norm_forward(first_sum, first_gain, first_shift)
    first_low = first_out.astype(BF16)
    second_ring.send(first_low[:8, :128])
    normed_full = gather_rows(first_low)
    up_full, down_turned = second_ring.send(None)
    pre_act = matmul(normed_full, up_full) + up_bias
    activated, slope = lax.optimization_barrier((gelu_value(pre_act).astype(BF16), gelu_slope(pre_act)))
    mlp_rows = scatter_rows(matmul_nt(activated, down_turned).astype(BF16))
    second_sum = first_out + mlp_rows + down_bias
    second_out, second_normed, second_inverse = norm_forward(second_sum, second_gain, second_shift)
    hidden_out = second_out.astype(BF16)

    upstream = cotangent.astype(F32)
    grad_second_gain = jnp.sum(upstream * second_normed, axis=0)
    grad_second_shift = jnp.sum(upstream, axis=0)
    second_grad = norm_backward(upstream, second_gain, second_normed, second_inverse)
    grad_down_bias = jnp.sum(second_grad, axis=0)
    second_full = gather_rows(second_grad.astype(BF16))
    pre_grad = matmul(second_full, down_turned) * slope
    grad_up_bias = jnp.sum(pre_grad, axis=0)
    pre_low = pre_grad.astype(BF16)
    partial = matmul_nt(pre_low, up_full).astype(BF16)
    normed_gated, second_gated, _ = lax.optimization_barrier((normed_full, second_full, partial[:8, :128]))
    grad_up = matmul_tn(normed_gated, pre_low).astype(BF16)
    grad_down = matmul_tn(second_gated, activated).astype(BF16)
    second_back = ring.scatter([grad_up, grad_down])
    next(second_back)
    first_grad_in = second_grad + scatter_rows(partial)
    grad_first_gain = jnp.sum(first_grad_in * first_normed, axis=0)
    grad_first_shift = jnp.sum(first_grad_in, axis=0)
    first_grad = norm_backward(first_grad_in, first_gain, first_normed, first_inverse)
    grad_output_bias = jnp.sum(first_grad, axis=0)
    grad_low = first_grad.astype(BF16)
    second_back.send(grad_low[:8, :128])
    attn_grad_full = gather_rows(grad_low)
    context_grad = matmul(attn_grad_full, output_turned).astype(BF16)
    second_back.send(context_grad[:8, :128])

    everywhere = jnp.stack(
        [grad_second_gain, grad_second_shift, grad_down_bias, grad_first_gain, grad_first_shift, grad_output_bias]
    )
    everywhere = sum_over(everywhere, "tensor")

    query_low, key_low, value_low, query_sum, value_sum = attention_grad(
        qkv_low, context_grad, log_total, counts, local_width, score_scale
    )
    second_back.send(query_sum)
    narrow = jnp.concatenate([query_sum.reshape(-1), value_sum.reshape(-1), grad_up_bias])
    low = jnp.concatenate([query_low, key_low, value_low], axis=1)
    packed_grad = jnp.concatenate([matmul_tn(hidden_full, low), matmul_tn(attn_grad_full, context)], axis=1)
    packed_grad = packed_grad.astype(BF16)
    first_back = ring.scatter([packed_grad])
    next(first_back)
    back = scatter_rows(matmul_nt(low, qkv_full).astype(BF16))
    grad_in = (first_grad + back).astype(BF16)
    vectors = sum_over(jnp.concatenate([everywhere.reshape(-1), narrow]), "dp")
    everywhere = vectors[: everywhere.size].reshape(everywhere.shape)
    narrow = vectors[everywhere.size :]
    first_back.send(None)
    first_back.send(None)
    first_back.send(None)
    up_owned, down_owned = second_back.send(None)
    (packed_owned,) = first_back.send(None)
    return (
        hidden_out,
        grad_in,
        packed_owned[:, :local_width],
        packed_owned[:, local_width : 2 * local_width],
        packed_owned[:, 2 * local_width : 3 * local_width],
        packed_owned[:, 3 * local_width :].T,
        up_owned,
        down_owned.T,
        narrow[:local_width],
        narrow[local_width : 2 * local_width],
        everywhere[5],
        narrow[2 * local_width :],
        everywhere[2],
        everywhere[3],
        everywhere[4],
        everywhere[0],
        everywhere[1],
    )


def solution(mesh):
    in_specs = (
        P(("dp", "tensor"), None),
        P(("dp", "tensor"), None),
        P("dp"),
        P("dp", "tensor"),
        P("dp", "tensor"),
        P("dp", "tensor"),
        P("tensor", "dp"),
        P("dp", "tensor"),
        P("tensor", "dp"),
        P("tensor"),
        P("tensor"),
        P(),
        P("tensor"),
        P(),
        P(),
        P(),
        P(),
        P(),
    )
    out_specs = (
        P(("dp", "tensor"), None),
        P(("dp", "tensor"), None),
        P("dp", "tensor"),
        P("dp", "tensor"),
        P("dp", "tensor"),
        P("tensor", "dp"),
        P("dp", "tensor"),
        P("tensor", "dp"),
        P("tensor"),
        P("tensor"),
        P(),
        P("tensor"),
        P(),
        P(),
        P(),
        P(),
        P(),
    )
    return jax.shard_map(shards, mesh=mesh, in_specs=in_specs, out_specs=out_specs, check_vma=False)
```

```python
import functools

import jax
import jax.numpy as jnp
from jax import lax
from jax.experimental import pallas as pl
from jax.experimental.layout import Layout, with_layout_constraint
from jax.experimental.pallas import tpu as pltpu
from jax.sharding import PartitionSpec as P


HD = 64


EPSILON = 1e-12
ROOT_HALF = 0.7071067811865476
INV_ROOT_TWO_PI = 0.3989422804014327
MASKED = -1e30
BF16 = jnp.bfloat16
F32 = jnp.float32


def matmul(left_side, right_side):
    return jnp.dot(left_side, right_side, preferred_element_type=F32)


def matmul_nt(left_side, right_side):
    return lax.dot_general(left_side, right_side, (((1,), (1,)), ((), ())), preferred_element_type=F32)


def matmul_tn(left_side, right_side):
    return lax.dot_general(left_side, right_side, (((0,), (0,)), ((), ())), preferred_element_type=F32)


def gelu_value(pre_act):
    return pre_act * 0.5 * (1.0 + lax.erf(pre_act * ROOT_HALF))


def gelu_slope(pre_act):
    cumulative = 0.5 * (1.0 + lax.erf(pre_act * ROOT_HALF))
    density = jnp.exp(-0.5 * pre_act * pre_act) * INV_ROOT_TWO_PI
    return cumulative + pre_act * density


def norm_forward(summed, gain_vector, shift_vector):
    centre = summed - jnp.mean(summed, axis=-1, keepdims=True)
    spread = jnp.mean(centre * centre, axis=-1, keepdims=True)
    inverse = lax.rsqrt(spread + EPSILON)
    normed = centre * inverse
    return (normed * gain_vector + shift_vector, normed, inverse)


def norm_backward(upstream, gain_vector, normed, inverse):
    scaled = upstream * gain_vector
    return inverse * (
        scaled
        - jnp.mean(scaled, axis=-1, keepdims=True)
        - normed * jnp.mean(scaled * normed, axis=-1, keepdims=True)
    )


def swap(array, axis, bit):
    size = lax.axis_size(axis)
    return lax.ppermute(array, axis, [(i, i ^ bit) for i in range(size)])


def sum_over(array, axis):
    size = lax.axis_size(axis)
    if size & (size - 1) or size > 16:
        return lax.psum(array, axis)
    bit = 1
    while bit < size:
        array = array + swap(array, axis, bit)
        bit *= 2
    return array


def gather_rows(block):
    far = swap(block, "tensor", 2)
    other_core = swap(block, "tensor", 1)
    far_core = swap(far, "tensor", 1)
    return jnp.concatenate([block, other_core, far, far_core], axis=0)


def scatter_rows(partial):
    rows = partial.shape[0] // 4
    own, other_core, far, far_core = (partial[i * rows : (i + 1) * rows] for i in range(4))
    far_sum = (far.astype(F32) + swap(far_core, "tensor", 1).astype(F32)).astype(BF16)
    from_far = swap(far_sum, "tensor", 2)
    from_core = swap(other_core, "tensor", 1)
    return own.astype(F32) + from_core.astype(F32) + from_far.astype(F32)


class Ring:
    def __init__(self):
        self.size = lax.axis_size("dp")
        half = self.size // 2
        order = [2 * i for i in range(half)] + [2 * (self.size - 1 - i) + 1 for i in range(half, self.size)]
        self.up = [(order[i], order[(i + 1) % self.size]) for i in range(self.size)]
        self.down = [(b, a) for a, b in self.up]
        index = lax.axis_index("dp")
        row, column = index // 2, index % 2
        self.place = jnp.where(column == 0, row, self.size - 1 - row)
        self.small = self.size <= 16 and self.size % 2 == 0

    def owner(self, distance):
        place = (self.place + distance + 2 * self.size) % self.size
        return jnp.where(place < self.size // 2, 2 * place, 2 * (self.size - 1 - place) + 1)

    def step(self, going_up, going_down):
        going_up = lax.ppermute(going_up, "dp", self.up)
        going_down = lax.ppermute(going_down, "dp", self.down)
        return going_up, going_down

    def gather(self, block, splits):
        if not self.small:
            whole = lax.all_gather(block.reshape(1, *block.shape), "dp", axis=0, tiled=True)
            parts, start = [], 0
            for rows in splits:
                part = whole[:, start : start + rows]
                parts.append(part.reshape(self.size * rows, block.shape[1]))
                start += rows
            return parts
        total = block.shape[0]
        wholes = [jnp.zeros((self.size * rows, block.shape[1]), block.dtype) for rows in splits]

        def put(part, first, distance):
            start = 0
            for i, rows in enumerate(splits):
                low, high = max(start, first), min(start + rows, first + part.shape[0])
                if low < high:
                    wholes[i] = lax.dynamic_update_slice_in_dim(
                        wholes[i],
                        part[low - first : high - first],
                        self.owner(distance) * rows + (low - start),
                        0,
                    )
                start += rows

        put(block, 0, 0)
        going_up = going_down = block
        middle = self.size // 2
        for step in range(1, middle):
            going_up, going_down = self.step(going_up, going_down)
            put(going_up, 0, -step)
            put(going_down, 0, step)
        cut = total // 2
        first, second = self.step(going_up[:cut], going_down[cut:])
        put(first, 0, middle)
        put(second, cut, middle)
        return wholes

    def scatter(self, wholes):
        lengths = [whole.shape[0] // self.size for whole in wholes]
        if not self.small:
            return [
                lax.psum_scatter(whole.astype(BF16), "dp", scatter_dimension=0, tiled=True).astype(F32)
                for whole in wholes
            ]

        def term(distance):
            pieces = [
                lax.dynamic_slice_in_dim(whole, self.owner(distance) * length, length, 0)
                for whole, length in zip(wholes, lengths)
            ]
            return jnp.concatenate(pieces, axis=0) if len(pieces) > 1 else pieces[0]

        middle = self.size // 2
        far = term(middle)
        cut = far.shape[0] // 2
        from_below, from_above = self.step(far[:cut], far[cut:])
        for step in range(middle - 1, 0, -1):
            above, below = term(step), term(-step)
            if step == middle - 1:
                lower, upper = above[:cut].astype(F32) + from_below, below[cut:].astype(F32) + from_above
                above = jnp.concatenate([lower.astype(BF16), above[cut:]], axis=0)
                below = jnp.concatenate([below[:cut], upper.astype(BF16)], axis=0)
            else:
                above = (above.astype(F32) + from_below).astype(BF16)
                below = (below.astype(F32) + from_above).astype(BF16)
            from_below, from_above = self.step(above, below)
        total = term(0).astype(F32) + from_below.astype(F32) + from_above.astype(F32)
        owned, start = [], 0
        for length in lengths:
            owned.append(total[start : start + length])
            start += length
        return owned


def row_major(array):
    return with_layout_constraint(array, Layout(major_to_minor=(0, 1)))


LANES = 128
QUERY_TILE = 256


def head_lanes(shape, head):
    lane = lax.broadcasted_iota(jnp.int32, shape, 1)
    return (lane >= head * HD) & (lane < (head + 1) * HD)


def keep_head(block, head):
    return jnp.where(head_lanes(block.shape, head), block, jnp.zeros_like(block))


def scores_of(key_block, query_block, counts_ref, score_scale):
    scores = matmul_nt(key_block, query_block) * score_scale
    rows = scores.shape[0] // counts_ref.shape[0]
    valid = [
        lax.broadcasted_iota(jnp.int32, (rows, scores.shape[1]), 0) < counts_ref[r]
        for r in range(counts_ref.shape[0])
    ]
    return jnp.where(jnp.concatenate(valid, axis=0), scores, MASKED)


def attention_kernel(score_scale, counts_ref, query_ref, key_ref, value_ref, context_ref, log_total_ref):
    keys, values = key_ref[...], value_ref[...]
    pieces = []
    for head in range(LANES // HD):
        scores = scores_of(keys, keep_head(query_ref[...], head), counts_ref, score_scale)
        row_peak = jnp.max(scores, axis=0, keepdims=True)
        raised = jnp.exp(scores - row_peak)
        total = jnp.sum(raised, axis=0, keepdims=True)
        log_total_ref[0, head : head + 1, :] = row_peak + jnp.log(total)
        probs_low = (raised * (1.0 / total)).astype(BF16)
        both = matmul_tn(values, probs_low)
        pieces.append(both[head * HD : (head + 1) * HD])
    context_ref[...] = jnp.concatenate(pieces, axis=0).T.astype(BF16)


def attention(qkv_low, counts, local_width, score_scale):
    seq_len = qkv_low.shape[0]
    pairs = local_width // LANES
    tiles = seq_len // QUERY_TILE
    return pl.pallas_call(
        functools.partial(attention_kernel, score_scale),
        grid=(pairs, tiles),
        in_specs=[
            pl.BlockSpec(memory_space=pltpu.SMEM),
            pl.BlockSpec((QUERY_TILE, LANES), lambda j, i: (i, j)),
            pl.BlockSpec((seq_len, LANES), lambda j, i: (0, pairs + j)),
            pl.BlockSpec((seq_len, LANES), lambda j, i: (0, 2 * pairs + j)),
        ],
        out_specs=[
            pl.BlockSpec((QUERY_TILE, LANES), lambda j, i: (i, j)),
            pl.BlockSpec((1, LANES // HD, QUERY_TILE), lambda j, i: (j, 0, i)),
        ],
        out_shape=[
            jax.ShapeDtypeStruct((seq_len, local_width), BF16),
            jax.ShapeDtypeStruct((pairs, LANES // HD, seq_len), F32),
        ],
        cost_estimate=pl.CostEstimate(
            flops=4 * seq_len * seq_len * local_width,
            bytes_accessed=8 * seq_len * local_width,
            transcendentals=seq_len * seq_len * local_width // HD,
        ),
        name="attention",
    )(counts, qkv_low, qkv_low, qkv_low)


def attention_grad_kernel(
    score_scale,
    counts_ref,
    query_ref,
    key_ref,
    value_ref,
    upstream_ref,
    log_total_ref,
    low_ref,
    query_sum_ref,
    value_sum_ref,
    key_total,
    value_total,
):
    pair, step = pl.program_id(0), pl.program_id(1)
    width = low_ref.shape[1] // 3

    @pl.when(step == 0)
    def _():
        key_total[...] = jnp.zeros_like(key_total)
        value_total[...] = jnp.zeros_like(value_total)
        query_sum_ref[...] = jnp.zeros_like(query_sum_ref)

    keys, values = key_ref[...], value_ref[...]
    pieces = []
    for head in range(LANES // HD):
        queries = keep_head(query_ref[...], head)
        upstream = keep_head(upstream_ref[...], head)
        scores = scores_of(keys, queries, counts_ref, score_scale)
        probs = jnp.exp(scores - log_total_ref[0, head : head + 1, :])
        prob_grad = matmul_nt(values, upstream)
        row_inner = jnp.sum(probs * prob_grad, axis=0, keepdims=True)
        score_grad = (probs * (prob_grad - row_inner) * score_scale).astype(BF16)
        value_total[...] += matmul(probs.astype(BF16), upstream)
        key_total[...] += matmul(score_grad, queries)
        both = matmul_tn(keys, score_grad)
        pieces.append(both[head * HD : (head + 1) * HD])
    query_grad = jnp.concatenate(pieces, axis=0).T
    rows = pl.ds(pl.multiple_of(step * QUERY_TILE, QUERY_TILE), QUERY_TILE)
    start = pl.multiple_of(pair * LANES, LANES)
    low_ref[rows, pl.ds(start, LANES)] = query_grad.astype(BF16)
    query_sum_ref[...] += jnp.sum(query_grad, axis=0, keepdims=True)

    @pl.when(step == pl.num_programs(1) - 1)
    def _():
        low_ref[:, pl.ds(start + width, LANES)] = key_total[...].astype(BF16)
        low_ref[:, pl.ds(start + 2 * width, LANES)] = value_total[...].astype(BF16)
        value_sum_ref[...] = jnp.sum(value_total[...], axis=0, keepdims=True)


def attention_grad(qkv_low, upstream, log_total, counts, local_width, score_scale):
    seq_len = qkv_low.shape[0]
    pairs = local_width // LANES
    tiles = seq_len // QUERY_TILE
    tile_spec = pl.BlockSpec((QUERY_TILE, LANES), lambda j, i: (i, j))
    sum_spec = pl.BlockSpec((1, LANES), lambda j, i: (0, j))
    sums = jax.ShapeDtypeStruct((1, local_width), F32)
    return pl.pallas_call(
        functools.partial(attention_grad_kernel, score_scale),
        grid=(pairs, tiles),
        in_specs=[
            pl.BlockSpec(memory_space=pltpu.SMEM),
            tile_spec,
            pl.BlockSpec((seq_len, LANES), lambda j, i: (0, pairs + j)),
            pl.BlockSpec((seq_len, LANES), lambda j, i: (0, 2 * pairs + j)),
            tile_spec,
            pl.BlockSpec((1, LANES // HD, QUERY_TILE), lambda j, i: (j, 0, i)),
        ],
        out_specs=[pl.BlockSpec((seq_len, 3 * local_width), lambda j, i: (0, 0)), sum_spec, sum_spec],
        out_shape=[jax.ShapeDtypeStruct((seq_len, 3 * local_width), BF16), sums, sums],
        scratch_shapes=[pltpu.VMEM((seq_len, LANES), F32), pltpu.VMEM((seq_len, LANES), F32)],
        cost_estimate=pl.CostEstimate(
            flops=10 * seq_len * seq_len * local_width,
            bytes_accessed=16 * seq_len * local_width,
            transcendentals=seq_len * seq_len * local_width // HD,
        ),
        name="attention_grad",
    )(counts, qkv_low, qkv_low, qkv_low, upstream, log_total)


def layer(
    hidden_in,
    cotangent,
    lengths,
    query_weight,
    key_weight,
    value_weight,
    output_weight,
    up_weight,
    down_weight,
    query_bias,
    value_bias,
    output_bias,
    up_bias,
    down_bias,
    first_gain,
    first_shift,
    second_gain,
    second_shift,
):
    n_tensor = lax.axis_size("tensor")
    tensor_index = lax.axis_index("tensor")
    local_rows = hidden_in.shape[0]
    local_width = query_weight.shape[1]
    score_scale = HD ** (-0.5)
    ring = Ring()
    blocks = jnp.arange(n_tensor, dtype=jnp.int32) ^ tensor_index
    counts = lengths[0] - blocks * local_rows

    packed = row_major(jnp.concatenate([query_weight, key_weight, value_weight, output_weight.T], axis=1))
    (packed_full,) = ring.gather(packed, (packed.shape[0],))
    hidden_full = gather_rows(hidden_in)
    stacked = row_major(jnp.concatenate([up_weight, down_weight.T], axis=0))
    up_full, down_turned = ring.gather(stacked, (up_weight.shape[0], down_weight.shape[1]))
    qkv_full = packed_full[:, : 3 * local_width]
    output_turned = packed_full[:, 3 * local_width :]

    qkv_bias = jnp.concatenate([query_bias, jnp.zeros_like(query_bias), value_bias])
    qkv_low = (matmul(hidden_full, qkv_full) + qkv_bias).astype(BF16)
    context, log_total = attention(qkv_low, counts, local_width, score_scale)
    attn_rows = scatter_rows(matmul_nt(context, output_turned).astype(BF16))
    first_sum = hidden_in.astype(F32) + attn_rows + output_bias
    first_out, first_normed, first_inverse = norm_forward(first_sum, first_gain, first_shift)
    normed_full = gather_rows(first_out.astype(BF16))
    pre_act = matmul(normed_full, up_full) + up_bias
    activated, slope = lax.optimization_barrier((gelu_value(pre_act).astype(BF16), gelu_slope(pre_act)))
    mlp_rows = scatter_rows(matmul_nt(activated, down_turned).astype(BF16))
    second_sum = first_out + mlp_rows + down_bias
    second_out, second_normed, second_inverse = norm_forward(second_sum, second_gain, second_shift)
    hidden_out = second_out.astype(BF16)

    upstream = cotangent.astype(F32)
    grad_second_gain = jnp.sum(upstream * second_normed, axis=0)
    grad_second_shift = jnp.sum(upstream, axis=0)
    second_grad = norm_backward(upstream, second_gain, second_normed, second_inverse)
    grad_down_bias = jnp.sum(second_grad, axis=0)
    second_full = gather_rows(second_grad.astype(BF16))
    pre_grad = matmul(second_full, down_turned) * slope
    grad_up_bias = jnp.sum(pre_grad, axis=0)
    pre_low = pre_grad.astype(BF16)
    partial = matmul_nt(pre_low, up_full).astype(BF16)
    grad_down = row_major(matmul_tn(second_full, activated).astype(BF16))
    grad_up = row_major(matmul_tn(normed_full, pre_low).astype(BF16))
    up_owned, down_owned = ring.scatter([grad_up, grad_down])
    first_grad_in = second_grad + scatter_rows(partial)
    grad_first_gain = jnp.sum(first_grad_in * first_normed, axis=0)
    grad_first_shift = jnp.sum(first_grad_in, axis=0)
    first_grad = norm_backward(first_grad_in, first_gain, first_normed, first_inverse)
    grad_output_bias = jnp.sum(first_grad, axis=0)
    attn_grad_full = gather_rows(first_grad.astype(BF16))
    context_grad = matmul(attn_grad_full, output_turned).astype(BF16)

    everywhere = jnp.stack(
        [grad_second_gain, grad_second_shift, grad_down_bias, grad_first_gain, grad_first_shift, grad_output_bias]
    )
    everywhere = sum_over(everywhere, "tensor")

    low, query_sum, value_sum = attention_grad(
        qkv_low, context_grad, log_total, counts, local_width, score_scale
    )
    qkv_grad = matmul_tn(hidden_full, low).astype(BF16)
    output_grad = matmul_tn(attn_grad_full, context).astype(BF16)
    packed_grad = row_major(jnp.concatenate([qkv_grad, output_grad], axis=1))
    (packed_owned,) = ring.scatter([packed_grad])
    packed_owned = row_major(packed_owned)
    back = scatter_rows(matmul_nt(low, qkv_full).astype(BF16))
    grad_in = (first_grad + back).astype(BF16)
    narrow = jnp.concatenate([query_sum.reshape(-1), value_sum.reshape(-1), grad_up_bias])
    vectors = sum_over(jnp.concatenate([everywhere.reshape(-1), narrow]), "dp")
    everywhere = vectors[: everywhere.size].reshape(everywhere.shape)
    narrow = vectors[everywhere.size :]
    return (
        hidden_out,
        grad_in,
        packed_owned[:, :local_width],
        packed_owned[:, local_width : 2 * local_width],
        packed_owned[:, 2 * local_width : 3 * local_width],
        packed_owned[:, 3 * local_width :].T,
        up_owned,
        down_owned.T,
        narrow[:local_width],
        narrow[local_width : 2 * local_width],
        everywhere[5],
        narrow[2 * local_width :],
        everywhere[2],
        everywhere[3],
        everywhere[4],
        everywhere[0],
        everywhere[1],
    )


def solution(mesh):
    in_specs = (
        P(("dp", "tensor"), None),
        P(("dp", "tensor"), None),
        P("dp"),
        P("dp", "tensor"),
        P("dp", "tensor"),
        P("dp", "tensor"),
        P("tensor", "dp"),
        P("dp", "tensor"),
        P("tensor", "dp"),
        P("tensor"),
        P("tensor"),
        P(),
        P("tensor"),
        P(),
        P(),
        P(),
        P(),
        P(),
    )
    out_specs = (
        P(("dp", "tensor"), None),
        P(("dp", "tensor"), None),
        P("dp", "tensor"),
        P("dp", "tensor"),
        P("dp", "tensor"),
        P("tensor", "dp"),
        P("dp", "tensor"),
        P("tensor", "dp"),
        P("tensor"),
        P("tensor"),
        P(),
        P("tensor"),
        P(),
        P(),
        P(),
        P(),
        P(),
    )
    return jax.shard_map(layer, mesh=mesh, in_specs=in_specs, out_specs=out_specs, check_vma=False)
```

```python
import functools

import jax
import jax.numpy as jnp
from jax import lax
from jax.experimental import pallas as pl
from jax.experimental.layout import Layout, with_layout_constraint
from jax.experimental.pallas import tpu as pltpu
from jax.sharding import PartitionSpec as P


HD = 64


EPSILON = 1e-12
ROOT_HALF = 0.7071067811865476
INV_ROOT_TWO_PI = 0.3989422804014327
MASKED = -1e30
BF16 = jnp.bfloat16
F32 = jnp.float32
KERNEL_VMEM = 16 << 20


def matmul(left_side, right_side):
    return jnp.dot(left_side, right_side, preferred_element_type=F32)


def matmul_nt(left_side, right_side):
    return lax.dot_general(left_side, right_side, (((1,), (1,)), ((), ())), preferred_element_type=F32)


def matmul_tn(left_side, right_side):
    return lax.dot_general(left_side, right_side, (((0,), (0,)), ((), ())), preferred_element_type=F32)


def gelu_value(pre_act):
    return pre_act * 0.5 * (1.0 + lax.erf(pre_act * ROOT_HALF))


def gelu_slope(pre_act):
    cumulative = 0.5 * (1.0 + lax.erf(pre_act * ROOT_HALF))
    density = jnp.exp(-0.5 * pre_act * pre_act) * INV_ROOT_TWO_PI
    return cumulative + pre_act * density


def norm_forward(summed, gain_vector, shift_vector):
    centre = summed - jnp.mean(summed, axis=-1, keepdims=True)
    spread = jnp.mean(centre * centre, axis=-1, keepdims=True)
    inverse = lax.rsqrt(spread + EPSILON)
    normed = centre * inverse
    return (normed * gain_vector + shift_vector, normed, inverse)


def norm_backward(upstream, gain_vector, normed, inverse):
    scaled = upstream * gain_vector
    return inverse * (
        scaled
        - jnp.mean(scaled, axis=-1, keepdims=True)
        - normed * jnp.mean(scaled * normed, axis=-1, keepdims=True)
    )


def swap(array, axis, bit):
    size = lax.axis_size(axis)
    return lax.ppermute(array, axis, [(i, i ^ bit) for i in range(size)])


def gather_rows(block):
    far = swap(block, "tensor", 2)
    other_core = swap(block, "tensor", 1)
    far_core = swap(far, "tensor", 1)
    return jnp.concatenate([block, other_core, far, far_core], axis=0)


def scatter_rows(partial):
    rows = partial.shape[0] // 4
    own, other_core, far, far_core = (partial[i * rows : (i + 1) * rows] for i in range(4))
    far_sum = (far.astype(F32) + swap(far_core, "tensor", 1).astype(F32)).astype(BF16)
    from_far = swap(far_sum, "tensor", 2)
    from_core = swap(other_core, "tensor", 1)
    return own.astype(F32) + from_core.astype(F32) + from_far.astype(F32)


class Ring:
    def __init__(self):
        self.size = lax.axis_size("dp")
        half = self.size // 2
        order = [2 * i for i in range(half)] + [2 * (self.size - 1 - i) + 1 for i in range(half, self.size)]
        self.up = [(order[i], order[(i + 1) % self.size]) for i in range(self.size)]
        self.down = [(b, a) for a, b in self.up]
        index = lax.axis_index("dp")
        row, column = index // 2, index % 2
        self.place = jnp.where(column == 0, row, self.size - 1 - row)
        self.small = self.size <= 16 and self.size % 2 == 0

    def owner(self, distance):
        place = (self.place + distance + 2 * self.size) % self.size
        return jnp.where(place < self.size // 2, 2 * place, 2 * (self.size - 1 - place) + 1)

    def step(self, going_up, going_down):
        going_up = lax.ppermute(going_up, "dp", self.up)
        going_down = lax.ppermute(going_down, "dp", self.down)
        return going_up, going_down

    def gather(self, block, splits):
        if not self.small:
            whole = lax.all_gather(block.reshape(1, *block.shape), "dp", axis=0, tiled=True)
            parts, start = [], 0
            for rows in splits:
                part = whole[:, start : start + rows]
                parts.append(part.reshape(self.size * rows, block.shape[1]))
                start += rows
            return parts
        total = block.shape[0]
        wholes = [jnp.zeros((self.size * rows, block.shape[1]), block.dtype) for rows in splits]

        def put(part, first, distance):
            start = 0
            for i, rows in enumerate(splits):
                low, high = max(start, first), min(start + rows, first + part.shape[0])
                if low < high:
                    wholes[i] = lax.dynamic_update_slice_in_dim(
                        wholes[i],
                        part[low - first : high - first],
                        self.owner(distance) * rows + (low - start),
                        0,
                    )
                start += rows

        put(block, 0, 0)
        going_up = going_down = block
        middle = self.size // 2
        for step in range(1, middle):
            going_up, going_down = self.step(going_up, going_down)
            put(going_up, 0, -step)
            put(going_down, 0, step)
        cut = total // 2
        first, second = self.step(going_up[:cut], going_down[cut:])
        put(first, 0, middle)
        put(second, cut, middle)
        return wholes

    def scatter(self, layout, shapes, vectors=()):
        if not self.small:
            owned = []
            for row in layout:
                for left, right in row:
                    whole = matmul_tn(left, right).astype(BF16)
                    owned.append(lax.psum_scatter(whole, "dp", scatter_dimension=0, tiled=True).astype(F32))
            outs = []
            for term, start, stop, turned in shapes:
                piece = owned[term][:, start:stop]
                outs.append(piece.T if turned else piece)
            if vectors:
                partial, other, *singles = vectors
                rows = [(partial + other)[i : i + 1] for i in range(partial.shape[0])] + singles
                outs.extend(lax.psum(rows, "dp"))
            return outs
        middle = self.size // 2
        arrived = list(ring_sum(layout, [self.owner(middle)] * 2, (), FIRST, (), vectors))
        for step in range(1, middle + 1):
            arrived[:2] = self.step(arrived[0], arrived[1])
            distance = middle - step
            stage = STEP if distance else LAST
            arrived = list(
                ring_sum(layout, [self.owner(distance), self.owner(-distance)], arrived, stage, shapes, vectors)
            )
        return arrived


FIRST, STEP, LAST = range(3)
VECTOR_ROWS = 8


def split_low(value):
    high = value.astype(BF16)
    return high, (value - high.astype(F32)).astype(BF16)


def ring_sum_kernel(places, stage, shapes, has_vectors, owners_ref, *refs):
    count = len(places)
    lefts, rights, rest = refs[:count], refs[count : 2 * count], refs[2 * count :]
    rows = places[0][2]
    total = max(place[0] for place in places) + rows
    half = total // 2
    extra = 2 * VECTOR_ROWS if has_vectors else 0

    def term(i, direction):
        start = pl.multiple_of(owners_ref[direction] * rows, rows)
        return matmul_tn(lefts[i][:, pl.ds(start, rows)], rights[i][...])

    def vectors_in(ref):
        first = ref.shape[0] - extra
        high = ref[first : first + VECTOR_ROWS].astype(F32)
        return high + ref[first + VECTOR_ROWS : first + extra].astype(F32)

    if has_vectors and stage == FIRST:
        partial_ref, other_ref, *single_refs = rest[:5]
        rest = rest[5:]
        sum_ref = rest[2]
        row, column = partial_ref.shape[0], 0
        sum_ref[...] = jnp.zeros_like(sum_ref)
        sum_ref[:row] = partial_ref[...] + other_ref[...]
        for ref in single_refs:
            width = ref.shape[1]
            if column + width > sum_ref.shape[1]:
                row, column = row + 1, 0
            sum_ref[row : row + 1, column : column + width] = ref[...]
            column += width
        high, low = split_low(sum_ref[...])
        for target in rest[:2]:
            first = target.shape[0] - extra
            target[first : first + VECTOR_ROWS] = high
            target[first + VECTOR_ROWS : first + extra] = low
    elif has_vectors and stage == STEP:
        rest[5][...] = rest[2][...] + vectors_in(rest[0]) + vectors_in(rest[1])
        for arrived, target in zip(rest[:2], rest[3:5]):
            target[target.shape[0] - extra :] = arrived[arrived.shape[0] - extra :]
        rest = (rest[0], rest[1], rest[3], rest[4])
    elif has_vectors:
        sums = rest[2][...] + vectors_in(rest[0])
        rest = rest[:2] + rest[3:]
        for target, (row, column) in zip(rest[2 + len(shapes) :], vector_places(rest[2 + len(shapes) :])):
            target[...] = sums[row : row + 1, column : column + target.shape[1]]

    for i, (row, column, _, width) in enumerate(places):
        columns = slice(column, column + width)
        if stage == FIRST:
            value = term(i, 0).astype(BF16)
            if row < half:
                rest[0][row : min(row + rows, half), columns] = value[: half - row]
            if row + rows > half:
                first = max(row, half)
                rest[1][first - half : row + rows - half, columns] = value[first - row :]
        elif stage == STEP:
            whole = rest[0].shape[0] == total + extra
            for direction, (low, high) in enumerate(((0, half), (half, total))):
                if whole:
                    low, high = 0, total
                value, arrived, target = term(i, direction), rest[direction], rest[2 + direction]
                first, last = max(row, low), min(row + rows, high)
                if first < last:
                    added = value[first - row : last - row] + arrived[first - low : last - low, columns].astype(F32)
                    target[first:last, columns] = added.astype(BF16)
                for begin, end in ((row, min(low, row + rows)), (max(high, row), row + rows)):
                    if begin < end:
                        target[begin:end, columns] = value[begin - row : end - row].astype(BF16)
        else:
            value = term(i, 0) + rest[0][row : row + rows, columns].astype(F32)
            value = value + rest[1][row : row + rows, columns].astype(F32)
            for target, (source, start, stop, turned) in zip(rest[2 : 2 + len(shapes)], shapes):
                if source == i:
                    target[...] = value[:, start:stop].T if turned else value[:, start:stop]


def vector_places(arrays):
    places, row, column, full = [], 0, 0, arrays[0].shape[1]
    for array in arrays:
        if column + array.shape[1] > full:
            row, column = row + 1, 0
        places.append((row, column))
        column += array.shape[1]
    return places


def ring_sum(layout, owners, arrived, stage, shapes, vectors):
    size = lax.axis_size("dp")
    places, lefts, rights, row = [], [], [], 0
    for terms in layout:
        column = 0
        for left, right in terms:
            rows = left.shape[1] // size
            places.append((row, column, rows, right.shape[1]))
            lefts.append(left)
            rights.append(right)
            column += right.shape[1]
        row += rows
    extra = 2 * VECTOR_ROWS if vectors else 0
    operands = [*lefts, *rights, *arrived]
    out_shape = []
    if stage == LAST:
        for term, start, stop, turned in shapes:
            shape = (places[term][2], stop - start)
            out_shape.append(jax.ShapeDtypeStruct(shape[::-1] if turned else shape, F32))
        if vectors:
            out_shape += [jax.ShapeDtypeStruct((1, column), F32)] * vectors[0].shape[0]
            out_shape += [jax.ShapeDtypeStruct(single.shape, F32) for single in vectors[2:]]
    else:
        travels = (row // 2 if stage == FIRST else row) + extra
        out_shape = [jax.ShapeDtypeStruct((travels, column), BF16)] * 2
        if vectors:
            out_shape.append(jax.ShapeDtypeStruct((VECTOR_ROWS, column), F32))
        if stage == FIRST:
            operands += vectors
    vmem = pl.BlockSpec(memory_space=pltpu.VMEM)
    return pl.pallas_call(
        functools.partial(ring_sum_kernel, places, stage, shapes, bool(vectors)),
        in_specs=[pl.BlockSpec(memory_space=pltpu.SMEM)] + [vmem] * len(operands),
        out_specs=[vmem] * len(out_shape),
        out_shape=out_shape,
        cost_estimate=pl.CostEstimate(
            flops=4 * row * column * lefts[0].shape[0],
            bytes_accessed=12 * row * column,
            transcendentals=0,
        ),
        compiler_params=pltpu.CompilerParams(vmem_limit_bytes=KERNEL_VMEM),
        name="ring_sum",
    )(jnp.stack(owners), *operands)


def row_major(array):
    return with_layout_constraint(array, Layout(major_to_minor=(0, 1)))


LANES = 128
QUERY_TILE = 256


def head_lanes(shape, head):
    lane = lax.broadcasted_iota(jnp.int32, shape, 1)
    return (lane >= head * HD) & (lane < (head + 1) * HD)


def keep_head(block, head):
    return jnp.where(head_lanes(block.shape, head), block, jnp.zeros_like(block))


def scores_of(key_block, query_block, counts_ref, score_scale):
    scores = matmul_nt(key_block, query_block) * score_scale
    rows = scores.shape[0] // counts_ref.shape[0]
    valid = [
        lax.broadcasted_iota(jnp.int32, (rows, scores.shape[1]), 0) < counts_ref[r]
        for r in range(counts_ref.shape[0])
    ]
    return jnp.where(jnp.concatenate(valid, axis=0), scores, MASKED)


def attention_kernel(score_scale, counts_ref, query_ref, key_ref, value_ref, context_ref, log_total_ref):
    keys, values = key_ref[...], value_ref[...]
    pieces = []
    for head in range(LANES // HD):
        scores = scores_of(keys, keep_head(query_ref[...], head), counts_ref, score_scale)
        row_peak = jnp.max(scores, axis=0, keepdims=True)
        raised = jnp.exp(scores - row_peak)
        total = jnp.sum(raised, axis=0, keepdims=True)
        log_total_ref[0, head : head + 1, :] = row_peak + jnp.log(total)
        probs_low = (raised * (1.0 / total)).astype(BF16)
        both = matmul_tn(values, probs_low)
        pieces.append(both[head * HD : (head + 1) * HD])
    context_ref[...] = jnp.concatenate(pieces, axis=0).T.astype(BF16)


def attention(qkv_low, counts, local_width, score_scale):
    seq_len = qkv_low.shape[0]
    pairs = local_width // LANES
    tiles = seq_len // QUERY_TILE
    return pl.pallas_call(
        functools.partial(attention_kernel, score_scale),
        grid=(pairs, tiles),
        in_specs=[
            pl.BlockSpec(memory_space=pltpu.SMEM),
            pl.BlockSpec((QUERY_TILE, LANES), lambda j, i: (i, j)),
            pl.BlockSpec((seq_len, LANES), lambda j, i: (0, pairs + j)),
            pl.BlockSpec((seq_len, LANES), lambda j, i: (0, 2 * pairs + j)),
        ],
        out_specs=[
            pl.BlockSpec((QUERY_TILE, LANES), lambda j, i: (i, j)),
            pl.BlockSpec((1, LANES // HD, QUERY_TILE), lambda j, i: (j, 0, i)),
        ],
        out_shape=[
            jax.ShapeDtypeStruct((seq_len, local_width), BF16),
            jax.ShapeDtypeStruct((pairs, LANES // HD, seq_len), F32),
        ],
        cost_estimate=pl.CostEstimate(
            flops=4 * seq_len * seq_len * local_width,
            bytes_accessed=8 * seq_len * local_width,
            transcendentals=seq_len * seq_len * local_width // HD,
        ),
        compiler_params=pltpu.CompilerParams(vmem_limit_bytes=KERNEL_VMEM),
        name="attention",
    )(counts, qkv_low, qkv_low, qkv_low)


def attention_grad_kernel(
    score_scale,
    counts_ref,
    query_ref,
    key_ref,
    value_ref,
    upstream_ref,
    log_total_ref,
    low_ref,
    query_sum_ref,
    value_sum_ref,
    key_total,
    value_total,
):
    pair, step = pl.program_id(0), pl.program_id(1)
    width = low_ref.shape[1] // 3

    @pl.when(step == 0)
    def _():
        key_total[...] = jnp.zeros_like(key_total)
        value_total[...] = jnp.zeros_like(value_total)
        query_sum_ref[...] = jnp.zeros_like(query_sum_ref)

    keys, values = key_ref[...], value_ref[...]
    pieces = []
    for head in range(LANES // HD):
        queries = keep_head(query_ref[...], head)
        upstream = keep_head(upstream_ref[...], head)
        scores = scores_of(keys, queries, counts_ref, score_scale)
        probs = jnp.exp(scores - log_total_ref[0, head : head + 1, :])
        prob_grad = matmul_nt(values, upstream)
        row_inner = jnp.sum(probs * prob_grad, axis=0, keepdims=True)
        score_grad = (probs * (prob_grad - row_inner) * score_scale).astype(BF16)
        value_total[...] += matmul(probs.astype(BF16), upstream)
        key_total[...] += matmul(score_grad, queries)
        both = matmul_tn(keys, score_grad)
        pieces.append(both[head * HD : (head + 1) * HD])
    query_grad = jnp.concatenate(pieces, axis=0).T
    rows = pl.ds(pl.multiple_of(step * QUERY_TILE, QUERY_TILE), QUERY_TILE)
    start = pl.multiple_of(pair * LANES, LANES)
    low_ref[rows, pl.ds(start, LANES)] = query_grad.astype(BF16)
    query_sum_ref[...] += jnp.sum(query_grad, axis=0, keepdims=True)

    @pl.when(step == pl.num_programs(1) - 1)
    def _():
        low_ref[:, pl.ds(start + width, LANES)] = key_total[...].astype(BF16)
        low_ref[:, pl.ds(start + 2 * width, LANES)] = value_total[...].astype(BF16)
        value_sum_ref[...] = jnp.sum(value_total[...], axis=0, keepdims=True)


def attention_grad(qkv_low, upstream, log_total, counts, local_width, score_scale):
    seq_len = qkv_low.shape[0]
    pairs = local_width // LANES
    tiles = seq_len // QUERY_TILE
    tile_spec = pl.BlockSpec((QUERY_TILE, LANES), lambda j, i: (i, j))
    sum_spec = pl.BlockSpec((1, LANES), lambda j, i: (0, j))
    sums = jax.ShapeDtypeStruct((1, local_width), F32)
    return pl.pallas_call(
        functools.partial(attention_grad_kernel, score_scale),
        grid=(pairs, tiles),
        in_specs=[
            pl.BlockSpec(memory_space=pltpu.SMEM),
            tile_spec,
            pl.BlockSpec((seq_len, LANES), lambda j, i: (0, pairs + j)),
            pl.BlockSpec((seq_len, LANES), lambda j, i: (0, 2 * pairs + j)),
            tile_spec,
            pl.BlockSpec((1, LANES // HD, QUERY_TILE), lambda j, i: (j, 0, i)),
        ],
        out_specs=[pl.BlockSpec((seq_len, 3 * local_width), lambda j, i: (0, 0)), sum_spec, sum_spec],
        out_shape=[jax.ShapeDtypeStruct((seq_len, 3 * local_width), BF16), sums, sums],
        scratch_shapes=[pltpu.VMEM((seq_len, LANES), F32), pltpu.VMEM((seq_len, LANES), F32)],
        cost_estimate=pl.CostEstimate(
            flops=10 * seq_len * seq_len * local_width,
            bytes_accessed=16 * seq_len * local_width,
            transcendentals=seq_len * seq_len * local_width // HD,
        ),
        compiler_params=pltpu.CompilerParams(vmem_limit_bytes=KERNEL_VMEM),
        name="attention_grad",
    )(counts, qkv_low, qkv_low, qkv_low, upstream, log_total)


def layer(
    hidden_in,
    cotangent,
    lengths,
    query_weight,
    key_weight,
    value_weight,
    output_weight,
    up_weight,
    down_weight,
    query_bias,
    value_bias,
    output_bias,
    up_bias,
    down_bias,
    first_gain,
    first_shift,
    second_gain,
    second_shift,
):
    n_tensor = lax.axis_size("tensor")
    tensor_index = lax.axis_index("tensor")
    local_rows = hidden_in.shape[0]
    local_width = query_weight.shape[1]
    score_scale = HD ** (-0.5)
    ring = Ring()
    blocks = jnp.arange(n_tensor, dtype=jnp.int32) ^ tensor_index
    counts = lengths[0] - blocks * local_rows

    packed = row_major(jnp.concatenate([query_weight, key_weight, value_weight, output_weight.T], axis=1))
    (packed_full,) = ring.gather(packed, (packed.shape[0],))
    hidden_full = gather_rows(hidden_in)
    stacked = row_major(jnp.concatenate([up_weight, down_weight.T], axis=0))
    up_full, down_turned = ring.gather(stacked, (up_weight.shape[0], down_weight.shape[1]))
    qkv_full = packed_full[:, : 3 * local_width]
    output_turned = packed_full[:, 3 * local_width :]

    qkv_bias = jnp.concatenate([query_bias, jnp.zeros_like(query_bias), value_bias])
    qkv_low = (matmul(hidden_full, qkv_full) + qkv_bias).astype(BF16)
    context, log_total = attention(qkv_low, counts, local_width, score_scale)
    attn_rows = scatter_rows(matmul_nt(context, output_turned).astype(BF16))
    first_sum = hidden_in.astype(F32) + attn_rows + output_bias
    first_out, first_normed, first_inverse = norm_forward(first_sum, first_gain, first_shift)
    normed_full = gather_rows(first_out.astype(BF16))
    pre_act = matmul(normed_full, up_full) + up_bias
    activated, slope = lax.optimization_barrier((gelu_value(pre_act).astype(BF16), gelu_slope(pre_act)))
    mlp_rows = scatter_rows(matmul_nt(activated, down_turned).astype(BF16))
    second_sum = first_out + mlp_rows + down_bias
    second_out, second_normed, second_inverse = norm_forward(second_sum, second_gain, second_shift)
    hidden_out = second_out.astype(BF16)

    upstream = cotangent.astype(F32)
    grad_second_gain = jnp.sum(upstream * second_normed, axis=0)
    grad_second_shift = jnp.sum(upstream, axis=0)
    second_grad = norm_backward(upstream, second_gain, second_normed, second_inverse)
    grad_down_bias = jnp.sum(second_grad, axis=0)
    second_full = gather_rows(second_grad.astype(BF16))
    pre_grad = matmul(second_full, down_turned) * slope
    grad_up_bias, pre_low = lax.optimization_barrier((jnp.sum(pre_grad, axis=0), pre_grad.astype(BF16)))
    partial = matmul_nt(pre_low, up_full).astype(BF16)
    up_owned, down_owned = ring.scatter(
        [[(normed_full, pre_low)], [(second_full, activated)]],
        ((0, 0, up_weight.shape[1], False), (1, 0, down_weight.shape[0], True)),
    )
    first_grad_in = second_grad + scatter_rows(partial)
    grad_first_gain = jnp.sum(first_grad_in * first_normed, axis=0)
    grad_first_shift = jnp.sum(first_grad_in, axis=0)
    first_grad = norm_backward(first_grad_in, first_gain, first_normed, first_inverse)
    grad_output_bias = jnp.sum(first_grad, axis=0)
    attn_grad_full = lax.optimization_barrier(gather_rows(first_grad.astype(BF16)))
    context_grad = matmul(attn_grad_full, output_turned).astype(BF16)

    everywhere = jnp.stack(
        [grad_second_gain, grad_second_shift, grad_down_bias, grad_first_gain, grad_first_shift, grad_output_bias]
    )
    everywhere = everywhere + swap(everywhere, "tensor", 1)
    everywhere_far = swap(everywhere, "tensor", 2)

    low, query_sum, value_sum = attention_grad(
        qkv_low, context_grad, log_total, counts, local_width, score_scale
    )
    query_owned, key_owned, value_owned, output_owned, *sums = ring.scatter(
        [[(hidden_full, low), (attn_grad_full, context)]],
        tuple((0, i * local_width, (i + 1) * local_width, False) for i in range(3)) + ((1, 0, local_width, True),),
        (everywhere, everywhere_far, grad_up_bias.reshape(1, -1), query_sum, value_sum),
    )
    sums = [vector.reshape(-1) for vector in sums]
    back = matmul_nt(low, qkv_full).astype(BF16)
    back = scatter_rows(back)
    grad_in = (first_grad + back).astype(BF16)
    return (
        hidden_out,
        grad_in,
        query_owned,
        key_owned,
        value_owned,
        output_owned,
        up_owned,
        down_owned,
        sums[7],
        sums[8],
        sums[5],
        sums[6],
        sums[2],
        sums[3],
        sums[4],
        sums[0],
        sums[1],
    )


def solution(mesh):
    in_specs = (
        P(("dp", "tensor"), None),
        P(("dp", "tensor"), None),
        P("dp"),
        P("dp", "tensor"),
        P("dp", "tensor"),
        P("dp", "tensor"),
        P("tensor", "dp"),
        P("dp", "tensor"),
        P("tensor", "dp"),
        P("tensor"),
        P("tensor"),
        P(),
        P("tensor"),
        P(),
        P(),
        P(),
        P(),
        P(),
    )
    out_specs = (
        P(("dp", "tensor"), None),
        P(("dp", "tensor"), None),
        P("dp", "tensor"),
        P("dp", "tensor"),
        P("dp", "tensor"),
        P("tensor", "dp"),
        P("dp", "tensor"),
        P("tensor", "dp"),
        P("tensor"),
        P("tensor"),
        P(),
        P("tensor"),
        P(),
        P(),
        P(),
        P(),
        P(),
    )
    return jax.shard_map(layer, mesh=mesh, in_specs=in_specs, out_specs=out_specs, check_vma=False)
```

```python
import functools

import jax
import jax.numpy as jnp
from jax import lax
from jax.experimental import pallas as pl
from jax.experimental.layout import Layout, with_layout_constraint
from jax.experimental.pallas import tpu as pltpu
from jax.sharding import PartitionSpec as P


HD = 64


EPSILON = 1e-12
ROOT_HALF = 0.7071067811865476
INV_ROOT_TWO_PI = 0.3989422804014327
MASKED = -1e30
BF16 = jnp.bfloat16
F32 = jnp.float32
KERNEL_VMEM = 16 << 20


def matmul(left_side, right_side):
    return jnp.dot(left_side, right_side, preferred_element_type=F32)


def matmul_nt(left_side, right_side):
    return lax.dot_general(left_side, right_side, (((1,), (1,)), ((), ())), preferred_element_type=F32)


def matmul_tn(left_side, right_side):
    return lax.dot_general(left_side, right_side, (((0,), (0,)), ((), ())), preferred_element_type=F32)


def gelu_value(pre_act):
    return pre_act * 0.5 * (1.0 + lax.erf(pre_act * ROOT_HALF))


def gelu_slope(pre_act):
    cumulative = 0.5 * (1.0 + lax.erf(pre_act * ROOT_HALF))
    density = jnp.exp(-0.5 * pre_act * pre_act) * INV_ROOT_TWO_PI
    return cumulative + pre_act * density


def norm_forward(summed, gain_vector, shift_vector):
    centre = summed - jnp.mean(summed, axis=-1, keepdims=True)
    spread = jnp.mean(centre * centre, axis=-1, keepdims=True)
    inverse = lax.rsqrt(spread + EPSILON)
    normed = centre * inverse
    return (normed * gain_vector + shift_vector, normed, inverse)


def norm_backward(upstream, gain_vector, normed, inverse):
    scaled = upstream * gain_vector
    return inverse * (
        scaled
        - jnp.mean(scaled, axis=-1, keepdims=True)
        - normed * jnp.mean(scaled * normed, axis=-1, keepdims=True)
    )


def swap(array, axis, bit):
    size = lax.axis_size(axis)
    return lax.ppermute(array, axis, [(i, i ^ bit) for i in range(size)])


def gather_rows(block):
    far = swap(block, "tensor", 2)
    other_core = swap(block, "tensor", 1)
    far_core = swap(far, "tensor", 1)
    return jnp.concatenate([block, other_core, far, far_core], axis=0)


def scatter_rows(partial):
    rows = partial.shape[0] // 4
    own, other_core, far, far_core = (partial[i * rows : (i + 1) * rows] for i in range(4))
    far_sum = (far.astype(F32) + swap(far_core, "tensor", 1).astype(F32)).astype(BF16)
    from_far = swap(far_sum, "tensor", 2)
    from_core = swap(other_core, "tensor", 1)
    return own.astype(F32) + from_core.astype(F32) + from_far.astype(F32)


class Ring:
    def __init__(self):
        self.size = lax.axis_size("dp")
        half = self.size // 2
        order = [2 * i for i in range(half)] + [2 * (self.size - 1 - i) + 1 for i in range(half, self.size)]
        self.up = [(order[i], order[(i + 1) % self.size]) for i in range(self.size)]
        self.down = [(b, a) for a, b in self.up]
        index = lax.axis_index("dp")
        row, column = index // 2, index % 2
        self.place = jnp.where(column == 0, row, self.size - 1 - row)
        self.small = self.size <= 16 and self.size % 2 == 0

    def owner(self, distance):
        place = (self.place + distance + 2 * self.size) % self.size
        return jnp.where(place < self.size // 2, 2 * place, 2 * (self.size - 1 - place) + 1)

    def step(self, going_up, going_down):
        going_up = lax.ppermute(going_up, "dp", self.up)
        going_down = lax.ppermute(going_down, "dp", self.down)
        return going_up, going_down

    def gather(self, block, splits):
        if not self.small:
            whole = lax.all_gather(block.reshape(1, *block.shape), "dp", axis=0, tiled=True)
            parts, start = [], 0
            for rows in splits:
                part = whole[:, start : start + rows]
                parts.append(part.reshape(self.size * rows, block.shape[1]))
                start += rows
            return parts
        total = block.shape[0]
        wholes = [jnp.zeros((self.size * rows, block.shape[1]), block.dtype) for rows in splits]

        def put(part, first, distance):
            start = 0
            for i, rows in enumerate(splits):
                low, high = max(start, first), min(start + rows, first + part.shape[0])
                if low < high:
                    wholes[i] = lax.dynamic_update_slice_in_dim(
                        wholes[i],
                        part[low - first : high - first],
                        self.owner(distance) * rows + (low - start),
                        0,
                    )
                start += rows

        put(block, 0, 0)
        going_up = going_down = block
        middle = self.size // 2
        for step in range(1, middle):
            going_up, going_down = self.step(going_up, going_down)
            put(going_up, 0, -step)
            put(going_down, 0, step)
        cut = total // 2
        first, second = self.step(going_up[:cut], going_down[cut:])
        put(first, 0, middle)
        put(second, cut, middle)
        return wholes

    def scatter(self, layout, shapes, vectors=()):
        if not self.small:
            owned = []
            for row in layout:
                for left, right in row:
                    whole = matmul_tn(left, right).astype(BF16)
                    owned.append(lax.psum_scatter(whole, "dp", scatter_dimension=0, tiled=True).astype(F32))
            outs = []
            for term, start, stop, turned in shapes:
                piece = owned[term][:, start:stop]
                outs.append(piece.T if turned else piece)
            if vectors:
                partial, other, *singles = vectors
                rows = [(partial + other)[i : i + 1] for i in range(partial.shape[0])] + singles
                outs.extend(lax.psum(rows, "dp"))
            return outs
        middle = self.size // 2
        arrived = list(ring_sum(layout, [self.owner(middle)] * 2, (), FIRST, (), vectors))
        for step in range(1, middle + 1):
            arrived[:2] = self.step(arrived[0], arrived[1])
            distance = middle - step
            stage = STEP if distance else LAST
            arrived = list(
                ring_sum(layout, [self.owner(distance), self.owner(-distance)], arrived, stage, shapes, vectors)
            )
        return arrived


FIRST, STEP, LAST = range(3)
VECTOR_ROWS = 8


def split_low(value):
    high = value.astype(BF16)
    return high, (value - high.astype(F32)).astype(BF16)


def ring_sum_kernel(places, stage, shapes, has_vectors, owners_ref, *refs):
    count = len(places)
    lefts, rights, rest = refs[:count], refs[count : 2 * count], refs[2 * count :]
    rows = places[0][2]
    total = max(place[0] for place in places) + rows
    half = total // 2
    extra = 2 * VECTOR_ROWS if has_vectors else 0

    def term(i, direction):
        start = pl.multiple_of(owners_ref[direction] * rows, rows)
        return matmul_tn(lefts[i][:, pl.ds(start, rows)], rights[i][...])

    def vectors_in(ref):
        first = ref.shape[0] - extra
        high = ref[first : first + VECTOR_ROWS].astype(F32)
        return high + ref[first + VECTOR_ROWS : first + extra].astype(F32)

    if has_vectors and stage == FIRST:
        partial_ref, other_ref, *single_refs = rest[:5]
        rest = rest[5:]
        sum_ref = rest[2]
        row, column = partial_ref.shape[0], 0
        sum_ref[...] = jnp.zeros_like(sum_ref)
        sum_ref[:row] = partial_ref[...] + other_ref[...]
        for ref in single_refs:
            width = ref.shape[1]
            if column + width > sum_ref.shape[1]:
                row, column = row + 1, 0
            sum_ref[row : row + 1, column : column + width] = ref[...]
            column += width
        high, low = split_low(sum_ref[...])
        for target in rest[:2]:
            first = target.shape[0] - extra
            target[first : first + VECTOR_ROWS] = high
            target[first + VECTOR_ROWS : first + extra] = low
    elif has_vectors and stage == STEP:
        rest[5][...] = rest[2][...] + vectors_in(rest[0]) + vectors_in(rest[1])
        for arrived, target in zip(rest[:2], rest[3:5]):
            target[target.shape[0] - extra :] = arrived[arrived.shape[0] - extra :]
        rest = (rest[0], rest[1], rest[3], rest[4])
    elif has_vectors:
        sums = rest[2][...] + vectors_in(rest[0])
        rest = rest[:2] + rest[3:]
        for target, (row, column) in zip(rest[2 + len(shapes) :], vector_places(rest[2 + len(shapes) :])):
            target[...] = sums[row : row + 1, column : column + target.shape[1]]

    for i, (row, column, _, width) in enumerate(places):
        columns = slice(column, column + width)
        if stage == FIRST:
            value = term(i, 0).astype(BF16)
            if row < half:
                rest[0][row : min(row + rows, half), columns] = value[: half - row]
            if row + rows > half:
                first = max(row, half)
                rest[1][first - half : row + rows - half, columns] = value[first - row :]
        elif stage == STEP:
            whole = rest[0].shape[0] == total + extra
            for direction, (low, high) in enumerate(((0, half), (half, total))):
                if whole:
                    low, high = 0, total
                value, arrived, target = term(i, direction), rest[direction], rest[2 + direction]
                first, last = max(row, low), min(row + rows, high)
                if first < last:
                    added = value[first - row : last - row] + arrived[first - low : last - low, columns].astype(F32)
                    target[first:last, columns] = added.astype(BF16)
                for begin, end in ((row, min(low, row + rows)), (max(high, row), row + rows)):
                    if begin < end:
                        target[begin:end, columns] = value[begin - row : end - row].astype(BF16)
        else:
            value = term(i, 0) + rest[0][row : row + rows, columns].astype(F32)
            value = value + rest[1][row : row + rows, columns].astype(F32)
            for target, (source, start, stop, turned) in zip(rest[2 : 2 + len(shapes)], shapes):
                if source == i:
                    target[...] = value[:, start:stop].T if turned else value[:, start:stop]


def vector_places(arrays):
    places, row, column, full = [], 0, 0, arrays[0].shape[1]
    for array in arrays:
        if column + array.shape[1] > full:
            row, column = row + 1, 0
        places.append((row, column))
        column += array.shape[1]
    return places


def ring_sum(layout, owners, arrived, stage, shapes, vectors):
    size = lax.axis_size("dp")
    places, lefts, rights, row = [], [], [], 0
    for terms in layout:
        column = 0
        for left, right in terms:
            rows = left.shape[1] // size
            places.append((row, column, rows, right.shape[1]))
            lefts.append(left)
            rights.append(right)
            column += right.shape[1]
        row += rows
    extra = 2 * VECTOR_ROWS if vectors else 0
    operands = [*lefts, *rights, *arrived]
    out_shape = []
    if stage == LAST:
        for term, start, stop, turned in shapes:
            shape = (places[term][2], stop - start)
            out_shape.append(jax.ShapeDtypeStruct(shape[::-1] if turned else shape, F32))
        if vectors:
            out_shape += [jax.ShapeDtypeStruct((1, column), F32)] * vectors[0].shape[0]
            out_shape += [jax.ShapeDtypeStruct(single.shape, F32) for single in vectors[2:]]
    else:
        travels = (row // 2 if stage == FIRST else row) + extra
        out_shape = [jax.ShapeDtypeStruct((travels, column), BF16)] * 2
        if vectors:
            out_shape.append(jax.ShapeDtypeStruct((VECTOR_ROWS, column), F32))
        if stage == FIRST:
            operands += vectors
    vmem = pl.BlockSpec(memory_space=pltpu.VMEM)
    return pl.pallas_call(
        functools.partial(ring_sum_kernel, places, stage, shapes, bool(vectors)),
        in_specs=[pl.BlockSpec(memory_space=pltpu.SMEM)] + [vmem] * len(operands),
        out_specs=[vmem] * len(out_shape),
        out_shape=out_shape,
        cost_estimate=pl.CostEstimate(
            flops=4 * row * column * lefts[0].shape[0],
            bytes_accessed=12 * row * column,
            transcendentals=0,
        ),
        compiler_params=pltpu.CompilerParams(vmem_limit_bytes=KERNEL_VMEM),
        name="ring_sum",
    )(jnp.stack(owners), *operands)


def row_major(array):
    return with_layout_constraint(array, Layout(major_to_minor=(0, 1)))


LANES = 128
QUERY_TILE = 256


def keep_head(block, head, other=None):
    lane = lax.broadcasted_iota(jnp.int32, block.shape, 1)
    kept = (lane >= head * HD) & (lane < (head + 1) * HD)
    rest = jnp.zeros_like(block)
    if other is not None:
        spare = HD * (1 - head)
        rest = jnp.where(lane == spare, other, rest)
    return jnp.where(kept, block, rest)


def key_offsets(shape, counts_ref):
    rows = shape[0] // counts_ref.shape[0]
    row = lax.broadcasted_iota(jnp.int32, (rows, shape[1]), 0)
    parts = [jnp.where(row < counts_ref[r], 0.0, MASKED) for r in range(counts_ref.shape[0])]
    return jnp.concatenate(parts, axis=0).astype(BF16)


def scores_of(keys, offsets, scaled_queries, head):
    with_offsets = keep_head(keys, head, offsets)
    with_ones = keep_head(scaled_queries, head, jnp.ones_like(scaled_queries))
    return matmul_nt(with_offsets, with_ones)


def attention_kernel(score_scale, counts_ref, query_ref, key_ref, value_ref, context_ref, log_total_ref):
    keys, values = key_ref[...], value_ref[...]
    offsets = key_offsets(keys.shape, counts_ref)
    queries = query_ref[...] * jnp.asarray(score_scale, BF16)
    pieces = []
    for head in range(LANES // HD):
        scores = scores_of(keys, offsets, queries, head)
        row_peak = jnp.max(scores, axis=0, keepdims=True)
        raised = jnp.exp(scores - row_peak)
        total = jnp.sum(raised, axis=0, keepdims=True)
        log_total_ref[0, head : head + 1, :] = row_peak + jnp.log(total)
        both = matmul_tn(values, raised.astype(BF16))
        pieces.append(both[head * HD : (head + 1) * HD] * (1.0 / total))
    context_ref[...] = jnp.concatenate(pieces, axis=0).T.astype(BF16)


def attention(qkv_low, counts, local_width, score_scale):
    seq_len = qkv_low.shape[0]
    pairs = local_width // LANES
    tiles = seq_len // QUERY_TILE
    return pl.pallas_call(
        functools.partial(attention_kernel, score_scale),
        grid=(pairs, tiles),
        in_specs=[
            pl.BlockSpec(memory_space=pltpu.SMEM),
            pl.BlockSpec((QUERY_TILE, LANES), lambda j, i: (i, j)),
            pl.BlockSpec((seq_len, LANES), lambda j, i: (0, pairs + j)),
            pl.BlockSpec((seq_len, LANES), lambda j, i: (0, 2 * pairs + j)),
        ],
        out_specs=[
            pl.BlockSpec((QUERY_TILE, LANES), lambda j, i: (i, j)),
            pl.BlockSpec((1, LANES // HD, QUERY_TILE), lambda j, i: (j, 0, i)),
        ],
        out_shape=[
            jax.ShapeDtypeStruct((seq_len, local_width), BF16),
            jax.ShapeDtypeStruct((pairs, LANES // HD, seq_len), F32),
        ],
        cost_estimate=pl.CostEstimate(
            flops=4 * seq_len * seq_len * local_width,
            bytes_accessed=8 * seq_len * local_width,
            transcendentals=seq_len * seq_len * local_width // HD,
        ),
        compiler_params=pltpu.CompilerParams(vmem_limit_bytes=KERNEL_VMEM),
        name="attention",
    )(counts, qkv_low, qkv_low, qkv_low)


def attention_grad_kernel(
    score_scale,
    counts_ref,
    query_ref,
    key_ref,
    value_ref,
    upstream_ref,
    log_total_ref,
    low_ref,
    query_sum_ref,
    value_sum_ref,
    key_total,
    value_total,
):
    pair, step = pl.program_id(0), pl.program_id(1)
    width = low_ref.shape[1] // 3

    @pl.when(step == 0)
    def _():
        key_total[...] = jnp.zeros_like(key_total)
        value_total[...] = jnp.zeros_like(value_total)
        query_sum_ref[...] = jnp.zeros_like(query_sum_ref)

    keys, values = key_ref[...], value_ref[...]
    offsets = key_offsets(keys.shape, counts_ref)
    scale = jnp.asarray(score_scale, BF16)
    queries, scaled_keys = query_ref[...] * scale, keys * scale
    pieces = []
    for head in range(LANES // HD):
        upstream = keep_head(upstream_ref[...], head)
        scores = scores_of(keys, offsets, queries, head)
        probs = jnp.exp(scores - log_total_ref[0, head : head + 1, :])
        prob_grad = matmul_nt(values, upstream)
        row_inner = jnp.sum(probs * prob_grad, axis=0, keepdims=True)
        score_grad = (probs * (prob_grad - row_inner)).astype(BF16)
        value_total[...] += matmul(probs.astype(BF16), upstream)
        key_total[...] += matmul(score_grad, keep_head(queries, head))
        both = matmul_tn(scaled_keys, score_grad)
        pieces.append(both[head * HD : (head + 1) * HD])
    query_grad = jnp.concatenate(pieces, axis=0).T
    rows = pl.ds(pl.multiple_of(step * QUERY_TILE, QUERY_TILE), QUERY_TILE)
    start = pl.multiple_of(pair * LANES, LANES)
    low_ref[rows, pl.ds(start, LANES)] = query_grad.astype(BF16)
    query_sum_ref[...] += jnp.sum(query_grad, axis=0, keepdims=True)

    @pl.when(step == pl.num_programs(1) - 1)
    def _():
        low_ref[:, pl.ds(start + width, LANES)] = key_total[...].astype(BF16)
        low_ref[:, pl.ds(start + 2 * width, LANES)] = value_total[...].astype(BF16)
        value_sum_ref[...] = jnp.sum(value_total[...], axis=0, keepdims=True)


def attention_grad(qkv_low, upstream, log_total, counts, local_width, score_scale):
    seq_len = qkv_low.shape[0]
    pairs = local_width // LANES
    tiles = seq_len // QUERY_TILE
    tile_spec = pl.BlockSpec((QUERY_TILE, LANES), lambda j, i: (i, j))
    sum_spec = pl.BlockSpec((1, LANES), lambda j, i: (0, j))
    sums = jax.ShapeDtypeStruct((1, local_width), F32)
    return pl.pallas_call(
        functools.partial(attention_grad_kernel, score_scale),
        grid=(pairs, tiles),
        in_specs=[
            pl.BlockSpec(memory_space=pltpu.SMEM),
            tile_spec,
            pl.BlockSpec((seq_len, LANES), lambda j, i: (0, pairs + j)),
            pl.BlockSpec((seq_len, LANES), lambda j, i: (0, 2 * pairs + j)),
            tile_spec,
            pl.BlockSpec((1, LANES // HD, QUERY_TILE), lambda j, i: (j, 0, i)),
        ],
        out_specs=[pl.BlockSpec((seq_len, 3 * local_width), lambda j, i: (0, 0)), sum_spec, sum_spec],
        out_shape=[jax.ShapeDtypeStruct((seq_len, 3 * local_width), BF16), sums, sums],
        scratch_shapes=[pltpu.VMEM((seq_len, LANES), F32), pltpu.VMEM((seq_len, LANES), F32)],
        cost_estimate=pl.CostEstimate(
            flops=10 * seq_len * seq_len * local_width,
            bytes_accessed=16 * seq_len * local_width,
            transcendentals=seq_len * seq_len * local_width // HD,
        ),
        compiler_params=pltpu.CompilerParams(vmem_limit_bytes=KERNEL_VMEM),
        name="attention_grad",
    )(counts, qkv_low, qkv_low, qkv_low, upstream, log_total)


def layer(
    hidden_in,
    cotangent,
    lengths,
    query_weight,
    key_weight,
    value_weight,
    output_weight,
    up_weight,
    down_weight,
    query_bias,
    value_bias,
    output_bias,
    up_bias,
    down_bias,
    first_gain,
    first_shift,
    second_gain,
    second_shift,
):
    n_tensor = lax.axis_size("tensor")
    tensor_index = lax.axis_index("tensor")
    local_rows = hidden_in.shape[0]
    local_width = query_weight.shape[1]
    score_scale = HD ** (-0.5)
    ring = Ring()
    blocks = jnp.arange(n_tensor, dtype=jnp.int32) ^ tensor_index
    counts = lengths[0] - blocks * local_rows

    packed = row_major(jnp.concatenate([query_weight, key_weight, value_weight, output_weight.T], axis=1))
    (packed_full,) = ring.gather(packed, (packed.shape[0],))
    hidden_full = gather_rows(hidden_in)
    (up_full,) = ring.gather(up_weight, (up_weight.shape[0],))
    (down_turned,) = ring.gather(row_major(down_weight.T), (down_weight.shape[1],))
    qkv_full = packed_full[:, : 3 * local_width]
    output_turned = packed_full[:, 3 * local_width :]

    qkv_bias = jnp.concatenate([query_bias, jnp.zeros_like(query_bias), value_bias])
    qkv_low = (matmul(hidden_full, qkv_full) + qkv_bias).astype(BF16)
    context, log_total = attention(qkv_low, counts, local_width, score_scale)
    attn_rows = scatter_rows(matmul_nt(context, output_turned).astype(BF16))
    first_sum = hidden_in.astype(F32) + attn_rows + output_bias
    first_out, first_normed, first_inverse = norm_forward(first_sum, first_gain, first_shift)
    normed_full = gather_rows(first_out.astype(BF16))
    pre_act = matmul(normed_full, up_full) + up_bias
    activated, slope = lax.optimization_barrier((gelu_value(pre_act).astype(BF16), gelu_slope(pre_act)))
    mlp_rows = scatter_rows(matmul_nt(activated, down_turned).astype(BF16))
    second_sum = first_out + mlp_rows + down_bias
    second_out, second_normed, second_inverse = norm_forward(second_sum, second_gain, second_shift)
    hidden_out = second_out.astype(BF16)

    upstream = cotangent.astype(F32)
    grad_second_gain = jnp.sum(upstream * second_normed, axis=0)
    grad_second_shift = jnp.sum(upstream, axis=0)
    second_grad = norm_backward(upstream, second_gain, second_normed, second_inverse)
    grad_down_bias = jnp.sum(second_grad, axis=0)
    second_full = gather_rows(second_grad.astype(BF16))
    pre_grad = matmul(second_full, down_turned) * slope
    grad_up_bias, pre_low = lax.optimization_barrier((jnp.sum(pre_grad, axis=0), pre_grad.astype(BF16)))
    partial = matmul_nt(pre_low, up_full).astype(BF16)
    up_owned, down_owned = ring.scatter(
        [[(normed_full, pre_low)], [(second_full, activated)]],
        ((0, 0, up_weight.shape[1], False), (1, 0, down_weight.shape[0], True)),
    )
    first_grad_in = second_grad + scatter_rows(partial)
    grad_first_gain = jnp.sum(first_grad_in * first_normed, axis=0)
    grad_first_shift = jnp.sum(first_grad_in, axis=0)
    first_grad = norm_backward(first_grad_in, first_gain, first_normed, first_inverse)
    grad_output_bias = jnp.sum(first_grad, axis=0)
    attn_grad_full = lax.optimization_barrier(gather_rows(first_grad.astype(BF16)))
    context_grad = matmul(attn_grad_full, output_turned).astype(BF16)

    everywhere = jnp.stack(
        [grad_second_gain, grad_second_shift, grad_down_bias, grad_first_gain, grad_first_shift, grad_output_bias]
    )
    everywhere = everywhere + swap(everywhere, "tensor", 1)
    everywhere_far = swap(everywhere, "tensor", 2)

    low, query_sum, value_sum = attention_grad(
        qkv_low, context_grad, log_total, counts, local_width, score_scale
    )
    query_owned, key_owned, value_owned, output_owned, *sums = ring.scatter(
        [[(hidden_full, low), (attn_grad_full, context)]],
        tuple((0, i * local_width, (i + 1) * local_width, False) for i in range(3)) + ((1, 0, local_width, True),),
        (everywhere, everywhere_far, grad_up_bias.reshape(1, -1), query_sum, value_sum),
    )
    sums = [vector.reshape(-1) for vector in sums]
    back = matmul_nt(low, qkv_full).astype(BF16)
    back = scatter_rows(back)
    grad_in = (first_grad + back).astype(BF16)
    return (
        hidden_out,
        grad_in,
        query_owned,
        key_owned,
        value_owned,
        output_owned,
        up_owned,
        down_owned,
        sums[7],
        sums[8],
        sums[5],
        sums[6],
        sums[2],
        sums[3],
        sums[4],
        sums[0],
        sums[1],
    )


def solution(mesh):
    in_specs = (
        P(("dp", "tensor"), None),
        P(("dp", "tensor"), None),
        P("dp"),
        P("dp", "tensor"),
        P("dp", "tensor"),
        P("dp", "tensor"),
        P("tensor", "dp"),
        P("dp", "tensor"),
        P("tensor", "dp"),
        P("tensor"),
        P("tensor"),
        P(),
        P("tensor"),
        P(),
        P(),
        P(),
        P(),
        P(),
    )
    out_specs = (
        P(("dp", "tensor"), None),
        P(("dp", "tensor"), None),
        P("dp", "tensor"),
        P("dp", "tensor"),
        P("dp", "tensor"),
        P("tensor", "dp"),
        P("dp", "tensor"),
        P("tensor", "dp"),
        P("tensor"),
        P("tensor"),
        P(),
        P("tensor"),
        P(),
        P(),
        P(),
        P(),
        P(),
    )
    return jax.shard_map(layer, mesh=mesh, in_specs=in_specs, out_specs=out_specs, check_vma=False)
```

```python
import functools

import jax
import jax.numpy as jnp
from jax import lax
from jax.experimental import pallas as pl
from jax.experimental.layout import Layout, with_layout_constraint
from jax.experimental.pallas import tpu as pltpu
from jax.sharding import PartitionSpec as P


HD = 64


EPSILON = 1e-12
ROOT_HALF = 0.7071067811865476
INV_ROOT_TWO_PI = 0.3989422804014327
MASKED = -1e30
BF16 = jnp.bfloat16
F32 = jnp.float32
KERNEL_VMEM = 16 << 20


def matmul(left_side, right_side):
    return jnp.dot(left_side, right_side, preferred_element_type=F32)


def matmul_nt(left_side, right_side):
    return lax.dot_general(left_side, right_side, (((1,), (1,)), ((), ())), preferred_element_type=F32)


def matmul_tn(left_side, right_side):
    return lax.dot_general(left_side, right_side, (((0,), (0,)), ((), ())), preferred_element_type=F32)


def gelu_value(pre_act):
    return pre_act * 0.5 * (1.0 + lax.erf(pre_act * ROOT_HALF))


def gelu_slope(pre_act):
    cumulative = 0.5 * (1.0 + lax.erf(pre_act * ROOT_HALF))
    density = jnp.exp(-0.5 * pre_act * pre_act) * INV_ROOT_TWO_PI
    return cumulative + pre_act * density


def norm_forward(summed, gain_vector, shift_vector):
    centre = summed - jnp.mean(summed, axis=-1, keepdims=True)
    spread = jnp.mean(centre * centre, axis=-1, keepdims=True)
    inverse = lax.rsqrt(spread + EPSILON)
    normed = centre * inverse
    return (normed * gain_vector + shift_vector, normed, inverse)


def norm_backward(upstream, gain_vector, normed, inverse):
    scaled = upstream * gain_vector
    return inverse * (
        scaled
        - jnp.mean(scaled, axis=-1, keepdims=True)
        - normed * jnp.mean(scaled * normed, axis=-1, keepdims=True)
    )


def swap(array, axis, bit):
    size = lax.axis_size(axis)
    return lax.ppermute(array, axis, [(i, i ^ bit) for i in range(size)])


def gather_rows(block):
    far = swap(block, "tensor", 2)
    other_core = swap(block, "tensor", 1)
    far_core = swap(far, "tensor", 1)
    rows = block.shape[0]
    whole = jnp.zeros((4 * rows, block.shape[1]), block.dtype)
    for i, part in enumerate((block, other_core, far, far_core)):
        whole = lax.dynamic_update_slice_in_dim(whole, part, i * rows, 0)
    return lax.optimization_barrier(whole)


def scatter_rows(partial):
    rows = partial.shape[0] // 4
    own, other_core, far, far_core = (partial[i * rows : (i + 1) * rows] for i in range(4))
    far_sum = (far.astype(F32) + swap(far_core, "tensor", 1).astype(F32)).astype(BF16)
    from_far = swap(far_sum, "tensor", 2)
    from_core = swap(other_core, "tensor", 1)
    return own.astype(F32) + from_core.astype(F32) + from_far.astype(F32)


class Ring:
    def __init__(self):
        self.size = lax.axis_size("dp")
        half = self.size // 2
        order = [2 * i for i in range(half)] + [2 * (self.size - 1 - i) + 1 for i in range(half, self.size)]
        self.up = [(order[i], order[(i + 1) % self.size]) for i in range(self.size)]
        self.down = [(b, a) for a, b in self.up]
        index = lax.axis_index("dp")
        row, column = index // 2, index % 2
        self.place = jnp.where(column == 0, row, self.size - 1 - row)
        self.small = self.size <= 16 and self.size % 2 == 0

    def owner(self, distance):
        place = (self.place + distance + 2 * self.size) % self.size
        return jnp.where(place < self.size // 2, 2 * place, 2 * (self.size - 1 - place) + 1)

    def step(self, going_up, going_down):
        going_up = lax.ppermute(going_up, "dp", self.up)
        going_down = lax.ppermute(going_down, "dp", self.down)
        return going_up, going_down

    def gather(self, block, splits):
        if not self.small:
            whole = lax.all_gather(block.reshape(1, *block.shape), "dp", axis=0, tiled=True)
            parts, start = [], 0
            for rows in splits:
                part = whole[:, start : start + rows]
                parts.append(part.reshape(self.size * rows, block.shape[1]))
                start += rows
            return parts
        total = block.shape[0]
        wholes = [jnp.zeros((self.size * rows, block.shape[1]), block.dtype) for rows in splits]

        def put(part, first, distance):
            start = 0
            for i, rows in enumerate(splits):
                low, high = max(start, first), min(start + rows, first + part.shape[0])
                if low < high:
                    wholes[i] = lax.dynamic_update_slice_in_dim(
                        wholes[i],
                        part[low - first : high - first],
                        self.owner(distance) * rows + (low - start),
                        0,
                    )
                start += rows

        put(block, 0, 0)
        going_up = going_down = block
        middle = self.size // 2
        for step in range(1, middle):
            going_up, going_down = self.step(going_up, going_down)
            put(going_up, 0, -step)
            put(going_down, 0, step)
        cut = total // 2
        first, second = self.step(going_up[:cut], going_down[cut:])
        put(first, 0, middle)
        put(second, cut, middle)
        return wholes

    def scatter(self, layout, shapes, vectors=()):
        if not self.small:
            owned = []
            for row in layout:
                for left, right in row:
                    whole = matmul_tn(left, right).astype(BF16)
                    owned.append(lax.psum_scatter(whole, "dp", scatter_dimension=0, tiled=True).astype(F32))
            outs = []
            for term, start, stop, turned in shapes:
                piece = owned[term][:, start:stop]
                outs.append(piece.T if turned else piece)
            if vectors:
                partial, other, *singles = vectors
                rows = [(partial + other)[i : i + 1] for i in range(partial.shape[0])] + singles
                outs.extend(lax.psum(rows, "dp"))
            return outs
        middle = self.size // 2
        arrived = list(ring_sum(layout, [self.owner(middle)] * 2, (), FIRST, (), vectors))
        apart = len(layout) > 1 and middle > 2
        for step in range(1, middle + 1):
            arrived[:2] = self.step(arrived[0], arrived[1])
            distance = middle - step
            if not distance and apart:
                arrived[2:] = self.step(arrived[2], arrived[3])
            stage = STEP if distance else LAST
            arrived = list(
                ring_sum(
                    layout,
                    [self.owner(distance), self.owner(-distance)],
                    arrived,
                    stage,
                    shapes,
                    vectors,
                    distance == 1 and apart,
                )
            )
        return arrived


FIRST, STEP, LAST = range(3)
VECTOR_ROWS = 8


def split_low(value):
    high = value.astype(BF16)
    return high, (value - high.astype(F32)).astype(BF16)


def ring_sum_kernel(places, stage, shapes, has_vectors, owners_ref, *refs):
    count = len(places)
    lefts, rights, rest = refs[:count], refs[count : 2 * count], refs[2 * count :]
    rows = places[0][2]
    total = max(place[0] for place in places) + rows
    half = total // 2
    extra = 2 * VECTOR_ROWS if has_vectors else 0

    def term(i, direction):
        start = pl.multiple_of(owners_ref[direction] * rows, rows)
        return matmul_tn(lefts[i][:, pl.ds(start, rows)], rights[i][...])

    by_row = stage != FIRST and not has_vectors and len(rest) == (4 + len(shapes) if stage == LAST else 6)

    def vectors_in(ref):
        first = ref.shape[0] - extra
        high = ref[first : first + VECTOR_ROWS].astype(F32)
        return high + ref[first + VECTOR_ROWS : first + extra].astype(F32)

    if has_vectors and stage == FIRST:
        partial_ref, other_ref, *single_refs = rest[:5]
        rest = rest[5:]
        sum_ref = rest[2]
        row, column = partial_ref.shape[0], 0
        sum_ref[...] = jnp.zeros_like(sum_ref)
        sum_ref[:row] = partial_ref[...] + other_ref[...]
        for ref in single_refs:
            width = ref.shape[1]
            if column + width > sum_ref.shape[1]:
                row, column = row + 1, 0
            sum_ref[row : row + 1, column : column + width] = ref[...]
            column += width
        high, low = split_low(sum_ref[...])
        for target in rest[:2]:
            first = target.shape[0] - extra
            target[first : first + VECTOR_ROWS] = high
            target[first + VECTOR_ROWS : first + extra] = low
    elif has_vectors and stage == STEP:
        rest[5][...] = rest[2][...] + vectors_in(rest[0]) + vectors_in(rest[1])
        for arrived, target in zip(rest[:2], rest[3:5]):
            target[target.shape[0] - extra :] = arrived[arrived.shape[0] - extra :]
        rest = (rest[0], rest[1], rest[3], rest[4])
    elif has_vectors:
        sums = rest[2][...] + vectors_in(rest[0])
        rest = rest[:2] + rest[3:]
        for target, (row, column) in zip(rest[2 + len(shapes) :], vector_places(rest[2 + len(shapes) :])):
            target[...] = sums[row : row + 1, column : column + target.shape[1]]

    for i, (row, column, _, width) in enumerate(places):
        columns = slice(column, column + width)
        if stage == FIRST:
            value = term(i, 0).astype(BF16)
            if row < half:
                rest[0][row : min(row + rows, half), columns] = value[: half - row]
            if row + rows > half:
                first = max(row, half)
                rest[1][first - half : row + rows - half, columns] = value[first - row :]
        elif stage == STEP:
            whole = rest[0].shape[0] == total + extra
            for direction, (low, high) in enumerate(((0, half), (half, total))):
                if whole:
                    low, high = 0, total
                value, arrived = term(i, direction), rest[direction]
                if by_row:
                    added = value + arrived[row : row + rows, columns].astype(F32)
                    rest[2 + 2 * (row // rows) + direction][:, columns] = added.astype(BF16)
                    continue
                target = rest[2 + direction]
                first, last = max(row, low), min(row + rows, high)
                if first < last:
                    added = value[first - row : last - row] + arrived[first - low : last - low, columns].astype(F32)
                    target[first:last, columns] = added.astype(BF16)
                for begin, end in ((row, min(low, row + rows)), (max(high, row), row + rows)):
                    if begin < end:
                        target[begin:end, columns] = value[begin - row : end - row].astype(BF16)
        else:
            pair, first = (2 * (row // rows), 0) if by_row else (0, row)
            value = term(i, 0) + rest[pair][first : first + rows, columns].astype(F32)
            value = value + rest[pair + 1][first : first + rows, columns].astype(F32)
            targets = rest[4:] if by_row else rest[2 : 2 + len(shapes)]
            for target, (source, start, stop, turned) in zip(targets, shapes):
                if source == i:
                    target[...] = value[:, start:stop].T if turned else value[:, start:stop]


def vector_places(arrays):
    places, row, column, full = [], 0, 0, arrays[0].shape[1]
    for array in arrays:
        if column + array.shape[1] > full:
            row, column = row + 1, 0
        places.append((row, column))
        column += array.shape[1]
    return places


def ring_sum(layout, owners, arrived, stage, shapes, vectors, apart=False):
    size = lax.axis_size("dp")
    places, lefts, rights, row = [], [], [], 0
    for terms in layout:
        column = 0
        for left, right in terms:
            rows = left.shape[1] // size
            places.append((row, column, rows, right.shape[1]))
            lefts.append(left)
            rights.append(right)
            column += right.shape[1]
        row += rows
    extra = 2 * VECTOR_ROWS if vectors else 0
    operands = [*lefts, *rights, *arrived]
    out_shape = []
    if stage == LAST:
        for term, start, stop, turned in shapes:
            shape = (places[term][2], stop - start)
            out_shape.append(jax.ShapeDtypeStruct(shape[::-1] if turned else shape, F32))
        if vectors:
            out_shape += [jax.ShapeDtypeStruct((1, column), F32)] * vectors[0].shape[0]
            out_shape += [jax.ShapeDtypeStruct(single.shape, F32) for single in vectors[2:]]
    else:
        travels = (row // 2 if stage == FIRST else row) + extra
        out_shape = [jax.ShapeDtypeStruct((travels, column), BF16)] * 2
        if apart:
            out_shape = [jax.ShapeDtypeStruct((row // len(layout), column), BF16)] * (2 * len(layout))
        if vectors:
            out_shape.append(jax.ShapeDtypeStruct((VECTOR_ROWS, column), F32))
        if stage == FIRST:
            operands += vectors
    vmem = pl.BlockSpec(memory_space=pltpu.VMEM)
    return pl.pallas_call(
        functools.partial(ring_sum_kernel, places, stage, shapes, bool(vectors)),
        in_specs=[pl.BlockSpec(memory_space=pltpu.SMEM)] + [vmem] * len(operands),
        out_specs=[vmem] * len(out_shape),
        out_shape=out_shape,
        cost_estimate=pl.CostEstimate(
            flops=4 * row * column * lefts[0].shape[0],
            bytes_accessed=12 * row * column,
            transcendentals=0,
        ),
        compiler_params=pltpu.CompilerParams(vmem_limit_bytes=KERNEL_VMEM),
        name="ring_sum",
    )(jnp.stack(owners), *operands)


def row_major(array):
    return with_layout_constraint(array, Layout(major_to_minor=(0, 1)))


LANES = 128
QUERY_TILE = 256


def keep_head(block, head, other=None):
    lane = lax.broadcasted_iota(jnp.int32, block.shape, 1)
    kept = (lane >= head * HD) & (lane < (head + 1) * HD)
    rest = jnp.zeros_like(block)
    if other is not None:
        spare = HD * (1 - head)
        rest = jnp.where(lane == spare, other, rest)
    return jnp.where(kept, block, rest)


def key_offsets(shape, counts_ref):
    rows = shape[0] // counts_ref.shape[0]
    row = lax.broadcasted_iota(jnp.int32, (rows, shape[1]), 0)
    parts = [jnp.where(row < counts_ref[r], 0.0, MASKED) for r in range(counts_ref.shape[0])]
    return jnp.concatenate(parts, axis=0).astype(BF16)


def scores_of(keys, offsets, scaled_queries, head):
    with_offsets = keep_head(keys, head, offsets)
    with_ones = keep_head(scaled_queries, head, jnp.ones_like(scaled_queries))
    return matmul_nt(with_offsets, with_ones)


def attention_kernel(score_scale, counts_ref, query_ref, key_ref, value_ref, context_ref, log_total_ref):
    keys, values = key_ref[...], value_ref[...]
    offsets = key_offsets(keys.shape, counts_ref)
    queries = query_ref[...] * jnp.asarray(score_scale, BF16)
    pieces = []
    for head in range(LANES // HD):
        scores = scores_of(keys, offsets, queries, head)
        row_peak = jnp.max(scores, axis=0, keepdims=True)
        raised = jnp.exp(scores - row_peak)
        total = jnp.sum(raised, axis=0, keepdims=True)
        log_total_ref[0, head : head + 1, :] = row_peak + jnp.log(total)
        both = matmul_tn(values, raised.astype(BF16))
        pieces.append(both[head * HD : (head + 1) * HD] * (1.0 / total))
    context_ref[...] = jnp.concatenate(pieces, axis=0).T.astype(BF16)


def attention(qkv_low, counts, local_width, score_scale):
    seq_len = qkv_low.shape[0]
    pairs = local_width // LANES
    tiles = seq_len // QUERY_TILE
    return pl.pallas_call(
        functools.partial(attention_kernel, score_scale),
        grid=(pairs, tiles),
        in_specs=[
            pl.BlockSpec(memory_space=pltpu.SMEM),
            pl.BlockSpec((QUERY_TILE, LANES), lambda j, i: (i, j)),
            pl.BlockSpec((seq_len, LANES), lambda j, i: (0, pairs + j)),
            pl.BlockSpec((seq_len, LANES), lambda j, i: (0, 2 * pairs + j)),
        ],
        out_specs=[
            pl.BlockSpec((QUERY_TILE, LANES), lambda j, i: (i, j)),
            pl.BlockSpec((1, LANES // HD, QUERY_TILE), lambda j, i: (j, 0, i)),
        ],
        out_shape=[
            jax.ShapeDtypeStruct((seq_len, local_width), BF16),
            jax.ShapeDtypeStruct((pairs, LANES // HD, seq_len), F32),
        ],
        cost_estimate=pl.CostEstimate(
            flops=4 * seq_len * seq_len * local_width,
            bytes_accessed=8 * seq_len * local_width,
            transcendentals=seq_len * seq_len * local_width // HD,
        ),
        compiler_params=pltpu.CompilerParams(vmem_limit_bytes=KERNEL_VMEM),
        name="attention",
    )(counts, qkv_low, qkv_low, qkv_low)


def attention_grad_kernel(
    score_scale,
    counts_ref,
    query_ref,
    key_ref,
    value_ref,
    upstream_ref,
    log_total_ref,
    low_ref,
    query_sum_ref,
    value_sum_ref,
    key_total,
    value_total,
):
    pair, step = pl.program_id(0), pl.program_id(1)
    width = low_ref.shape[1] // 3

    @pl.when(step == 0)
    def _():
        key_total[...] = jnp.zeros_like(key_total)
        value_total[...] = jnp.zeros_like(value_total)
        query_sum_ref[...] = jnp.zeros_like(query_sum_ref)

    keys, values = key_ref[...], value_ref[...]
    offsets = key_offsets(keys.shape, counts_ref)
    scale = jnp.asarray(score_scale, BF16)
    queries, scaled_keys = query_ref[...] * scale, keys * scale
    pieces = []
    for head in range(LANES // HD):
        upstream = keep_head(upstream_ref[...], head)
        scores = scores_of(keys, offsets, queries, head)
        probs = jnp.exp(scores - log_total_ref[0, head : head + 1, :])
        prob_grad = matmul_nt(values, upstream)
        row_inner = jnp.sum(probs * prob_grad, axis=0, keepdims=True)
        score_grad = (probs * (prob_grad - row_inner)).astype(BF16)
        value_total[...] += matmul(probs.astype(BF16), upstream)
        key_total[...] += matmul(score_grad, keep_head(queries, head))
        both = matmul_tn(scaled_keys, score_grad)
        pieces.append(both[head * HD : (head + 1) * HD])
    query_grad = jnp.concatenate(pieces, axis=0).T
    rows = pl.ds(pl.multiple_of(step * QUERY_TILE, QUERY_TILE), QUERY_TILE)
    start = pl.multiple_of(pair * LANES, LANES)
    low_ref[rows, pl.ds(start, LANES)] = query_grad.astype(BF16)
    query_sum_ref[...] += jnp.sum(query_grad, axis=0, keepdims=True)

    @pl.when(step == pl.num_programs(1) - 1)
    def _():
        low_ref[:, pl.ds(start + width, LANES)] = key_total[...].astype(BF16)
        low_ref[:, pl.ds(start + 2 * width, LANES)] = value_total[...].astype(BF16)
        value_sum_ref[...] = jnp.sum(value_total[...], axis=0, keepdims=True)


def attention_grad(qkv_low, upstream, log_total, counts, local_width, score_scale):
    seq_len = qkv_low.shape[0]
    pairs = local_width // LANES
    tiles = seq_len // QUERY_TILE
    tile_spec = pl.BlockSpec((QUERY_TILE, LANES), lambda j, i: (i, j))
    sum_spec = pl.BlockSpec((1, LANES), lambda j, i: (0, j))
    sums = jax.ShapeDtypeStruct((1, local_width), F32)
    return pl.pallas_call(
        functools.partial(attention_grad_kernel, score_scale),
        grid=(pairs, tiles),
        in_specs=[
            pl.BlockSpec(memory_space=pltpu.SMEM),
            tile_spec,
            pl.BlockSpec((seq_len, LANES), lambda j, i: (0, pairs + j)),
            pl.BlockSpec((seq_len, LANES), lambda j, i: (0, 2 * pairs + j)),
            tile_spec,
            pl.BlockSpec((1, LANES // HD, QUERY_TILE), lambda j, i: (j, 0, i)),
        ],
        out_specs=[pl.BlockSpec((seq_len, 3 * local_width), lambda j, i: (0, 0)), sum_spec, sum_spec],
        out_shape=[jax.ShapeDtypeStruct((seq_len, 3 * local_width), BF16), sums, sums],
        scratch_shapes=[pltpu.VMEM((seq_len, LANES), F32), pltpu.VMEM((seq_len, LANES), F32)],
        cost_estimate=pl.CostEstimate(
            flops=10 * seq_len * seq_len * local_width,
            bytes_accessed=16 * seq_len * local_width,
            transcendentals=seq_len * seq_len * local_width // HD,
        ),
        compiler_params=pltpu.CompilerParams(vmem_limit_bytes=KERNEL_VMEM),
        name="attention_grad",
    )(counts, qkv_low, qkv_low, qkv_low, upstream, log_total)


def layer(
    hidden_in,
    cotangent,
    lengths,
    query_weight,
    key_weight,
    value_weight,
    output_weight,
    up_weight,
    down_weight,
    query_bias,
    value_bias,
    output_bias,
    up_bias,
    down_bias,
    first_gain,
    first_shift,
    second_gain,
    second_shift,
):
    n_tensor = lax.axis_size("tensor")
    tensor_index = lax.axis_index("tensor")
    local_rows = hidden_in.shape[0]
    local_width = query_weight.shape[1]
    score_scale = HD ** (-0.5)
    ring = Ring()
    blocks = jnp.arange(n_tensor, dtype=jnp.int32) ^ tensor_index
    counts = lengths[0] - blocks * local_rows

    packed = row_major(jnp.concatenate([query_weight, key_weight, value_weight, output_weight.T], axis=1))
    (packed_full,) = ring.gather(packed, (packed.shape[0],))
    hidden_full = gather_rows(hidden_in)
    (up_full,) = ring.gather(up_weight, (up_weight.shape[0],))
    (down_turned,) = ring.gather(row_major(down_weight.T), (down_weight.shape[1],))
    qkv_full = packed_full[:, : 3 * local_width]
    output_turned = packed_full[:, 3 * local_width :]

    qkv_bias = jnp.concatenate([query_bias, jnp.zeros_like(query_bias), value_bias])
    qkv_low = (matmul(hidden_full, qkv_full) + qkv_bias).astype(BF16)
    context, log_total = attention(qkv_low, counts, local_width, score_scale)
    attn_rows = scatter_rows(matmul_nt(context, output_turned).astype(BF16))
    first_sum = hidden_in.astype(F32) + attn_rows + output_bias
    first_out, first_normed, first_inverse = norm_forward(first_sum, first_gain, first_shift)
    normed_full = gather_rows(first_out.astype(BF16))
    pre_act = matmul(normed_full, up_full) + up_bias
    activated, slope = lax.optimization_barrier((gelu_value(pre_act).astype(BF16), gelu_slope(pre_act)))
    mlp_rows = scatter_rows(matmul_nt(activated, down_turned).astype(BF16))
    second_sum = first_out + mlp_rows + down_bias
    second_out, second_normed, second_inverse = norm_forward(second_sum, second_gain, second_shift)
    hidden_out = second_out.astype(BF16)

    upstream = cotangent.astype(F32)
    grad_second_gain = jnp.sum(upstream * second_normed, axis=0)
    grad_second_shift = jnp.sum(upstream, axis=0)
    second_grad = norm_backward(upstream, second_gain, second_normed, second_inverse)
    grad_down_bias = jnp.sum(second_grad, axis=0)
    second_full = gather_rows(second_grad.astype(BF16))
    pre_grad = matmul(second_full, down_turned) * slope
    grad_up_bias, pre_low = lax.optimization_barrier((jnp.sum(pre_grad, axis=0), pre_grad.astype(BF16)))
    partial = matmul_nt(pre_low, up_full).astype(BF16)
    up_owned, down_owned = ring.scatter(
        [[(normed_full, pre_low)], [(second_full, activated)]],
        ((0, 0, up_weight.shape[1], False), (1, 0, down_weight.shape[0], True)),
    )
    first_grad_in = second_grad + scatter_rows(partial)
    grad_first_gain = jnp.sum(first_grad_in * first_normed, axis=0)
    grad_first_shift = jnp.sum(first_grad_in, axis=0)
    first_grad = norm_backward(first_grad_in, first_gain, first_normed, first_inverse)
    grad_output_bias = jnp.sum(first_grad, axis=0)
    attn_grad_full = gather_rows(first_grad.astype(BF16))
    context_grad = matmul(attn_grad_full, output_turned).astype(BF16)

    everywhere = jnp.stack(
        [grad_second_gain, grad_second_shift, grad_down_bias, grad_first_gain, grad_first_shift, grad_output_bias]
    )
    everywhere = everywhere + swap(everywhere, "tensor", 1)
    everywhere_far = swap(everywhere, "tensor", 2)

    low, query_sum, value_sum = attention_grad(
        qkv_low, context_grad, log_total, counts, local_width, score_scale
    )
    query_owned, key_owned, value_owned, output_owned, *sums = ring.scatter(
        [[(hidden_full, low), (attn_grad_full, context)]],
        tuple((0, i * local_width, (i + 1) * local_width, False) for i in range(3)) + ((1, 0, local_width, True),),
        (everywhere, everywhere_far, grad_up_bias.reshape(1, -1), query_sum, value_sum),
    )
    sums = [vector.reshape(-1) for vector in sums]
    back = matmul_nt(low, qkv_full).astype(BF16)
    back = scatter_rows(back)
    grad_in = (first_grad + back).astype(BF16)
    return (
        hidden_out,
        grad_in,
        query_owned,
        key_owned,
        value_owned,
        output_owned,
        up_owned,
        down_owned,
        sums[7],
        sums[8],
        sums[5],
        sums[6],
        sums[2],
        sums[3],
        sums[4],
        sums[0],
        sums[1],
    )


def solution(mesh):
    in_specs = (
        P(("dp", "tensor"), None),
        P(("dp", "tensor"), None),
        P("dp"),
        P("dp", "tensor"),
        P("dp", "tensor"),
        P("dp", "tensor"),
        P("tensor", "dp"),
        P("dp", "tensor"),
        P("tensor", "dp"),
        P("tensor"),
        P("tensor"),
        P(),
        P("tensor"),
        P(),
        P(),
        P(),
        P(),
        P(),
    )
    out_specs = (
        P(("dp", "tensor"), None),
        P(("dp", "tensor"), None),
        P("dp", "tensor"),
        P("dp", "tensor"),
        P("dp", "tensor"),
        P("tensor", "dp"),
        P("dp", "tensor"),
        P("tensor", "dp"),
        P("tensor"),
        P("tensor"),
        P(),
        P("tensor"),
        P(),
        P(),
        P(),
        P(),
        P(),
    )
    return jax.shard_map(layer, mesh=mesh, in_specs=in_specs, out_specs=out_specs, check_vma=False)
```

```python
import functools

import jax
import jax.numpy as jnp
from jax import lax
from jax.experimental import pallas as pl
from jax.experimental.layout import Layout, with_layout_constraint
from jax.experimental.pallas import tpu as pltpu
from jax.sharding import PartitionSpec as P


HD = 64


EPSILON = 1e-12
ROOT_HALF = 0.7071067811865476
INV_ROOT_TWO_PI = 0.3989422804014327
MASKED = -1e30
BF16 = jnp.bfloat16
F32 = jnp.float32
KERNEL_VMEM = 16 << 20


def matmul(left_side, right_side):
    return jnp.dot(left_side, right_side, preferred_element_type=F32)


def matmul_nt(left_side, right_side):
    return lax.dot_general(left_side, right_side, (((1,), (1,)), ((), ())), preferred_element_type=F32)


def matmul_tn(left_side, right_side):
    return lax.dot_general(left_side, right_side, (((0,), (0,)), ((), ())), preferred_element_type=F32)


def gelu_value(pre_act):
    return pre_act * 0.5 * (1.0 + lax.erf(pre_act * ROOT_HALF))


def gelu_slope(pre_act):
    cumulative = 0.5 * (1.0 + lax.erf(pre_act * ROOT_HALF))
    density = jnp.exp(-0.5 * pre_act * pre_act) * INV_ROOT_TWO_PI
    return cumulative + pre_act * density


def norm_forward(summed, gain_vector, shift_vector):
    centre = summed - jnp.mean(summed, axis=-1, keepdims=True)
    spread = jnp.mean(centre * centre, axis=-1, keepdims=True)
    inverse = lax.rsqrt(spread + EPSILON)
    normed = centre * inverse
    return (normed * gain_vector + shift_vector, normed, inverse)


def norm_backward(upstream, gain_vector, normed, inverse):
    scaled = upstream * gain_vector
    return inverse * (
        scaled
        - jnp.mean(scaled, axis=-1, keepdims=True)
        - normed * jnp.mean(scaled * normed, axis=-1, keepdims=True)
    )


def sum_of(refs):
    first, *others = refs
    total = first[...].astype(F32)
    for ref in others:
        total = total + ref[...].astype(F32)
    return total


def first_norm_kernel(*refs):
    bias, gain, shift = (ref[...] for ref in refs[4:7])
    out_ref, normed_ref, inverse_ref, low_ref = refs[7:]
    out, normed, inverse = norm_forward(sum_of(refs[:4]) + bias, gain, shift)
    out_ref[...], normed_ref[...], inverse_ref[...] = out, normed, inverse
    low_ref[...] = out.astype(BF16)


def second_norm_kernel(*refs):
    bias, gain, shift, upstream = (ref[...].astype(F32) for ref in refs[4:8])
    out_ref, grad_ref, low_ref, sums_ref = refs[8:]
    out, normed, inverse = norm_forward(sum_of(refs[:4]) + bias, gain, shift)
    out_ref[...] = out.astype(BF16)
    grad = norm_backward(upstream, gain, normed, inverse)
    grad_ref[...] = grad
    low_ref[...] = grad.astype(BF16)
    sums_ref[0:1] = jnp.sum(upstream * normed, axis=0, keepdims=True)
    sums_ref[1:2] = jnp.sum(upstream, axis=0, keepdims=True)
    sums_ref[2:3] = jnp.sum(grad, axis=0, keepdims=True)


def first_grad_kernel(*refs):
    gain, normed, inverse = (ref[...] for ref in refs[4:7])
    grad_ref, low_ref, sums_ref = refs[7:]
    upstream = sum_of(refs[:4])
    grad = norm_backward(upstream, gain, normed, inverse)
    grad_ref[...] = grad
    low_ref[...] = grad.astype(BF16)
    sums_ref[0:1] = jnp.sum(upstream * normed, axis=0, keepdims=True)
    sums_ref[1:2] = jnp.sum(upstream, axis=0, keepdims=True)
    sums_ref[2:3] = jnp.sum(grad, axis=0, keepdims=True)


def norm_stage(kernel, operands, outs):
    vmem = pl.BlockSpec(memory_space=pltpu.VMEM)
    size = operands[0].size
    return pl.pallas_call(
        kernel,
        in_specs=[vmem] * len(operands),
        out_specs=[vmem] * len(outs),
        out_shape=[jax.ShapeDtypeStruct(shape, dtype) for shape, dtype in outs],
        cost_estimate=pl.CostEstimate(flops=20 * size, bytes_accessed=16 * size, transcendentals=0),
        compiler_params=pltpu.CompilerParams(vmem_limit_bytes=KERNEL_VMEM),
    )(*(array.reshape(1, -1) if array.ndim == 1 else array for array in operands))


def swap(array, axis, bit):
    size = lax.axis_size(axis)
    return lax.ppermute(array, axis, [(i, i ^ bit) for i in range(size)])


def gather_rows(block):
    far = swap(block, "tensor", 2)
    other_core = swap(block, "tensor", 1)
    far_core = swap(far, "tensor", 1)
    return jnp.concatenate([block, other_core, far, far_core], axis=0)


def scatter_rows(partial):
    rows = partial.shape[0] // 4
    own, other_core, far, far_core = (partial[i * rows : (i + 1) * rows] for i in range(4))
    far_sum = (far.astype(F32) + swap(far_core, "tensor", 1).astype(F32)).astype(BF16)
    from_far = swap(far_sum, "tensor", 2)
    from_core = swap(other_core, "tensor", 1)
    return own, from_core, from_far


class Ring:
    def __init__(self):
        self.size = lax.axis_size("dp")
        half = self.size // 2
        order = [2 * i for i in range(half)] + [2 * (self.size - 1 - i) + 1 for i in range(half, self.size)]
        self.up = [(order[i], order[(i + 1) % self.size]) for i in range(self.size)]
        self.down = [(b, a) for a, b in self.up]
        index = lax.axis_index("dp")
        row, column = index // 2, index % 2
        self.place = jnp.where(column == 0, row, self.size - 1 - row)
        self.small = self.size <= 16 and self.size % 2 == 0

    def owner(self, distance):
        place = (self.place + distance + 2 * self.size) % self.size
        return jnp.where(place < self.size // 2, 2 * place, 2 * (self.size - 1 - place) + 1)

    def step(self, going_up, going_down):
        going_up = lax.ppermute(going_up, "dp", self.up)
        going_down = lax.ppermute(going_down, "dp", self.down)
        return going_up, going_down

    def gather(self, block, splits):
        if not self.small:
            whole = lax.all_gather(block.reshape(1, *block.shape), "dp", axis=0, tiled=True)
            parts, start = [], 0
            for rows in splits:
                part = whole[:, start : start + rows]
                parts.append(part.reshape(self.size * rows, block.shape[1]))
                start += rows
            return parts
        total = block.shape[0]
        wholes = [jnp.zeros((self.size * rows, block.shape[1]), block.dtype) for rows in splits]

        def put(part, first, distance):
            start = 0
            for i, rows in enumerate(splits):
                low, high = max(start, first), min(start + rows, first + part.shape[0])
                if low < high:
                    wholes[i] = lax.dynamic_update_slice_in_dim(
                        wholes[i],
                        part[low - first : high - first],
                        self.owner(distance) * rows + (low - start),
                        0,
                    )
                start += rows

        put(block, 0, 0)
        going_up = going_down = block
        middle = self.size // 2
        for step in range(1, middle):
            going_up, going_down = self.step(going_up, going_down)
            put(going_up, 0, -step)
            put(going_down, 0, step)
        cut = total // 2
        first, second = self.step(going_up[:cut], going_down[cut:])
        put(first, 0, middle)
        put(second, cut, middle)
        return wholes

    def scatter(self, layout, shapes, vectors=()):
        if not self.small:
            owned = []
            for row in layout:
                for left, right in row:
                    whole = matmul_tn(left, right).astype(BF16)
                    owned.append(lax.psum_scatter(whole, "dp", scatter_dimension=0, tiled=True).astype(F32))
            outs = []
            for term, start, stop, turned in shapes:
                piece = owned[term][:, start:stop]
                outs.append(piece.T if turned else piece)
            if vectors:
                partial, other, *singles = vectors
                rows = [(partial + other)[i : i + 1] for i in range(partial.shape[0])] + singles
                outs.extend(lax.psum(rows, "dp"))
            return outs
        middle = self.size // 2
        arrived = list(ring_sum(layout, [self.owner(middle)] * 2, (), FIRST, (), vectors))
        apart = len(layout) > 1 and middle > 2
        for step in range(1, middle + 1):
            arrived[:2] = self.step(arrived[0], arrived[1])
            distance = middle - step
            if not distance and apart:
                arrived[2:] = self.step(arrived[2], arrived[3])
            stage = STEP if distance else LAST
            arrived = list(
                ring_sum(
                    layout,
                    [self.owner(distance), self.owner(-distance)],
                    arrived,
                    stage,
                    shapes,
                    vectors,
                    distance == 1 and apart,
                )
            )
        return arrived


FIRST, STEP, LAST = range(3)
VECTOR_ROWS = 8


def split_low(value):
    high = value.astype(BF16)
    return high, (value - high.astype(F32)).astype(BF16)


def ring_sum_kernel(places, stage, shapes, has_vectors, owners_ref, *refs):
    count = len(places)
    lefts, rights, rest = refs[:count], refs[count : 2 * count], refs[2 * count :]
    rows = places[0][2]
    total = max(place[0] for place in places) + rows
    half = total // 2
    extra = 2 * VECTOR_ROWS if has_vectors else 0

    def term(i, direction):
        start = pl.multiple_of(owners_ref[direction] * rows, rows)
        return matmul_tn(lefts[i][:, pl.ds(start, rows)], rights[i][...])

    by_row = stage != FIRST and not has_vectors and len(rest) == (4 + len(shapes) if stage == LAST else 6)

    def vectors_in(ref):
        first = ref.shape[0] - extra
        high = ref[first : first + VECTOR_ROWS].astype(F32)
        return high + ref[first + VECTOR_ROWS : first + extra].astype(F32)

    if has_vectors and stage == FIRST:
        partial_ref, other_ref, *single_refs = rest[:5]
        rest = rest[5:]
        sum_ref = rest[2]
        row, column = partial_ref.shape[0], 0
        sum_ref[...] = jnp.zeros_like(sum_ref)
        sum_ref[:row] = partial_ref[...] + other_ref[...]
        for ref in single_refs:
            width = ref.shape[1]
            if column + width > sum_ref.shape[1]:
                row, column = row + 1, 0
            sum_ref[row : row + 1, column : column + width] = ref[...]
            column += width
        high, low = split_low(sum_ref[...])
        for target in rest[:2]:
            first = target.shape[0] - extra
            target[first : first + VECTOR_ROWS] = high
            target[first + VECTOR_ROWS : first + extra] = low
    elif has_vectors and stage == STEP:
        rest[5][...] = rest[2][...] + vectors_in(rest[0]) + vectors_in(rest[1])
        for arrived, target in zip(rest[:2], rest[3:5]):
            target[target.shape[0] - extra :] = arrived[arrived.shape[0] - extra :]
        rest = (rest[0], rest[1], rest[3], rest[4])
    elif has_vectors:
        sums = rest[2][...] + vectors_in(rest[0])
        rest = rest[:2] + rest[3:]
        for target, (row, column) in zip(rest[2 + len(shapes) :], vector_places(rest[2 + len(shapes) :])):
            target[...] = sums[row : row + 1, column : column + target.shape[1]]

    for i, (row, column, _, width) in enumerate(places):
        columns = slice(column, column + width)
        if stage == FIRST:
            value = term(i, 0).astype(BF16)
            if row < half:
                rest[0][row : min(row + rows, half), columns] = value[: half - row]
            if row + rows > half:
                first = max(row, half)
                rest[1][first - half : row + rows - half, columns] = value[first - row :]
        elif stage == STEP:
            whole = rest[0].shape[0] == total + extra
            for direction, (low, high) in enumerate(((0, half), (half, total))):
                if whole:
                    low, high = 0, total
                value, arrived = term(i, direction), rest[direction]
                if by_row:
                    added = value + arrived[row : row + rows, columns].astype(F32)
                    rest[2 + 2 * (row // rows) + direction][:, columns] = added.astype(BF16)
                    continue
                target = rest[2 + direction]
                first, last = max(row, low), min(row + rows, high)
                if first < last:
                    added = value[first - row : last - row] + arrived[first - low : last - low, columns].astype(F32)
                    target[first:last, columns] = added.astype(BF16)
                for begin, end in ((row, min(low, row + rows)), (max(high, row), row + rows)):
                    if begin < end:
                        target[begin:end, columns] = value[begin - row : end - row].astype(BF16)
        else:
            pair, first = (2 * (row // rows), 0) if by_row else (0, row)
            value = term(i, 0) + rest[pair][first : first + rows, columns].astype(F32)
            value = value + rest[pair + 1][first : first + rows, columns].astype(F32)
            targets = rest[4:] if by_row else rest[2 : 2 + len(shapes)]
            for target, (source, start, stop, turned) in zip(targets, shapes):
                if source == i:
                    target[...] = value[:, start:stop].T if turned else value[:, start:stop]


def vector_places(arrays):
    places, row, column, full = [], 0, 0, arrays[0].shape[1]
    for array in arrays:
        if column + array.shape[1] > full:
            row, column = row + 1, 0
        places.append((row, column))
        column += array.shape[1]
    return places


def ring_sum(layout, owners, arrived, stage, shapes, vectors, apart=False):
    size = lax.axis_size("dp")
    places, lefts, rights, row = [], [], [], 0
    for terms in layout:
        column = 0
        for left, right in terms:
            rows = left.shape[1] // size
            places.append((row, column, rows, right.shape[1]))
            lefts.append(left)
            rights.append(right)
            column += right.shape[1]
        row += rows
    extra = 2 * VECTOR_ROWS if vectors else 0
    operands = [*lefts, *rights, *arrived]
    out_shape = []
    if stage == LAST:
        for term, start, stop, turned in shapes:
            shape = (places[term][2], stop - start)
            out_shape.append(jax.ShapeDtypeStruct(shape[::-1] if turned else shape, F32))
        if vectors:
            out_shape += [jax.ShapeDtypeStruct((1, column), F32)] * vectors[0].shape[0]
            out_shape += [jax.ShapeDtypeStruct(single.shape, F32) for single in vectors[2:]]
    else:
        travels = (row // 2 if stage == FIRST else row) + extra
        out_shape = [jax.ShapeDtypeStruct((travels, column), BF16)] * 2
        if apart:
            out_shape = [jax.ShapeDtypeStruct((row // len(layout), column), BF16)] * (2 * len(layout))
        if vectors:
            out_shape.append(jax.ShapeDtypeStruct((VECTOR_ROWS, column), F32))
        if stage == FIRST:
            operands += vectors
    vmem = pl.BlockSpec(memory_space=pltpu.VMEM)
    return pl.pallas_call(
        functools.partial(ring_sum_kernel, places, stage, shapes, bool(vectors)),
        in_specs=[pl.BlockSpec(memory_space=pltpu.SMEM)] + [vmem] * len(operands),
        out_specs=[vmem] * len(out_shape),
        out_shape=out_shape,
        cost_estimate=pl.CostEstimate(
            flops=4 * row * column * lefts[0].shape[0],
            bytes_accessed=12 * row * column,
            transcendentals=0,
        ),
        compiler_params=pltpu.CompilerParams(vmem_limit_bytes=KERNEL_VMEM),
        name="ring_sum",
    )(jnp.stack(owners), *operands)


def row_major(array):
    return with_layout_constraint(array, Layout(major_to_minor=(0, 1)))


LANES = 128
QUERY_TILE = 256


def keep_head(block, head, other=None):
    lane = lax.broadcasted_iota(jnp.int32, block.shape, 1)
    kept = (lane >= head * HD) & (lane < (head + 1) * HD)
    rest = jnp.zeros_like(block)
    if other is not None:
        spare = HD * (1 - head)
        rest = jnp.where(lane == spare, other, rest)
    return jnp.where(kept, block, rest)


def key_offsets(shape, counts_ref):
    rows = shape[0] // counts_ref.shape[0]
    row = lax.broadcasted_iota(jnp.int32, (rows, shape[1]), 0)
    parts = [jnp.where(row < counts_ref[r], 0.0, MASKED) for r in range(counts_ref.shape[0])]
    return jnp.concatenate(parts, axis=0).astype(BF16)


def scores_of(keys, offsets, scaled_queries, head):
    with_offsets = keep_head(keys, head, offsets)
    with_ones = keep_head(scaled_queries, head, jnp.ones_like(scaled_queries))
    return matmul_nt(with_offsets, with_ones)


def attention_kernel(score_scale, counts_ref, query_ref, key_ref, value_ref, context_ref, log_total_ref):
    keys, values = key_ref[...], value_ref[...]
    offsets = key_offsets(keys.shape, counts_ref)
    queries = query_ref[...] * jnp.asarray(score_scale, BF16)
    pieces = []
    for head in range(LANES // HD):
        scores = scores_of(keys, offsets, queries, head)
        row_peak = jnp.max(scores, axis=0, keepdims=True)
        raised = jnp.exp(scores - row_peak)
        total = jnp.sum(raised, axis=0, keepdims=True)
        log_total_ref[0, head : head + 1, :] = row_peak + jnp.log(total)
        both = matmul_tn(values, raised.astype(BF16))
        pieces.append(both[head * HD : (head + 1) * HD] * (1.0 / total))
    context_ref[...] = jnp.concatenate(pieces, axis=0).T.astype(BF16)


def attention(qkv_low, counts, local_width, score_scale):
    seq_len = qkv_low.shape[0]
    pairs = local_width // LANES
    tiles = seq_len // QUERY_TILE
    return pl.pallas_call(
        functools.partial(attention_kernel, score_scale),
        grid=(pairs, tiles),
        in_specs=[
            pl.BlockSpec(memory_space=pltpu.SMEM),
            pl.BlockSpec((QUERY_TILE, LANES), lambda j, i: (i, j)),
            pl.BlockSpec((seq_len, LANES), lambda j, i: (0, pairs + j)),
            pl.BlockSpec((seq_len, LANES), lambda j, i: (0, 2 * pairs + j)),
        ],
        out_specs=[
            pl.BlockSpec((QUERY_TILE, LANES), lambda j, i: (i, j)),
            pl.BlockSpec((1, LANES // HD, QUERY_TILE), lambda j, i: (j, 0, i)),
        ],
        out_shape=[
            jax.ShapeDtypeStruct((seq_len, local_width), BF16),
            jax.ShapeDtypeStruct((pairs, LANES // HD, seq_len), F32),
        ],
        cost_estimate=pl.CostEstimate(
            flops=4 * seq_len * seq_len * local_width,
            bytes_accessed=8 * seq_len * local_width,
            transcendentals=seq_len * seq_len * local_width // HD,
        ),
        compiler_params=pltpu.CompilerParams(vmem_limit_bytes=KERNEL_VMEM),
        name="attention",
    )(counts, qkv_low, qkv_low, qkv_low)


def attention_grad_kernel(
    score_scale,
    counts_ref,
    query_ref,
    key_ref,
    value_ref,
    upstream_ref,
    log_total_ref,
    low_ref,
    query_sum_ref,
    value_sum_ref,
    key_total,
    value_total,
):
    pair, step = pl.program_id(0), pl.program_id(1)
    width = low_ref.shape[1] // 3

    @pl.when(step == 0)
    def _():
        key_total[...] = jnp.zeros_like(key_total)
        value_total[...] = jnp.zeros_like(value_total)
        query_sum_ref[...] = jnp.zeros_like(query_sum_ref)

    keys, values = key_ref[...], value_ref[...]
    offsets = key_offsets(keys.shape, counts_ref)
    scale = jnp.asarray(score_scale, BF16)
    queries, scaled_keys = query_ref[...] * scale, keys * scale
    pieces = []
    for head in range(LANES // HD):
        upstream = keep_head(upstream_ref[...], head)
        scores = scores_of(keys, offsets, queries, head)
        probs = jnp.exp(scores - log_total_ref[0, head : head + 1, :])
        prob_grad = matmul_nt(values, upstream)
        row_inner = jnp.sum(probs * prob_grad, axis=0, keepdims=True)
        score_grad = (probs * (prob_grad - row_inner)).astype(BF16)
        value_total[...] += matmul(probs.astype(BF16), upstream)
        key_total[...] += matmul(score_grad, keep_head(queries, head))
        both = matmul_tn(scaled_keys, score_grad)
        pieces.append(both[head * HD : (head + 1) * HD])
    query_grad = jnp.concatenate(pieces, axis=0).T
    rows = pl.ds(pl.multiple_of(step * QUERY_TILE, QUERY_TILE), QUERY_TILE)
    start = pl.multiple_of(pair * LANES, LANES)
    low_ref[rows, pl.ds(start, LANES)] = query_grad.astype(BF16)
    query_sum_ref[...] += jnp.sum(query_grad, axis=0, keepdims=True)

    @pl.when(step == pl.num_programs(1) - 1)
    def _():
        low_ref[:, pl.ds(start + width, LANES)] = key_total[...].astype(BF16)
        low_ref[:, pl.ds(start + 2 * width, LANES)] = value_total[...].astype(BF16)
        value_sum_ref[...] = jnp.sum(value_total[...], axis=0, keepdims=True)


def attention_grad(qkv_low, upstream, log_total, counts, local_width, score_scale):
    seq_len = qkv_low.shape[0]
    pairs = local_width // LANES
    tiles = seq_len // QUERY_TILE
    tile_spec = pl.BlockSpec((QUERY_TILE, LANES), lambda j, i: (i, j))
    sum_spec = pl.BlockSpec((1, LANES), lambda j, i: (0, j))
    sums = jax.ShapeDtypeStruct((1, local_width), F32)
    return pl.pallas_call(
        functools.partial(attention_grad_kernel, score_scale),
        grid=(pairs, tiles),
        in_specs=[
            pl.BlockSpec(memory_space=pltpu.SMEM),
            tile_spec,
            pl.BlockSpec((seq_len, LANES), lambda j, i: (0, pairs + j)),
            pl.BlockSpec((seq_len, LANES), lambda j, i: (0, 2 * pairs + j)),
            tile_spec,
            pl.BlockSpec((1, LANES // HD, QUERY_TILE), lambda j, i: (j, 0, i)),
        ],
        out_specs=[pl.BlockSpec((seq_len, 3 * local_width), lambda j, i: (0, 0)), sum_spec, sum_spec],
        out_shape=[jax.ShapeDtypeStruct((seq_len, 3 * local_width), BF16), sums, sums],
        scratch_shapes=[pltpu.VMEM((seq_len, LANES), F32), pltpu.VMEM((seq_len, LANES), F32)],
        cost_estimate=pl.CostEstimate(
            flops=10 * seq_len * seq_len * local_width,
            bytes_accessed=16 * seq_len * local_width,
            transcendentals=seq_len * seq_len * local_width // HD,
        ),
        compiler_params=pltpu.CompilerParams(vmem_limit_bytes=KERNEL_VMEM),
        name="attention_grad",
    )(counts, qkv_low, qkv_low, qkv_low, upstream, log_total)


def layer(
    hidden_in,
    cotangent,
    lengths,
    query_weight,
    key_weight,
    value_weight,
    output_weight,
    up_weight,
    down_weight,
    query_bias,
    value_bias,
    output_bias,
    up_bias,
    down_bias,
    first_gain,
    first_shift,
    second_gain,
    second_shift,
):
    n_tensor = lax.axis_size("tensor")
    tensor_index = lax.axis_index("tensor")
    local_rows = hidden_in.shape[0]
    local_width = query_weight.shape[1]
    score_scale = HD ** (-0.5)
    ring = Ring()
    blocks = jnp.arange(n_tensor, dtype=jnp.int32) ^ tensor_index
    counts = lengths[0] - blocks * local_rows

    packed = row_major(jnp.concatenate([query_weight, key_weight, value_weight, output_weight.T], axis=1))
    (packed_full,) = ring.gather(packed, (packed.shape[0],))
    hidden_full = gather_rows(hidden_in)
    (up_full,) = ring.gather(up_weight, (up_weight.shape[0],))
    (down_turned,) = ring.gather(row_major(down_weight.T), (down_weight.shape[1],))
    qkv_full = packed_full[:, : 3 * local_width]
    output_turned = packed_full[:, 3 * local_width :]

    qkv_bias = jnp.concatenate([query_bias, jnp.zeros_like(query_bias), value_bias])
    qkv_low = (matmul(hidden_full, qkv_full) + qkv_bias).astype(BF16)
    context, log_total = attention(qkv_low, counts, local_width, score_scale)
    block, column, total = hidden_in.shape, (local_rows, 1), (3, hidden_in.shape[1])
    attn_parts = scatter_rows(matmul_nt(context, output_turned).astype(BF16))
    first_out, first_normed, first_inverse, first_low = norm_stage(
        first_norm_kernel,
        [hidden_in, *attn_parts, output_bias, first_gain, first_shift],
        [(block, F32), (block, F32), (column, F32), (block, BF16)],
    )
    normed_full = gather_rows(first_low)
    pre_act = matmul(normed_full, up_full) + up_bias
    activated, slope = lax.optimization_barrier((gelu_value(pre_act).astype(BF16), gelu_slope(pre_act)))
    mlp_parts = scatter_rows(matmul_nt(activated, down_turned).astype(BF16))
    hidden_out, second_grad, second_low, second_sums = norm_stage(
        second_norm_kernel,
        [first_out, *mlp_parts, down_bias, second_gain, second_shift, cotangent],
        [(block, BF16), (block, F32), (block, BF16), (total, F32)],
    )
    second_full = gather_rows(second_low)
    pre_grad = matmul(second_full, down_turned) * slope
    grad_up_bias, pre_low = lax.optimization_barrier((jnp.sum(pre_grad, axis=0), pre_grad.astype(BF16)))
    partial = matmul_nt(pre_low, up_full).astype(BF16)
    up_owned, down_owned = ring.scatter(
        [[(normed_full, pre_low)], [(second_full, activated)]],
        ((0, 0, up_weight.shape[1], False), (1, 0, down_weight.shape[0], True)),
    )
    first_grad, first_grad_low, first_sums = norm_stage(
        first_grad_kernel,
        [second_grad, *scatter_rows(partial), first_gain, first_normed, first_inverse],
        [(block, F32), (block, BF16), (total, F32)],
    )
    attn_grad_full = lax.optimization_barrier(gather_rows(first_grad_low))
    context_grad = matmul(attn_grad_full, output_turned).astype(BF16)

    everywhere = jnp.concatenate([second_sums, first_sums], axis=0)
    everywhere = everywhere + swap(everywhere, "tensor", 1)
    everywhere_far = swap(everywhere, "tensor", 2)

    low, query_sum, value_sum = attention_grad(
        qkv_low, context_grad, log_total, counts, local_width, score_scale
    )
    query_owned, key_owned, value_owned, output_owned, *sums = ring.scatter(
        [[(hidden_full, low), (attn_grad_full, context)]],
        tuple((0, i * local_width, (i + 1) * local_width, False) for i in range(3)) + ((1, 0, local_width, True),),
        (everywhere, everywhere_far, grad_up_bias.reshape(1, -1), query_sum, value_sum),
    )
    sums = [vector.reshape(-1) for vector in sums]
    back = matmul_nt(low, qkv_full).astype(BF16)
    back_parts = scatter_rows(back)
    grad_in = (first_grad + sum(part.astype(F32) for part in back_parts)).astype(BF16)
    return (
        hidden_out,
        grad_in,
        query_owned,
        key_owned,
        value_owned,
        output_owned,
        up_owned,
        down_owned,
        sums[7],
        sums[8],
        sums[5],
        sums[6],
        sums[2],
        sums[3],
        sums[4],
        sums[0],
        sums[1],
    )


def solution(mesh):
    in_specs = (
        P(("dp", "tensor"), None),
        P(("dp", "tensor"), None),
        P("dp"),
        P("dp", "tensor"),
        P("dp", "tensor"),
        P("dp", "tensor"),
        P("tensor", "dp"),
        P("dp", "tensor"),
        P("tensor", "dp"),
        P("tensor"),
        P("tensor"),
        P(),
        P("tensor"),
        P(),
        P(),
        P(),
        P(),
        P(),
    )
    out_specs = (
        P(("dp", "tensor"), None),
        P(("dp", "tensor"), None),
        P("dp", "tensor"),
        P("dp", "tensor"),
        P("dp", "tensor"),
        P("tensor", "dp"),
        P("dp", "tensor"),
        P("tensor", "dp"),
        P("tensor"),
        P("tensor"),
        P(),
        P("tensor"),
        P(),
        P(),
        P(),
        P(),
        P(),
    )
    return jax.shard_map(layer, mesh=mesh, in_specs=in_specs, out_specs=out_specs, check_vma=False)
```

```python
import functools

import jax
import jax.numpy as jnp
from jax import lax
from jax.experimental import pallas as pl
from jax.experimental.layout import Layout, with_layout_constraint
from jax.experimental.pallas import tpu as pltpu
from jax.sharding import PartitionSpec as P


HD = 64


EPSILON = 1e-12
ROOT_HALF = 0.7071067811865476
INV_ROOT_TWO_PI = 0.3989422804014327
MASKED = -1e30
BF16 = jnp.bfloat16
F32 = jnp.float32
KERNEL_VMEM = 16 << 20


def matmul(left_side, right_side):
    return jnp.dot(left_side, right_side, preferred_element_type=F32)


def matmul_nt(left_side, right_side):
    return lax.dot_general(left_side, right_side, (((1,), (1,)), ((), ())), preferred_element_type=F32)


def matmul_tn(left_side, right_side):
    return lax.dot_general(left_side, right_side, (((0,), (0,)), ((), ())), preferred_element_type=F32)


def gelu_value(pre_act):
    return pre_act * 0.5 * (1.0 + lax.erf(pre_act * ROOT_HALF))


def gelu_slope(pre_act):
    cumulative = 0.5 * (1.0 + lax.erf(pre_act * ROOT_HALF))
    density = jnp.exp(-0.5 * pre_act * pre_act) * INV_ROOT_TWO_PI
    return cumulative + pre_act * density


def norm_forward(summed, gain_vector, shift_vector):
    centre = summed - jnp.mean(summed, axis=-1, keepdims=True)
    spread = jnp.mean(centre * centre, axis=-1, keepdims=True)
    inverse = lax.rsqrt(spread + EPSILON)
    normed = centre * inverse
    return (normed * gain_vector + shift_vector, normed, inverse)


def norm_backward(upstream, gain_vector, normed, inverse):
    scaled = upstream * gain_vector
    return inverse * (
        scaled
        - jnp.mean(scaled, axis=-1, keepdims=True)
        - normed * jnp.mean(scaled * normed, axis=-1, keepdims=True)
    )


def sum_of(refs):
    first, *others = refs
    total = first[...].astype(F32)
    for ref in others:
        total = total + ref[...].astype(F32)
    return total


def first_norm_kernel(*refs):
    bias, gain, shift = (ref[...] for ref in refs[4:7])
    out_ref, normed_ref, inverse_ref, low_ref = refs[7:]
    out, normed, inverse = norm_forward(sum_of(refs[:4]) + bias, gain, shift)
    out_ref[...], normed_ref[...], inverse_ref[...] = out, normed, inverse
    low_ref[...] = out.astype(BF16)


def second_norm_kernel(*refs):
    bias, gain, shift, upstream = (ref[...].astype(F32) for ref in refs[4:8])
    out_ref, grad_ref, low_ref, sums_ref = refs[8:]
    out, normed, inverse = norm_forward(sum_of(refs[:4]) + bias, gain, shift)
    out_ref[...] = out.astype(BF16)
    grad = norm_backward(upstream, gain, normed, inverse)
    grad_ref[...] = grad
    low_ref[...] = grad.astype(BF16)
    sums_ref[0:1] = jnp.sum(upstream * normed, axis=0, keepdims=True)
    sums_ref[1:2] = jnp.sum(upstream, axis=0, keepdims=True)
    sums_ref[2:3] = jnp.sum(grad, axis=0, keepdims=True)


def first_grad_kernel(*refs):
    gain, normed, inverse = (ref[...] for ref in refs[4:7])
    grad_ref, low_ref, sums_ref = refs[7:]
    upstream = sum_of(refs[:4])
    grad = norm_backward(upstream, gain, normed, inverse)
    grad_ref[...] = grad
    low_ref[...] = grad.astype(BF16)
    sums_ref[0:1] = jnp.sum(upstream * normed, axis=0, keepdims=True)
    sums_ref[1:2] = jnp.sum(upstream, axis=0, keepdims=True)
    sums_ref[2:3] = jnp.sum(grad, axis=0, keepdims=True)


def norm_stage(kernel, operands, outs):
    vmem = pl.BlockSpec(memory_space=pltpu.VMEM)
    size = operands[0].size
    return pl.pallas_call(
        kernel,
        in_specs=[vmem] * len(operands),
        out_specs=[vmem] * len(outs),
        out_shape=[jax.ShapeDtypeStruct(shape, dtype) for shape, dtype in outs],
        cost_estimate=pl.CostEstimate(flops=20 * size, bytes_accessed=16 * size, transcendentals=0),
        compiler_params=pltpu.CompilerParams(vmem_limit_bytes=KERNEL_VMEM),
    )(*(array.reshape(1, -1) if array.ndim == 1 else array for array in operands))


def swap(array, axis, bit):
    size = lax.axis_size(axis)
    return lax.ppermute(array, axis, [(i, i ^ bit) for i in range(size)])


def gather_rows(block):
    far = swap(block, "tensor", 2)
    other_core = swap(block, "tensor", 1)
    far_core = swap(far, "tensor", 1)
    return jnp.concatenate([block, other_core], axis=0), jnp.concatenate([far, far_core], axis=0)


def halves(array):
    return jnp.split(array, 2, axis=0)


def scatter_rows(near, distant):
    own, other_core = halves(near)
    far, far_core = halves(distant)
    far_sum = (far.astype(F32) + swap(far_core, "tensor", 1).astype(F32)).astype(BF16)
    from_far = swap(far_sum, "tensor", 2)
    from_core = swap(other_core, "tensor", 1)
    return own, from_core, from_far


class Ring:
    def __init__(self):
        self.size = lax.axis_size("dp")
        half = self.size // 2
        order = [2 * i for i in range(half)] + [2 * (self.size - 1 - i) + 1 for i in range(half, self.size)]
        self.up = [(order[i], order[(i + 1) % self.size]) for i in range(self.size)]
        self.down = [(b, a) for a, b in self.up]
        index = lax.axis_index("dp")
        row, column = index // 2, index % 2
        self.place = jnp.where(column == 0, row, self.size - 1 - row)
        self.small = self.size <= 16 and self.size % 2 == 0

    def owner(self, distance):
        place = (self.place + distance + 2 * self.size) % self.size
        return jnp.where(place < self.size // 2, 2 * place, 2 * (self.size - 1 - place) + 1)

    def step(self, going_up, going_down):
        going_up = lax.ppermute(going_up, "dp", self.up)
        going_down = lax.ppermute(going_down, "dp", self.down)
        return going_up, going_down

    def gather(self, block, splits):
        if not self.small:
            whole = lax.all_gather(block.reshape(1, *block.shape), "dp", axis=0, tiled=True)
            parts, start = [], 0
            for rows in splits:
                part = whole[:, start : start + rows]
                parts.append(part.reshape(self.size * rows, block.shape[1]))
                start += rows
            return parts
        total = block.shape[0]
        wholes = [jnp.zeros((self.size * rows, block.shape[1]), block.dtype) for rows in splits]

        def put(part, first, distance):
            start = 0
            for i, rows in enumerate(splits):
                low, high = max(start, first), min(start + rows, first + part.shape[0])
                if low < high:
                    wholes[i] = lax.dynamic_update_slice_in_dim(
                        wholes[i],
                        part[low - first : high - first],
                        self.owner(distance) * rows + (low - start),
                        0,
                    )
                start += rows

        put(block, 0, 0)
        going_up = going_down = block
        middle = self.size // 2
        for step in range(1, middle):
            going_up, going_down = self.step(going_up, going_down)
            put(going_up, 0, -step)
            put(going_down, 0, step)
        cut = total // 2
        first, second = self.step(going_up[:cut], going_down[cut:])
        put(first, 0, middle)
        put(second, cut, middle)
        return wholes

    def scatter(self, layout, shapes, vectors=()):
        if not self.small:
            owned = []
            for row in layout:
                for lefts, rights in row:
                    whole = sum(matmul_tn(left, right) for left, right in zip(lefts, rights)).astype(BF16)
                    owned.append(lax.psum_scatter(whole, "dp", scatter_dimension=0, tiled=True).astype(F32))
            outs = []
            for term, start, stop, turned in shapes:
                piece = owned[term][:, start:stop]
                outs.append(piece.T if turned else piece)
            if vectors:
                partial, other, *singles = vectors
                rows = [(partial + other)[i : i + 1] for i in range(partial.shape[0])] + singles
                outs.extend(lax.psum(rows, "dp"))
            return outs
        middle = self.size // 2
        arrived = list(ring_sum(layout, [self.owner(middle)] * 2, (), FIRST, (), vectors))
        apart = len(layout) > 1 and middle > 2
        for step in range(1, middle + 1):
            arrived[:2] = self.step(arrived[0], arrived[1])
            distance = middle - step
            if not distance and apart:
                arrived[2:] = self.step(arrived[2], arrived[3])
            stage = STEP if distance else LAST
            arrived = list(
                ring_sum(
                    layout,
                    [self.owner(distance), self.owner(-distance)],
                    arrived,
                    stage,
                    shapes,
                    vectors,
                    distance == 1 and apart,
                )
            )
        return arrived


FIRST, STEP, LAST = range(3)
VECTOR_ROWS = 8


def ring_sum_kernel(places, counts, stage, shapes, has_vectors, owners_ref, *refs):
    pairs, used = [], 0
    for count in counts:
        pairs.append((refs[used : used + count], refs[used + count : used + 2 * count]))
        used += 2 * count
    rest = refs[used:]
    rows = places[0][2]
    total = max(place[0] for place in places) + rows
    half = total // 2
    extra = VECTOR_ROWS if has_vectors else 0

    def term(i, direction):
        columns = pl.ds(pl.multiple_of(owners_ref[direction] * rows, rows), rows)
        products = [matmul_tn(left[:, columns], right[...]) for left, right in zip(*pairs[i])]
        return sum(products[1:], products[0])

    by_row = stage != FIRST and not has_vectors and len(rest) == (4 + len(shapes) if stage == LAST else 6)

    def vectors_in(ref):
        return ref[ref.shape[0] - extra :].astype(F32)

    if has_vectors and stage == FIRST:
        partial_ref, other_ref, *single_refs = rest[:5]
        rest = rest[5:]
        sum_ref = rest[2]
        row, column = partial_ref.shape[0], 0
        sum_ref[...] = jnp.zeros_like(sum_ref)
        sum_ref[:row] = partial_ref[...] + other_ref[...]
        for ref in single_refs:
            width = ref.shape[1]
            if column + width > sum_ref.shape[1]:
                row, column = row + 1, 0
            sum_ref[row : row + 1, column : column + width] = ref[...]
            column += width
        for target in rest[:2]:
            target[target.shape[0] - extra :] = sum_ref[...].astype(BF16)
    elif has_vectors and stage == STEP:
        rest[5][...] = rest[2][...] + vectors_in(rest[0]) + vectors_in(rest[1])
        for arrived, target in zip(rest[:2], rest[3:5]):
            target[target.shape[0] - extra :] = arrived[arrived.shape[0] - extra :]
        rest = (rest[0], rest[1], rest[3], rest[4])
    elif has_vectors:
        sums = rest[2][...] + vectors_in(rest[0])
        rest = rest[:2] + rest[3:]
        for target, (row, column) in zip(rest[2 + len(shapes) :], vector_places(rest[2 + len(shapes) :])):
            target[...] = sums[row : row + 1, column : column + target.shape[1]]

    for i, (row, column, _, width) in enumerate(places):
        columns = slice(column, column + width)
        if stage == FIRST:
            value = term(i, 0).astype(BF16)
            if row < half:
                rest[0][row : min(row + rows, half), columns] = value[: half - row]
            if row + rows > half:
                first = max(row, half)
                rest[1][first - half : row + rows - half, columns] = value[first - row :]
        elif stage == STEP:
            whole = rest[0].shape[0] == total + extra
            for direction, (low, high) in enumerate(((0, half), (half, total))):
                if whole:
                    low, high = 0, total
                value, arrived = term(i, direction), rest[direction]
                if by_row:
                    added = value + arrived[row : row + rows, columns].astype(F32)
                    rest[2 + 2 * (row // rows) + direction][:, columns] = added.astype(BF16)
                    continue
                target = rest[2 + direction]
                first, last = max(row, low), min(row + rows, high)
                if first < last:
                    added = value[first - row : last - row] + arrived[first - low : last - low, columns].astype(F32)
                    target[first:last, columns] = added.astype(BF16)
                for begin, end in ((row, min(low, row + rows)), (max(high, row), row + rows)):
                    if begin < end:
                        target[begin:end, columns] = value[begin - row : end - row].astype(BF16)
        else:
            pair, first = (2 * (row // rows), 0) if by_row else (0, row)
            value = term(i, 0) + rest[pair][first : first + rows, columns].astype(F32)
            value = value + rest[pair + 1][first : first + rows, columns].astype(F32)
            targets = rest[4:] if by_row else rest[2 : 2 + len(shapes)]
            for target, (source, start, stop, turned) in zip(targets, shapes):
                if source == i:
                    target[...] = value[:, start:stop].T if turned else value[:, start:stop]


def vector_places(arrays):
    places, row, column, full = [], 0, 0, arrays[0].shape[1]
    for array in arrays:
        if column + array.shape[1] > full:
            row, column = row + 1, 0
        places.append((row, column))
        column += array.shape[1]
    return places


def ring_sum(layout, owners, arrived, stage, shapes, vectors, apart=False):
    size = lax.axis_size("dp")
    places, counts, operands, row = [], [], [], 0
    for terms in layout:
        column = 0
        for lefts, rights in terms:
            rows, width = lefts[0].shape[1] // size, rights[0].shape[1]
            places.append((row, column, rows, width))
            counts.append(len(lefts))
            operands += [*lefts, *rights]
            column += width
        row += rows
    extra = VECTOR_ROWS if vectors else 0
    depth = sum(array.shape[0] for array in layout[0][0][0])
    operands += arrived
    out_shape = []
    if stage == LAST:
        for term, start, stop, turned in shapes:
            shape = (places[term][2], stop - start)
            out_shape.append(jax.ShapeDtypeStruct(shape[::-1] if turned else shape, F32))
        if vectors:
            out_shape += [jax.ShapeDtypeStruct((1, column), F32)] * vectors[0].shape[0]
            out_shape += [jax.ShapeDtypeStruct(single.shape, F32) for single in vectors[2:]]
    else:
        travels = (row // 2 if stage == FIRST else row) + extra
        out_shape = [jax.ShapeDtypeStruct((travels, column), BF16)] * 2
        if apart:
            out_shape = [jax.ShapeDtypeStruct((row // len(layout), column), BF16)] * (2 * len(layout))
        if vectors:
            out_shape.append(jax.ShapeDtypeStruct((VECTOR_ROWS, column), F32))
        if stage == FIRST:
            operands += vectors
    vmem = pl.BlockSpec(memory_space=pltpu.VMEM)
    return pl.pallas_call(
        functools.partial(ring_sum_kernel, places, counts, stage, shapes, bool(vectors)),
        in_specs=[pl.BlockSpec(memory_space=pltpu.SMEM)] + [vmem] * len(operands),
        out_specs=[vmem] * len(out_shape),
        out_shape=out_shape,
        cost_estimate=pl.CostEstimate(
            flops=4 * row * column * depth,
            bytes_accessed=12 * row * column,
            transcendentals=0,
        ),
        compiler_params=pltpu.CompilerParams(vmem_limit_bytes=KERNEL_VMEM),
        name="ring_sum",
    )(jnp.stack(owners), *operands)


def row_major(array):
    return with_layout_constraint(array, Layout(major_to_minor=(0, 1)))


LANES = 128
QUERY_TILE = 256


def keep_head(block, head, other=None):
    lane = lax.broadcasted_iota(jnp.int32, block.shape, 1)
    kept = (lane >= head * HD) & (lane < (head + 1) * HD)
    rest = jnp.zeros_like(block)
    if other is not None:
        spare = HD * (1 - head)
        rest = jnp.where(lane == spare, other, rest)
    return jnp.where(kept, block, rest)


def key_offsets(shape, counts_ref):
    rows = shape[0] // counts_ref.shape[0]
    row = lax.broadcasted_iota(jnp.int32, (rows, shape[1]), 0)
    parts = [jnp.where(row < counts_ref[r], 0.0, MASKED) for r in range(counts_ref.shape[0])]
    return jnp.concatenate(parts, axis=0).astype(BF16)


def scores_of(keys, offsets, scaled_queries, head):
    with_offsets = keep_head(keys, head, offsets)
    with_ones = keep_head(scaled_queries, head, jnp.ones_like(scaled_queries))
    return matmul_nt(with_offsets, with_ones)


def attention_kernel(score_scale, counts_ref, query_ref, key_ref, value_ref, context_ref, log_total_ref):
    keys, values = key_ref[...], value_ref[...]
    offsets = key_offsets(keys.shape, counts_ref)
    queries = query_ref[...] * jnp.asarray(score_scale, BF16)
    pieces = []
    for head in range(LANES // HD):
        scores = scores_of(keys, offsets, queries, head)
        row_peak = jnp.max(scores, axis=0, keepdims=True)
        raised = jnp.exp(scores - row_peak)
        total = jnp.sum(raised, axis=0, keepdims=True)
        log_total_ref[0, head : head + 1, :] = row_peak + jnp.log(total)
        both = matmul_tn(values, raised.astype(BF16))
        pieces.append(both[head * HD : (head + 1) * HD] * (1.0 / total))
    context_ref[...] = jnp.concatenate(pieces, axis=0).T.astype(BF16)


def attention(qkv_low, counts, local_width, score_scale):
    seq_len = qkv_low.shape[0]
    pairs = local_width // LANES
    tiles = seq_len // QUERY_TILE
    return pl.pallas_call(
        functools.partial(attention_kernel, score_scale),
        grid=(pairs, tiles),
        in_specs=[
            pl.BlockSpec(memory_space=pltpu.SMEM),
            pl.BlockSpec((QUERY_TILE, LANES), lambda j, i: (i, j)),
            pl.BlockSpec((seq_len, LANES), lambda j, i: (0, pairs + j)),
            pl.BlockSpec((seq_len, LANES), lambda j, i: (0, 2 * pairs + j)),
        ],
        out_specs=[
            pl.BlockSpec((QUERY_TILE, LANES), lambda j, i: (i, j)),
            pl.BlockSpec((1, LANES // HD, QUERY_TILE), lambda j, i: (j, 0, i)),
        ],
        out_shape=[
            jax.ShapeDtypeStruct((seq_len, local_width), BF16),
            jax.ShapeDtypeStruct((pairs, LANES // HD, seq_len), F32),
        ],
        cost_estimate=pl.CostEstimate(
            flops=4 * seq_len * seq_len * local_width,
            bytes_accessed=8 * seq_len * local_width,
            transcendentals=seq_len * seq_len * local_width // HD,
        ),
        compiler_params=pltpu.CompilerParams(vmem_limit_bytes=KERNEL_VMEM),
        name="attention",
    )(counts, qkv_low, qkv_low, qkv_low)


def attention_grad_kernel(
    score_scale,
    counts_ref,
    query_ref,
    key_ref,
    value_ref,
    upstream_ref,
    log_total_ref,
    low_ref,
    query_sum_ref,
    value_sum_ref,
    key_total,
    value_total,
):
    pair, step = pl.program_id(0), pl.program_id(1)
    width = low_ref.shape[1] // 3

    @pl.when(step == 0)
    def _():
        key_total[...] = jnp.zeros_like(key_total)
        value_total[...] = jnp.zeros_like(value_total)
        query_sum_ref[...] = jnp.zeros_like(query_sum_ref)

    keys, values = key_ref[...], value_ref[...]
    offsets = key_offsets(keys.shape, counts_ref)
    scale = jnp.asarray(score_scale, BF16)
    queries, scaled_keys = query_ref[...] * scale, keys * scale
    pieces = []
    for head in range(LANES // HD):
        upstream = keep_head(upstream_ref[...], head)
        scores = scores_of(keys, offsets, queries, head)
        probs = jnp.exp(scores - log_total_ref[0, head : head + 1, :])
        prob_grad = matmul_nt(values, upstream)
        row_inner = jnp.sum(probs * prob_grad, axis=0, keepdims=True)
        score_grad = (probs * (prob_grad - row_inner)).astype(BF16)
        value_total[...] += matmul(probs.astype(BF16), upstream)
        key_total[...] += matmul(score_grad, keep_head(queries, head))
        both = matmul_tn(scaled_keys, score_grad)
        pieces.append(both[head * HD : (head + 1) * HD])
    query_grad = jnp.concatenate(pieces, axis=0).T
    rows = pl.ds(pl.multiple_of(step * QUERY_TILE, QUERY_TILE), QUERY_TILE)
    start = pl.multiple_of(pair * LANES, LANES)
    low_ref[rows, pl.ds(start, LANES)] = query_grad.astype(BF16)
    query_sum_ref[...] += jnp.sum(query_grad, axis=0, keepdims=True)

    @pl.when(step == pl.num_programs(1) - 1)
    def _():
        low_ref[:, pl.ds(start + width, LANES)] = key_total[...].astype(BF16)
        low_ref[:, pl.ds(start + 2 * width, LANES)] = value_total[...].astype(BF16)
        value_sum_ref[...] = jnp.sum(value_total[...], axis=0, keepdims=True)


def attention_grad(qkv_low, upstream, log_total, counts, local_width, score_scale):
    seq_len = qkv_low.shape[0]
    pairs = local_width // LANES
    tiles = seq_len // QUERY_TILE
    tile_spec = pl.BlockSpec((QUERY_TILE, LANES), lambda j, i: (i, j))
    sum_spec = pl.BlockSpec((1, LANES), lambda j, i: (0, j))
    sums = jax.ShapeDtypeStruct((1, local_width), F32)
    return pl.pallas_call(
        functools.partial(attention_grad_kernel, score_scale),
        grid=(pairs, tiles),
        in_specs=[
            pl.BlockSpec(memory_space=pltpu.SMEM),
            tile_spec,
            pl.BlockSpec((seq_len, LANES), lambda j, i: (0, pairs + j)),
            pl.BlockSpec((seq_len, LANES), lambda j, i: (0, 2 * pairs + j)),
            tile_spec,
            pl.BlockSpec((1, LANES // HD, QUERY_TILE), lambda j, i: (j, 0, i)),
        ],
        out_specs=[pl.BlockSpec((seq_len, 3 * local_width), lambda j, i: (0, 0)), sum_spec, sum_spec],
        out_shape=[jax.ShapeDtypeStruct((seq_len, 3 * local_width), BF16), sums, sums],
        scratch_shapes=[pltpu.VMEM((seq_len, LANES), F32), pltpu.VMEM((seq_len, LANES), F32)],
        cost_estimate=pl.CostEstimate(
            flops=10 * seq_len * seq_len * local_width,
            bytes_accessed=16 * seq_len * local_width,
            transcendentals=seq_len * seq_len * local_width // HD,
        ),
        compiler_params=pltpu.CompilerParams(vmem_limit_bytes=KERNEL_VMEM),
        name="attention_grad",
    )(counts, qkv_low, qkv_low, qkv_low, upstream, log_total)


def layer(
    hidden_in,
    cotangent,
    lengths,
    query_weight,
    key_weight,
    value_weight,
    output_weight,
    up_weight,
    down_weight,
    query_bias,
    value_bias,
    output_bias,
    up_bias,
    down_bias,
    first_gain,
    first_shift,
    second_gain,
    second_shift,
):
    n_tensor = lax.axis_size("tensor")
    tensor_index = lax.axis_index("tensor")
    local_rows = hidden_in.shape[0]
    local_width = query_weight.shape[1]
    score_scale = HD ** (-0.5)
    ring = Ring()
    blocks = jnp.arange(n_tensor, dtype=jnp.int32) ^ tensor_index
    counts = lengths[0] - blocks * local_rows

    packed = row_major(jnp.concatenate([query_weight, key_weight, value_weight, output_weight.T], axis=1))
    (packed_full,) = ring.gather(packed, (packed.shape[0],))
    hidden_full = jnp.concatenate(gather_rows(hidden_in), axis=0)
    (up_full,) = ring.gather(up_weight, (up_weight.shape[0],))
    (down_turned,) = ring.gather(row_major(down_weight.T), (down_weight.shape[1],))
    qkv_full = packed_full[:, : 3 * local_width]
    output_turned = packed_full[:, 3 * local_width :]

    qkv_bias = jnp.concatenate([query_bias, jnp.zeros_like(query_bias), value_bias])
    qkv_low = (matmul(hidden_full, qkv_full) + qkv_bias).astype(BF16)
    context, log_total = attention(qkv_low, counts, local_width, score_scale)
    block, column, total = hidden_in.shape, (local_rows, 1), (3, hidden_in.shape[1])
    attn_parts = scatter_rows(*halves(matmul_nt(context, output_turned).astype(BF16)))
    first_out, first_normed, first_inverse, first_low = norm_stage(
        first_norm_kernel,
        [hidden_in, *attn_parts, output_bias, first_gain, first_shift],
        [(block, F32), (block, F32), (column, F32), (block, BF16)],
    )
    normed = gather_rows(first_low)
    activated, slope, mlp = [None] * 2, [None] * 2, [None] * 2
    for i in (1, 0):
        pre_act = matmul(normed[i], up_full) + up_bias
        activated[i], slope[i] = lax.optimization_barrier((gelu_value(pre_act).astype(BF16), gelu_slope(pre_act)))
        mlp[i] = matmul_nt(activated[i], down_turned).astype(BF16)
    mlp_parts = scatter_rows(*mlp)
    hidden_out, second_grad, second_low, second_sums = norm_stage(
        second_norm_kernel,
        [first_out, *mlp_parts, down_bias, second_gain, second_shift, cotangent],
        [(block, BF16), (block, F32), (block, BF16), (total, F32)],
    )
    second = gather_rows(second_low)
    pre_low, up_sums, partial = [None] * 2, [None] * 2, [None] * 2
    for i in (0, 1):
        pre_grad = matmul(second[i], down_turned) * slope[i]
        up_sums[i], pre_low[i] = lax.optimization_barrier((jnp.sum(pre_grad, axis=0), pre_grad.astype(BF16)))
        partial[i] = matmul_nt(pre_low[i], up_full).astype(BF16)
    grad_up_bias = up_sums[0] + up_sums[1]
    up_owned, down_owned = ring.scatter(
        [[(normed, pre_low)], [(second, activated)]],
        ((0, 0, up_weight.shape[1], False), (1, 0, down_weight.shape[0], True)),
    )
    first_grad, first_grad_low, first_sums = norm_stage(
        first_grad_kernel,
        [second_grad, *scatter_rows(*partial), first_gain, first_normed, first_inverse],
        [(block, F32), (block, BF16), (total, F32)],
    )
    attn_grad_full = lax.optimization_barrier(jnp.concatenate(gather_rows(first_grad_low), axis=0))
    context_grad = matmul(attn_grad_full, output_turned).astype(BF16)

    everywhere = jnp.concatenate([second_sums, first_sums], axis=0)
    everywhere = everywhere + swap(everywhere, "tensor", 1)
    everywhere_far = swap(everywhere, "tensor", 2)

    low, query_sum, value_sum = attention_grad(
        qkv_low, context_grad, log_total, counts, local_width, score_scale
    )
    query_owned, key_owned, value_owned, output_owned, *sums = ring.scatter(
        [[((hidden_full,), (low,)), ((attn_grad_full,), (context,))]],
        tuple((0, i * local_width, (i + 1) * local_width, False) for i in range(3)) + ((1, 0, local_width, True),),
        (everywhere, everywhere_far, grad_up_bias.reshape(1, -1), query_sum, value_sum),
    )
    sums = [vector.reshape(-1) for vector in sums]
    back = matmul_nt(low, qkv_full).astype(BF16)
    back_parts = scatter_rows(*halves(back))
    grad_in = (first_grad + sum(part.astype(F32) for part in back_parts)).astype(BF16)
    return (
        hidden_out,
        grad_in,
        query_owned,
        key_owned,
        value_owned,
        output_owned,
        up_owned,
        down_owned,
        sums[7],
        sums[8],
        sums[5],
        sums[6],
        sums[2],
        sums[3],
        sums[4],
        sums[0],
        sums[1],
    )


def solution(mesh):
    in_specs = (
        P(("dp", "tensor"), None),
        P(("dp", "tensor"), None),
        P("dp"),
        P("dp", "tensor"),
        P("dp", "tensor"),
        P("dp", "tensor"),
        P("tensor", "dp"),
        P("dp", "tensor"),
        P("tensor", "dp"),
        P("tensor"),
        P("tensor"),
        P(),
        P("tensor"),
        P(),
        P(),
        P(),
        P(),
        P(),
    )
    out_specs = (
        P(("dp", "tensor"), None),
        P(("dp", "tensor"), None),
        P("dp", "tensor"),
        P("dp", "tensor"),
        P("dp", "tensor"),
        P("tensor", "dp"),
        P("dp", "tensor"),
        P("tensor", "dp"),
        P("tensor"),
        P("tensor"),
        P(),
        P("tensor"),
        P(),
        P(),
        P(),
        P(),
        P(),
    )
    return jax.shard_map(layer, mesh=mesh, in_specs=in_specs, out_specs=out_specs, check_vma=False)
```
